32 devices in a mesh: dp: 4 (over z), seq: 2 (over core), mp: 4 (over y, x).
Axes of the slice: x: 2, y: 2, z: 4, core: 2. Of those that a mesh axis runs over, the one named last changes fastest.
Arguments:
- frames: bfloat16 [16, 768, 768], P('dp', 'seq'), may hold values from -6 to 6
- cotangent: bfloat16 [16, 768, 768], P('dp', 'seq'), may hold values from -6 to 6
- lengths: int32 [16], P('dp'), may hold values from 256 to 768, as said below
- attn_master: float32 [4, 768, 768], P(None, ('dp', 'seq'), 'mp'), may hold values from -2 to 2
- attn_moment: float32 [4, 768, 768], P(None, ('dp', 'seq'), 'mp'), may hold values from -0.0546875 to 0.0546875
- attn_average: float32 [4, 768, 768], P(None, ('dp', 'seq'), 'mp'), may hold values from -0.21875 to 0.21875
- ffn_master: float32 [2, 768, 3072], P(None, ('dp', 'seq'), 'mp'), may hold values from -2 to 2
- ffn_moment: float32 [2, 768, 3072], P(None, ('dp', 'seq'), 'mp'), may hold values from -0.0546875 to 0.0546875
- ffn_average: float32 [2, 768, 3072], P(None, ('dp', 'seq'), 'mp'), may hold values from -0.21875 to 0.21875
- norm_vecs: float32 [6, 768], replicated, may hold values from -2 to 2
- norm_moment: float32 [6, 768], replicated, may hold values from -0.0546875 to 0.0546875
- norm_average: float32 [6, 768], replicated, may hold values from -3 to 3
- col_bias: float32 [4608], P('mp'), may hold values from -1.5 to 1.5
- col_moment: float32 [4608], P('mp'), may hold values from -0.0546875 to 0.0546875
- col_average: float32 [4608], P('mp'), may hold values from -1.5 to 1.5
- rel_table: float32 [320, 12], P(None, 'mp'), may hold values from -2.5 to 2.5
- rel_moment: float32 [320, 12], P(None, 'mp'), may hold values from -0.0546875 to 0.0546875
- rel_average: float32 [320, 12], P(None, 'mp'), may hold values from -2.5 to 2.5
- dec_frames: bfloat16 [16, 256, 768], P('dp', 'seq'), may hold values from -6 to 6
- dec_cotangent: bfloat16 [16, 256, 768], P('dp', 'seq'), may hold values from -6 to 6
- text_lengths: int32 [16], P('dp'), may hold values from 64 to 256, as said below
- dec_attn_master: float32 [8, 768, 768], P(None, ('dp', 'seq'), 'mp'), may hold values from -2 to 2
- dec_attn_moment: float32 [8, 768, 768], P(None, ('dp', 'seq'), 'mp'), may hold values from -0.0546875 to 0.0546875
- dec_attn_average: float32 [8, 768, 768], P(None, ('dp', 'seq'), 'mp'), may hold values from -0.21875 to 0.21875
- dec_ffn_master: float32 [2, 768, 3072], P(None, ('dp', 'seq'), 'mp'), may hold values from -2 to 2
- dec_ffn_moment: float32 [2, 768, 3072], P(None, ('dp', 'seq'), 'mp'), may hold values from -0.0546875 to 0.0546875
- dec_ffn_average: float32 [2, 768, 3072], P(None, ('dp', 'seq'), 'mp'), may hold values from -0.21875 to 0.21875
- dec_norm_vecs: float32 [9, 768], replicated, may hold values from -2 to 2
- dec_norm_moment: float32 [9, 768], replicated, may hold values from -0.0546875 to 0.0546875
- dec_norm_average: float32 [9, 768], replicated, may hold values from -3 to 3
- dec_col_bias: float32 [6144], P('mp'), may hold values from -1.5 to 1.5
- dec_col_moment: float32 [6144], P('mp'), may hold values from -0.0546875 to 0.0546875
- dec_col_average: float32 [6144], P('mp'), may hold values from -1.5 to 1.5
Outputs:
- output: bfloat16 [16, 768, 768], P('dp', 'seq')
- input_grad: bfloat16 [16, 768, 768], P('dp', 'seq')
- attn_grad: float32 [4, 768, 768], P(None, ('dp', 'seq'), 'mp')
- ffn_grad: float32 [2, 768, 3072], P(None, ('dp', 'seq'), 'mp')
- attn_master_new: float32 [4, 768, 768], P(None, ('dp', 'seq'), 'mp')
- attn_moment_new: float32 [4, 768, 768], P(None, ('dp', 'seq'), 'mp')
- attn_average_new: float32 [4, 768, 768], P(None, ('dp', 'seq'), 'mp')
- attn_copy: bfloat16 [4, 768, 768], P(None, ('dp', 'seq'), 'mp')
- ffn_master_new: float32 [2, 768, 3072], P(None, ('dp', 'seq'), 'mp')
- ffn_moment_new: float32 [2, 768, 3072], P(None, ('dp', 'seq'), 'mp')
- ffn_average_new: float32 [2, 768, 3072], P(None, ('dp', 'seq'), 'mp')
- ffn_copy: bfloat16 [2, 768, 3072], P(None, ('dp', 'seq'), 'mp')
- norm_vecs_new: float32 [6, 768], replicated
- norm_moment_new: float32 [6, 768], replicated
- norm_average_new: float32 [6, 768], replicated
- col_bias_new: float32 [4608], P('mp')
- col_moment_new: float32 [4608], P('mp')
- col_average_new: float32 [4608], P('mp')
- rel_table_new: float32 [320, 12], P(None, 'mp')
- rel_moment_new: float32 [320, 12], P(None, 'mp')
- rel_average_new: float32 [320, 12], P(None, 'mp')
- dec_output: bfloat16 [16, 256, 768], P('dp', 'seq')
- dec_input_grad: bfloat16 [16, 256, 768], P('dp', 'seq')
- dec_attn_grad: float32 [8, 768, 768], P(None, ('dp', 'seq'), 'mp')
- dec_ffn_grad: float32 [2, 768, 3072], P(None, ('dp', 'seq'), 'mp')
- dec_attn_master_new: float32 [8, 768, 768], P(None, ('dp', 'seq'), 'mp')
- dec_attn_moment_new: float32 [8, 768, 768], P(None, ('dp', 'seq'), 'mp')
- dec_attn_average_new: float32 [8, 768, 768], P(None, ('dp', 'seq'), 'mp')
- dec_attn_copy: bfloat16 [8, 768, 768], P(None, ('dp', 'seq'), 'mp')
- dec_ffn_master_new: float32 [2, 768, 3072], P(None, ('dp', 'seq'), 'mp')
- dec_ffn_moment_new: float32 [2, 768, 3072], P(None, ('dp', 'seq'), 'mp')
- dec_ffn_average_new: float32 [2, 768, 3072], P(None, ('dp', 'seq'), 'mp')
- dec_ffn_copy: bfloat16 [2, 768, 3072], P(None, ('dp', 'seq'), 'mp')
- dec_norm_vecs_new: float32 [9, 768], replicated
- dec_norm_moment_new: float32 [9, 768], replicated
- dec_norm_average_new: float32 [9, 768], replicated
- dec_col_bias_new: float32 [6144], P('mp')
- dec_col_moment_new: float32 [6144], P('mp')
- dec_col_average_new: float32 [6144], P('mp')
The draws below stay inside these ranges and needn't reach their ends.
Inputs may be any that keep to these rules, and one draw needn't show every extreme that they name: `lengths`: each utterance has 256, 512 or 768 valid frames; the first has 768. `text_lengths`: the first utterance's transcript fills all 256 slots.
All inputs are finite; a program needn't handle non-finite values.
Results may differ from the reference program's by a relative error of at most 0.025.
Values may be sent and summed in bfloat16 or wider, within the bound.
No kernel may reach another device: no remote copies, remote signals or barrier semaphores. Data moves between devices by JAX's collectives and lax.ppermute only.
A program may use at most 320 MiB of HBM per device.

```python
import math
import jax
import jax.numpy as jnp
from jax import lax

D = 768
H = 12
HD = 64
FF = 3072
REL = 160
LEN = 768
TLEN = 256
UTT = 16
NB = 320
FRAMES = 12288
N_MP = 4


def spread_values(key, shape):
    return jnp.clip(jax.random.normal(key, shape, jnp.float32), -6.0, 6.0)


def ffn_draw(key, salt):
    base_draw = spread_values(jax.random.fold_in(key, salt), (2, D, FF))
    factors = jnp.array([D ** (-0.5), 1.5 * FF ** (-0.5)], jnp.float32)
    return base_draw * factors[:, None, None]


def norm_draw(key, rows, gain_count, salt):
    gain_rows = jax.random.uniform(jax.random.fold_in(key, salt), (rows, D), jnp.float32, 0.6, 1.4)
    shifts = 0.3 * jnp.clip(jax.random.normal(jax.random.fold_in(key, salt + 1), (rows, D), jnp.float32), -4.0, 4.0)
    row_index = jnp.arange(rows)
    is_gain = (row_index % 2 == 0) & (row_index < 2 * gain_count)
    return jnp.where(is_gain[:, None], gain_rows, shifts)


def draw_lengths(key, part):
    bucket_pick = jax.random.randint(jax.random.fold_in(key, 11), (UTT,), 0, 12)
    lengths = jnp.where(bucket_pick < 3, LEN, jnp.where(bucket_pick < 7, 2 * LEN // 3, LEN // 3))
    return lengths.at[0].set(LEN).astype(jnp.int32)


def draw_text_lengths(key, part):
    text_len = jax.random.randint(jax.random.fold_in(key, 51), (UTT,), TLEN // 4, TLEN + 1)
    return text_len.at[0].set(TLEN).astype(jnp.int32)


def draw_attn_master(key, part):
    base_draw = spread_values(jax.random.fold_in(key, 21), (4, D, D))
    factors = jnp.array([1.0, 1.0, 1.0, LEN ** 0.5 / 4.0], jnp.float32) * D ** (-0.5)
    return base_draw * factors[:, None, None]


def draw_dec_attn_master(key, part):
    base_draw = spread_values(jax.random.fold_in(key, 23), (8, D, D))
    factors = jnp.array([1.0, 1.0, 1.0, TLEN ** 0.5 / 4.0, 1.0, 1.0, 1.0, LEN ** 0.5 / 4.0], jnp.float32) * D ** (-0.5)
    return base_draw * factors[:, None, None]


def draw_ffn_master(key, part):
    return ffn_draw(key, 31)


def draw_dec_ffn_master(key, part):
    return ffn_draw(key, 33)


def draw_norm_vecs(key, part):
    return norm_draw(key, 6, 2, 41)


def draw_dec_norm_vecs(key, part):
    return norm_draw(key, 9, 3, 45)


def steps_of(rng, shape, cuts, smallest, high):
    def one(position, shards_of):
        steps = jax.random.uniform(jax.random.fold_in(jax.random.fold_in(rng, 6), position), (shards_of,), jnp.float32, smallest / len(cuts), high / len(cuts))
        return jnp.repeat(jnp.exp(steps), shape[position] // shards_of).reshape((-1,) + (1,) * (len(shape) - position - 1))

    loudness = one(*cuts[0])
    for cut in cuts[1:]:
        loudness = loudness * one(*cut)
    return loudness


def scatter_about(rng, shape, width, reach, cuts=(), held_as=jnp.bfloat16):
    values = jax.random.normal(rng, shape, jnp.float32) * width
    if len(cuts) > 0:
        values = steps_of(rng, shape, cuts, -0.22, 0.18) * values
    return jnp.clip(values, min=-reach, max=reach).astype(held_as)


def setup_inputs(seed: int = 0) -> dict:
    keys = jax.random.split(jax.random.key(seed), 34)
    frames = scatter_about(keys[0], (UTT, LEN, D), 1.0, 6.0, ((0, 4), (1, 2)))
    cotangent = scatter_about(keys[1], (UTT, LEN, D), 1.0, 6.0, ((0, 4), (1, 2)))
    lengths = draw_lengths(jax.random.fold_in(keys[33], 71), 0)
    attn_master = draw_attn_master(jax.random.fold_in(keys[33], 71), 0)
    attn_moment = scatter_about(keys[4], (4, D, D), FRAMES ** -0.5, 0.0546875, ((1, 8), (2, 4)), jnp.float32)
    attn_average = scatter_about(keys[5], (4, D, D), D ** -0.5, 0.21875, ((1, 8), (2, 4)), jnp.float32)
    ffn_master = draw_ffn_master(jax.random.fold_in(keys[33], 71), 0)
    ffn_moment = scatter_about(keys[7], (2, D, FF), FRAMES ** -0.5, 0.0546875, ((1, 8), (2, 4)), jnp.float32)
    ffn_average = scatter_about(keys[8], (2, D, FF), D ** -0.5, 0.21875, ((1, 8), (2, 4)), jnp.float32)
    norm_vecs = draw_norm_vecs(jax.random.fold_in(keys[33], 71), 0)
    norm_moment = scatter_about(keys[10], (6, D), FRAMES ** -0.5, 0.0546875, (), jnp.float32)
    norm_average = scatter_about(keys[11], (6, D), 0.5, 3.0, (), jnp.float32)
    col_bias = scatter_about(keys[12], (2 * D + FF,), 0.3, 1.5, ((0, 4),), jnp.float32)
    col_moment = scatter_about(keys[13], (2 * D + FF,), FRAMES ** -0.5, 0.0546875, ((0, 4),), jnp.float32)
    col_average = scatter_about(keys[14], (2 * D + FF,), 0.3, 1.5, ((0, 4),), jnp.float32)
    rel_table = scatter_about(keys[15], (NB, H), 0.5, 2.5, ((1, 4),), jnp.float32)
    rel_moment = scatter_about(keys[16], (NB, H), FRAMES ** -0.5, 0.0546875, ((1, 4),), jnp.float32)
    rel_average = scatter_about(keys[17], (NB, H), 0.5, 2.5, ((1, 4),), jnp.float32)
    dec_frames = scatter_about(keys[18], (UTT, TLEN, D), 1.0, 6.0, ((0, 4), (1, 2)))
    dec_cotangent = scatter_about(keys[19], (UTT, TLEN, D), 1.0, 6.0, ((0, 4), (1, 2)))
    text_lengths = draw_text_lengths(jax.random.fold_in(keys[33], 71), 0)
    dec_attn_master = draw_dec_attn_master(jax.random.fold_in(keys[33], 71), 0)
    dec_attn_moment = scatter_about(keys[22], (8, D, D), FRAMES ** -0.5, 0.0546875, ((1, 8), (2, 4)), jnp.float32)
    dec_attn_average = scatter_about(keys[23], (8, D, D), D ** -0.5, 0.21875, ((1, 8), (2, 4)), jnp.float32)
    dec_ffn_master = draw_dec_ffn_master(jax.random.fold_in(keys[33], 71), 0)
    dec_ffn_moment = scatter_about(keys[25], (2, D, FF), FRAMES ** -0.5, 0.0546875, ((1, 8), (2, 4)), jnp.float32)
    dec_ffn_average = scatter_about(keys[26], (2, D, FF), D ** -0.5, 0.21875, ((1, 8), (2, 4)), jnp.float32)
    dec_norm_vecs = draw_dec_norm_vecs(jax.random.fold_in(keys[33], 71), 0)
    dec_norm_moment = scatter_about(keys[28], (9, D), FRAMES ** -0.5, 0.0546875, (), jnp.float32)
    dec_norm_average = scatter_about(keys[29], (9, D), 0.5, 3.0, (), jnp.float32)
    dec_col_bias = scatter_about(keys[30], (4 * D + FF,), 0.3, 1.5, ((0, 4),), jnp.float32)
    dec_col_moment = scatter_about(keys[31], (4 * D + FF,), FRAMES ** -0.5, 0.0546875, ((0, 4),), jnp.float32)
    dec_col_average = scatter_about(keys[32], (4 * D + FF,), 0.3, 1.5, ((0, 4),), jnp.float32)
    return {"frames": frames, "cotangent": cotangent, "lengths": lengths, "attn_master": attn_master, "attn_moment": attn_moment, "attn_average": attn_average, "ffn_master": ffn_master, "ffn_moment": ffn_moment, "ffn_average": ffn_average, "norm_vecs": norm_vecs, "norm_moment": norm_moment, "norm_average": norm_average, "col_bias": col_bias, "col_moment": col_moment, "col_average": col_average, "rel_table": rel_table, "rel_moment": rel_moment, "rel_average": rel_average, "dec_frames": dec_frames, "dec_cotangent": dec_cotangent, "text_lengths": text_lengths, "dec_attn_master": dec_attn_master, "dec_attn_moment": dec_attn_moment, "dec_attn_average": dec_attn_average, "dec_ffn_master": dec_ffn_master, "dec_ffn_moment": dec_ffn_moment, "dec_ffn_average": dec_ffn_average, "dec_norm_vecs": dec_norm_vecs, "dec_norm_moment": dec_norm_moment, "dec_norm_average": dec_norm_average, "dec_col_bias": dec_col_bias, "dec_col_moment": dec_col_moment, "dec_col_average": dec_col_average}


EPSILON = 1e-05
MOMENTUM = 0.9
AVERAGING = 0.75
MATRIX_RATE = 0.02
VECTOR_RATE = 0.2
MASK_VALUE = -1e+30
HIGHEST_PRECISION = lax.Precision.HIGHEST

@jax.custom_vjp
def low(v):
    return lax.optimization_barrier(v.astype(jnp.bfloat16)).astype(jnp.float32)

@jax.custom_vjp
def low_back(v):
    return v

def low_keep(v):
    return (low(v), None)

def low_pass(kept, grad):
    return (grad,)

def back_keep(v):
    return (v, None)

def back_low(kept, grad):
    return (low(grad),)
low.defvjp(low_keep, low_pass)
low_back.defvjp(back_keep, back_low)

def matmul(left_mat, right_mat):
    return jnp.dot(left_mat, right_mat, precision=HIGHEST_PRECISION, preferred_element_type=jnp.float32)

def matmul_nt(left_mat, right_mat):
    return lax.dot_general(left_mat, right_mat, (((1,), (1,)), ((), ())), precision=HIGHEST_PRECISION, preferred_element_type=jnp.float32)

def layer_norm(values, gain_vec, offset):
    center = values - lax.optimization_barrier(jnp.mean(values, axis=-1, keepdims=True))
    variance = lax.optimization_barrier(jnp.mean(center * center, axis=-1, keepdims=True))
    return center * lax.rsqrt(variance + EPSILON) * gain_vec + offset

def attention(query_in, memory_in, mats, biases, offset, block_len, key_valid, rel_parts, self_attn):
    head_count = H // N_MP
    head_cols = D // N_MP
    query_len = query_in.shape[0]
    key_len = memory_in.shape[0]
    total = jnp.zeros((query_len, D), jnp.float32)
    for group_index in range(N_MP):
        col_range = slice(group_index * head_cols, (group_index + 1) * head_cols)
        base_col = group_index * block_len + offset
        group_query = low_back(query_in)
        group_memory = group_query if self_attn else low_back(memory_in)
        queries = low(low_back(matmul(group_query, mats[0][:, col_range]) + biases[base_col:base_col + head_cols]))
        key_rows = low(low_back(matmul(group_memory, mats[1][:, col_range])))
        value_rows = low(low_back(matmul(group_memory, mats[2][:, col_range]) + biases[base_col + head_cols:base_col + 2 * head_cols]))
        query_heads = queries.reshape(query_len, head_count, HD)
        key_heads = key_rows.reshape(key_len, head_count, HD)
        value_heads = value_rows.reshape(key_len, head_count, HD)
        scores = jnp.einsum('qhe,khe->hqk', query_heads, key_heads, precision=HIGHEST_PRECISION) * HD ** (-0.5)
        if rel_parts is not None:
            bias_table, buckets = rel_parts
            table_part = bias_table[:, group_index * head_count:(group_index + 1) * head_count]
            scores = scores + jnp.transpose(jnp.take(table_part, buckets, axis=0), (2, 0, 1))
        scores = jnp.where(key_valid, low_back(scores), MASK_VALUE)
        prob_rows = jax.nn.softmax(scores, axis=-1)
        context = jnp.einsum('hqk,khe->qhe', low(prob_rows), value_heads, precision=HIGHEST_PRECISION)
        context = low(low_back(context.reshape(query_len, head_cols)))
        total = total + low(matmul_nt(context, mats[3][:, col_range]))
    return total

def feed_forward(normed_low, ffn_w, biases, offset, block_len):
    hidden_cols = FF // N_MP
    total = jnp.zeros((normed_low.shape[0], D), jnp.float32)
    for group_index in range(N_MP):
        col_range = slice(group_index * hidden_cols, (group_index + 1) * hidden_cols)
        base_col = group_index * block_len + offset
        gate_in = low_back(matmul(low_back(normed_low), ffn_w[0][:, col_range]) + biases[base_col:base_col + hidden_cols])
        activated = low(jax.nn.gelu(gate_in, approximate=False))
        total = total + low(matmul_nt(activated, ffn_w[1][:, col_range]))
    return total

def utterance(weights, frame_rows, length, text_rows, text_length):
    attn_w, ffn_w, norm_vecs, col_bias, rel_table, dec_attn, dec_ffn, dec_norm, dec_col = weights
    head_cols = D // N_MP
    enc_block = (2 * D + FF) // N_MP
    dec_block = (4 * D + FF) // N_MP
    positions = jnp.arange(LEN, dtype=jnp.int32)
    buckets = (jnp.clip(positions[None, :] - positions[:, None], -REL, REL - 1) + REL).astype(jnp.int32)
    key_valid = (positions < length)[None, None, :]
    attn_sum = attention(frame_rows, frame_rows, attn_w, col_bias, 0, enc_block, key_valid, (rel_table, buckets), True)
    hidden_one = layer_norm(frame_rows + low_back(attn_sum) + norm_vecs[4], norm_vecs[0], norm_vecs[1])
    ffn_sum = feed_forward(low(hidden_one), ffn_w, col_bias, 2 * head_cols, enc_block)
    enc_out = layer_norm(hidden_one + low_back(ffn_sum) + norm_vecs[5], norm_vecs[2], norm_vecs[3])
    enc_low = low(enc_out)
    text_pos = jnp.arange(TLEN, dtype=jnp.int32)
    self_valid = ((text_pos[None, :] <= text_pos[:, None]) & (text_pos[None, :] < text_length))[None]
    self_sum = attention(text_rows, text_rows, dec_attn[:4], dec_col, 0, dec_block, self_valid, None, True)
    dec_one = layer_norm(text_rows + low_back(self_sum) + dec_norm[6], dec_norm[0], dec_norm[1])
    cross_sum = attention(low(dec_one), enc_low, dec_attn[4:], dec_col, 2 * head_cols, dec_block, key_valid, None, False)
    dec_two = layer_norm(dec_one + low_back(cross_sum) + dec_norm[7], dec_norm[2], dec_norm[3])
    dec_ffn_sum = feed_forward(low(dec_two), dec_ffn, dec_col, 4 * head_cols, dec_block)
    dec_out = layer_norm(dec_two + low_back(dec_ffn_sum) + dec_norm[8], dec_norm[4], dec_norm[5])
    return (enc_out, dec_out)

def update(master, moment, average, gradient, step_rate, frame_total):
    mean_grad = gradient / frame_total
    new_moment = MOMENTUM * moment + mean_grad
    new_master = master - step_rate * (mean_grad + MOMENTUM * new_moment)
    new_average = AVERAGING * average + (1.0 - AVERAGING) * new_master
    return (mean_grad, new_master, new_moment, new_average)

def reference(frames, cotangent, lengths, attn_master, attn_moment, attn_average, ffn_master, ffn_moment, ffn_average, norm_vecs, norm_moment, norm_average, col_bias, col_moment, col_average, rel_table, rel_moment, rel_average, dec_frames, dec_cotangent, text_lengths, dec_attn_master, dec_attn_moment, dec_attn_average, dec_ffn_master, dec_ffn_moment, dec_ffn_average, dec_norm_vecs, dec_norm_moment, dec_norm_average, dec_col_bias, dec_col_moment, dec_col_average):
    params = (attn_master, ffn_master, norm_vecs, col_bias, rel_table, dec_attn_master, dec_ffn_master, dec_norm_vecs, dec_col_bias)
    frame_data = frames.astype(jnp.float32)
    text_data = dec_frames.astype(jnp.float32)

    def forward(params, frame_data, text_data):
        weights = (low(params[0]), low(params[1]), params[2], params[3], params[4], low(params[5]), low(params[6]), params[7], params[8])
        step_fn = jax.checkpoint(utterance)

        def visit_one(carry_val, pieces):
            return (carry_val, step_fn(weights, pieces[0], pieces[1], pieces[2], pieces[3]))
        _, outputs = lax.scan(visit_one, jnp.zeros((), jnp.float32), (frame_data, lengths, text_data, text_lengths))
        return outputs
    outputs, pullback = jax.vjp(forward, params, frame_data, text_data)
    positions = jnp.arange(LEN, dtype=jnp.int32)
    valid_rows = (positions[None, :] < lengths[:, None]).astype(jnp.float32)
    masked_cot = cotangent.astype(jnp.float32) * valid_rows[:, :, None]
    text_pos = jnp.arange(TLEN, dtype=jnp.int32)
    text_valid = (text_pos[None, :] < text_lengths[:, None]).astype(jnp.float32)
    masked_dec_cot = dec_cotangent.astype(jnp.float32) * text_valid[:, :, None]
    all_grads, frame_grad, text_grad = pullback((masked_cot, masked_dec_cot))
    frame_total = jnp.sum(valid_rows)
    root_frames = math.sqrt(float(FRAMES))
    matrix_rate = MATRIX_RATE * root_frames
    vector_rate = VECTOR_RATE * root_frames
    attn_new = update(attn_master, attn_moment, attn_average, all_grads[0], matrix_rate, frame_total)
    ffn_new = update(ffn_master, ffn_moment, ffn_average, all_grads[1], matrix_rate, frame_total)
    norm_new = update(norm_vecs, norm_moment, norm_average, all_grads[2], vector_rate, frame_total)
    col_new = update(col_bias, col_moment, col_average, all_grads[3], vector_rate, frame_total)
    rel_new = update(rel_table, rel_moment, rel_average, all_grads[4], vector_rate, frame_total)
    dattn_new = update(dec_attn_master, dec_attn_moment, dec_attn_average, all_grads[5], matrix_rate, frame_total)
    dffn_new = update(dec_ffn_master, dec_ffn_moment, dec_ffn_average, all_grads[6], matrix_rate, frame_total)
    dnorm_new = update(dec_norm_vecs, dec_norm_moment, dec_norm_average, all_grads[7], vector_rate, frame_total)
    dcol_new = update(dec_col_bias, dec_col_moment, dec_col_average, all_grads[8], vector_rate, frame_total)
    return (outputs[0].astype(jnp.bfloat16), frame_grad.astype(jnp.bfloat16), attn_new[0], ffn_new[0], attn_new[1], attn_new[2], attn_new[3], attn_new[1].astype(jnp.bfloat16), ffn_new[1], ffn_new[2], ffn_new[3], ffn_new[1].astype(jnp.bfloat16), norm_new[1], norm_new[2], norm_new[3], col_new[1], col_new[2], col_new[3], rel_new[1], rel_new[2], rel_new[3], outputs[1].astype(jnp.bfloat16), text_grad.astype(jnp.bfloat16), dattn_new[0], dffn_new[0], dattn_new[1], dattn_new[2], dattn_new[3], dattn_new[1].astype(jnp.bfloat16), dffn_new[1], dffn_new[2], dffn_new[3], dffn_new[1].astype(jnp.bfloat16), dnorm_new[1], dnorm_new[2], dnorm_new[3], dcol_new[1], dcol_new[2], dcol_new[3])
```

```python
import functools

import jax
import jax.numpy as jnp
from jax import lax
from jax.experimental import pallas as pl
from jax.experimental.pallas import tpu as pltpu
from jax.sharding import PartitionSpec as P

EPSILON = 1e-05
MOMENTUM = 0.9
AVERAGING = 0.75
MATRIX_RATE = 0.02
VECTOR_RATE = 0.2
MASK_VALUE = -1e30
ROOT_HALF = 0.7071067811865476
INV_ROOT_TAU = 0.3989422804014327
BLOCK = 256
PAIR = 128
BF16 = jnp.bfloat16
F32 = jnp.float32


def bf(a):
    return a.astype(BF16)


def wide(a):
    return a.astype(F32)


def dot_nn(left, right):
    return jnp.dot(left, right, preferred_element_type=F32)


def dot_nt(left, right):
    return lax.dot_general(left, right, (((1,), (1,)), ((), ())), preferred_element_type=F32)


def dot_tn(left, right):
    return lax.dot_general(left, right, (((0,), (0,)), ((), ())), preferred_element_type=F32)


def swap_core(v):
    return lax.ppermute(v, "seq", [(0, 1), (1, 0)])


def swap_mp(v, bits):
    return lax.ppermute(v, "mp", [(m, m ^ bits) for m in range(4)])


def spread_perm(flip):
    return [
        (s * 4 + y * 2 + x, y * 4 + (s ^ flip) * 2 + x)
        for s in range(2)
        for y in range(2)
        for x in range(2)
    ]


def spread(v, flip):
    return lax.ppermute(v, ("seq", "mp"), spread_perm(flip))


def unspread(v, flip):
    return lax.ppermute(v, ("seq", "mp"), [(d, s) for s, d in spread_perm(flip)])


def shift_dp(v, k):
    n = lax.axis_size("dp")
    return lax.ppermute(v, "dp", [(i, (i + k) % n) for i in range(n)])


def sum_dp(v):
    n = lax.axis_size("dp")
    if n > 4:
        return lax.psum(v, "dp")
    return v + sum(shift_dp(v, k) for k in range(1, n))


def gather_chunk(shard):
    n = lax.axis_size("dp")
    half = shard.shape[0] // 2
    if n > 4:
        whole = lax.all_gather(shard, "dp", axis=0, tiled=False)
        za, zb = whole[:, :half], whole[:, half:]
    else:
        blocks = [shard] + [shift_dp(shard, k) for k in range(1, n)]
        za = jnp.stack([b[:half] for b in blocks])
        zb = jnp.stack([b[half:] for b in blocks])
    ax = swap_mp(za, 1)
    first = [[spread(za, a) for a in range(2)], [spread(ax, a) for a in range(2)]]
    own = [spread(zb, a) for a in range(2)]
    second = [own, [swap_mp(b, 1) for b in own]]
    return [first, second]


def scatter_chunk(pieces):
    n = lax.axis_size("dp")
    first, second = pieces
    t = [sum(wide(unspread(first[dx][a], a)) for a in range(2)) for dx in range(2)]
    ta = wide(swap_mp(bf(t[1]), 1))
    u = [bf(wide(second[0][a]) + wide(swap_mp(second[1][a], 1))) for a in range(2)]
    tb = [wide(unspread(u[a], a)) for a in range(2)]
    if n > 4:
        whole = bf(jnp.concatenate([t[0] + ta, tb[0] + tb[1]], axis=1))
        return wide(lax.psum_scatter(whole, "dp", scatter_dimension=0, tiled=False))
    total = None
    for k in range(n):
        part = jnp.concatenate([t[0][k] + ta[k], tb[0][k] + tb[1][k]], axis=0)
        part = part if k == 0 else wide(shift_dp(bf(part), n - k))
        total = part if total is None else total + part
    return total


def pack_attn(shard):
    main, rest = shard[:, :, :PAIR], shard[:, :, PAIR:]
    return jnp.concatenate([main, jnp.concatenate([rest[0::2], rest[1::2]], axis=-1)], axis=0)


def unpack_attn(tiles, count):
    main, rest = tiles[:count], tiles[count:]
    left, right = rest[:, :, : PAIR // 2], rest[:, :, PAIR // 2 :]
    rest = jnp.stack([left, right], axis=1).reshape(count, tiles.shape[1], PAIR // 2)
    return jnp.concatenate([main, rest], axis=-1)


def half_lanes(shape):
    return lax.broadcasted_iota(jnp.int32, shape, len(shape) - 1) < PAIR // 2


def half_roll(v):
    return bf(pltpu.roll(wide(v), PAIR // 2, 1))


def assemble_attn(pieces, plans, count, zidx, yidx):
    flat = [pieces[h][dx][a] for h in range(2) for dx in range(2) for a in range(2)]
    n, half, rows, _ = flat[0].shape

    def kernel(zi, yi, *refs):
        ins, outs = refs[:8], refs[8:]
        low = half_lanes((rows, PAIR))
        for a in range(2):
            side = yi[a]

            def tile(t, dx):
                return ins[(t // half) * 4 + dx * 2 + a][0, t % half]

            for out, plan in zip(outs, plans):
                for place, (mat, j) in enumerate(plan):
                    if j < 2:
                        val = tile(mat, j)
                    else:
                        t0, t1 = tile(count + mat // 2, 0), tile(count + mat // 2, 1)
                        if mat % 2 == 0:
                            val = jnp.where(low, t0, half_roll(t1))
                        else:
                            val = jnp.where(low, half_roll(t0), t1)
                    out[0, side, :, place * PAIR : (place + 1) * PAIR] = val

    outs = pl.pallas_call(
        kernel,
        grid_spec=pltpu.PrefetchScalarGridSpec(
            num_scalar_prefetch=2,
            grid=(n,),
            in_specs=[pl.BlockSpec((1, half, rows, PAIR), lambda k, zi, yi: (k, 0, 0, 0))] * 8,
            out_specs=[
                pl.BlockSpec((1, 2, rows, PAIR * len(p)), lambda k, zi, yi: (zi[k], 0, 0, 0))
                for p in plans
            ],
        ),
        out_shape=[jax.ShapeDtypeStruct((n, 2, rows, PAIR * len(p)), BF16) for p in plans],
        cost_estimate=pl.CostEstimate(
            flops=0, transcendentals=0, bytes_accessed=2 * 8 * n * half * rows * PAIR * 2
        ),
        name="assemble_attn",
    )(zidx, yidx, *flat)
    return [o.reshape(n * 2 * rows, -1) for o in outs]


def split_attn(mats, plans, count, zidx, yidx):
    half = (count + count // 2) // 2
    n = zidx.shape[0]
    rows = mats[0].shape[0] // (2 * n)
    ins = [m.reshape(n, 2, rows, -1) for m in mats]
    where = {}
    for i, plan in enumerate(plans):
        for place, key in enumerate(plan):
            where[key] = (i, place)

    def kernel(zi, yi, *refs):
        srcs, outs = refs[: len(mats)], refs[len(mats) :]
        low = half_lanes((rows, PAIR))
        for a in range(2):
            side = yi[a]

            def get(mat, j):
                i, place = where[(mat, j)]
                return srcs[i][0, side, :, place * PAIR : (place + 1) * PAIR]

            for dx in range(2):
                for t in range(2 * half):
                    if t < count:
                        val = get(t, dx)
                    else:
                        p = t - count
                        t0, t1 = get(2 * p, 2), get(2 * p + 1, 2)
                        if dx == 0:
                            val = jnp.where(low, t0, half_roll(t1))
                        else:
                            val = jnp.where(low, half_roll(t0), t1)
                    outs[(t // half) * 4 + dx * 2 + a][0, t % half] = val

    outs = pl.pallas_call(
        kernel,
        grid_spec=pltpu.PrefetchScalarGridSpec(
            num_scalar_prefetch=2,
            grid=(n,),
            in_specs=[
                pl.BlockSpec((1, 2, rows, m.shape[-1]), lambda k, zi, yi: (zi[k], 0, 0, 0))
                for m in ins
            ],
            out_specs=[pl.BlockSpec((1, half, rows, PAIR), lambda k, zi, yi: (k, 0, 0, 0))] * 8,
        ),
        out_shape=[jax.ShapeDtypeStruct((n, half, rows, PAIR), BF16)] * 8,
        cost_estimate=pl.CostEstimate(
            flops=0, transcendentals=0, bytes_accessed=2 * 8 * n * half * rows * PAIR * 2
        ),
        name="split_attn",
    )(zidx, yidx, *ins)
    return [[[outs[h * 4 + dx * 2 + a] for a in range(2)] for dx in range(2)] for h in range(2)]


def assemble_ffn(pieces, zidx, yidx):
    flat = [pieces[h][dx][a] for h in range(2) for dx in range(2) for a in range(2)]
    n, _, rows, cols = flat[0].shape

    def kernel(zi, yi, *refs):
        ins, outs = refs[:8], refs[8:]
        for a in range(2):
            for h in range(2):
                for dx in range(2):
                    outs[h][0, yi[a], :, dx * cols : (dx + 1) * cols] = ins[h * 4 + dx * 2 + a][0, 0]

    outs = pl.pallas_call(
        kernel,
        grid_spec=pltpu.PrefetchScalarGridSpec(
            num_scalar_prefetch=2,
            grid=(n,),
            in_specs=[pl.BlockSpec((1, 1, rows, cols), lambda k, zi, yi: (k, 0, 0, 0))] * 8,
            out_specs=[
                pl.BlockSpec((1, 2, rows, 2 * cols), lambda k, zi, yi: (zi[k], 0, 0, 0))
            ]
            * 2,
        ),
        out_shape=[jax.ShapeDtypeStruct((n, 2, rows, 2 * cols), BF16)] * 2,
        cost_estimate=pl.CostEstimate(
            flops=0, transcendentals=0, bytes_accessed=2 * 8 * n * rows * cols * 2
        ),
        name="assemble_ffn",
    )(zidx, yidx, *flat)
    return [o.reshape(n * 2 * rows, 2 * cols) for o in outs]


def split_ffn(mats, zidx, yidx):
    n = zidx.shape[0]
    rows = mats[0].shape[0] // (2 * n)
    cols = mats[0].shape[1] // 2
    ins = [m.reshape(n, 2, rows, 2 * cols) for m in mats]

    def kernel(zi, yi, *refs):
        srcs, outs = refs[:2], refs[2:]
        for a in range(2):
            for h in range(2):
                for dx in range(2):
                    outs[h * 4 + dx * 2 + a][0, 0] = srcs[h][
                        0, yi[a], :, dx * cols : (dx + 1) * cols
                    ]

    outs = pl.pallas_call(
        kernel,
        grid_spec=pltpu.PrefetchScalarGridSpec(
            num_scalar_prefetch=2,
            grid=(n,),
            in_specs=[pl.BlockSpec((1, 2, rows, 2 * cols), lambda k, zi, yi: (zi[k], 0, 0, 0))] * 2,
            out_specs=[pl.BlockSpec((1, 1, rows, cols), lambda k, zi, yi: (k, 0, 0, 0))] * 8,
        ),
        out_shape=[jax.ShapeDtypeStruct((n, 1, rows, cols), BF16)] * 8,
        cost_estimate=pl.CostEstimate(
            flops=0, transcendentals=0, bytes_accessed=2 * 8 * n * rows * cols * 2
        ),
        name="split_ffn",
    )(zidx, yidx, *ins)
    return [[[outs[h * 4 + dx * 2 + a] for a in range(2)] for dx in range(2)] for h in range(2)]


def bias_tiles(line, blocks):
    heads, _, length = line.shape
    spans = 2 * blocks - 1
    width = 2 * BLOCK

    def kernel(line_ref, out_ref):
        row = lax.broadcasted_iota(jnp.int32, (8, width), 0)
        for d in range(spans):
            start = (spans - 1 - d) * BLOCK
            window = line_ref[0, :, start : start + width]
            turned = jnp.concatenate([window[:, BLOCK:], window[:, :BLOCK]], axis=1)
            tile = jnp.broadcast_to(turned, (8, width))
            for bit in (1, 2, 4):
                tile = jnp.where((row & bit) != 0, pltpu.roll(tile, bit, 1), tile)
            size = 8
            while size < BLOCK:
                tile = jnp.concatenate([tile, pltpu.roll(tile, size, 1)], axis=0)
                size *= 2
            out_ref[0, d] = tile[:, :BLOCK]

    return pl.pallas_call(
        kernel,
        grid=(heads,),
        in_specs=[pl.BlockSpec((1, 1, length), lambda h: (h, 0, 0))],
        out_specs=pl.BlockSpec((1, spans, BLOCK, BLOCK), lambda h: (h, 0, 0, 0)),
        out_shape=jax.ShapeDtypeStruct((heads, spans, BLOCK, BLOCK), F32),
        cost_estimate=pl.CostEstimate(
            flops=heads * spans * BLOCK * BLOCK * 8,
            transcendentals=0,
            bytes_accessed=heads * spans * BLOCK * BLOCK * 4,
        ),
        name="bias_tiles",
    )(line)


def diagonal_sums(tile):
    width = 2 * BLOCK
    t = jnp.concatenate([tile, jnp.zeros_like(tile)], axis=1)
    size = BLOCK
    while size > 8:
        size //= 2
        t = t[:size] + pltpu.roll(t[size:], width - size, 1)
    row = lax.broadcasted_iota(jnp.int32, (8, width), 0)
    for bit in (1, 2, 4):
        t = jnp.where((row & bit) != 0, pltpu.roll(t, width - bit, 1), t)
    return jnp.sum(t, axis=0, keepdims=True)


def head_keys(keys, limit, a):
    lane = lax.broadcasted_iota(jnp.int32, keys.shape, 1)
    place = lax.broadcasted_iota(jnp.int32, keys.shape, 0)
    mine = (lane // (PAIR // 2)) == a
    flag = jnp.where(place < limit, 0.0, MASK_VALUE)
    other = jnp.where(lane == (1 - a) * (PAIR // 2), flag, 0.0)
    return bf(jnp.where(mine, wide(keys), other))


def head_queries(queries, scale, a, mark):
    lane = lax.broadcasted_iota(jnp.int32, queries.shape, 1)
    mine = (lane // (PAIR // 2)) == a
    other = jnp.where(lane == (1 - a) * (PAIR // 2), mark, 0.0)
    return bf(jnp.where(mine, wide(queries) * scale, other))


def only_head(values, a):
    lane = lax.broadcasted_iota(jnp.int32, values.shape, 1)
    return bf(jnp.where((lane // (PAIR // 2)) == a, wide(values), 0.0))


def score_blocks(key_a, query_a, bias_ref, a, qb, key_blocks, causal):
    out = []
    for kb in range(key_blocks):
        st = dot_nt(key_a[kb * BLOCK : (kb + 1) * BLOCK], query_a)
        if bias_ref is not None:
            st = st + bias_ref[a, kb - qb + key_blocks - 1]
        if causal:
            kpos = lax.broadcasted_iota(jnp.int32, st.shape, 0)
            qpos = lax.broadcasted_iota(jnp.int32, st.shape, 1)
            st = jnp.where(kpos <= qpos, st, MASK_VALUE)
        out.append(st)
    return out


def attention_forward(queries, memory, limit, bias, causal, fused):
    query_len = queries.shape[0]
    key_len = query_len if fused else memory.shape[0]
    pairs = queries.shape[1] // ((3 if fused else 1) * PAIR)
    key_blocks, query_blocks = key_len // BLOCK, query_len // BLOCK
    scale = (PAIR // 2) ** (-0.5)

    def kernel(limit_ref, q_ref, *refs):
        refs = list(refs)
        kv_ref = q_ref if fused else refs.pop(0)
        bias_ref = refs.pop(0) if bias is not None else None
        c_ref, lse_ref = refs
        k0 = PAIR if fused else 0
        keys = kv_ref[:, k0 : k0 + PAIR]
        values = kv_ref[:, k0 + PAIR : k0 + 2 * PAIR]
        key_a = [head_keys(keys, limit_ref[0], a) for a in range(2)]

        def visit(qb):
            rows = pl.ds(pl.multiple_of(qb * BLOCK, BLOCK), BLOCK)
            q = q_ref[rows, 0:PAIR]
            parts = []
            for a in range(2):
                st = score_blocks(
                    key_a[a], head_queries(q, scale, a, 1.0), bias_ref, a, qb, key_blocks, causal
                )
                top = functools.reduce(
                    jnp.maximum, [jnp.max(b, axis=0, keepdims=True) for b in st]
                )
                ex = [jnp.exp(b - top) for b in st]
                total = sum(jnp.sum(b, axis=0, keepdims=True) for b in ex)
                ct = sum(
                    dot_tn(values[kb * BLOCK : (kb + 1) * BLOCK], bf(ex[kb]))
                    for kb in range(key_blocks)
                )
                parts.append(ct[a * (PAIR // 2) : (a + 1) * (PAIR // 2)] * (1.0 / total))
                lse_ref[0, a : a + 1, rows] = top + jnp.log(total)
            c_ref[rows, :] = bf(jnp.transpose(jnp.concatenate(parts, axis=0)))

        if query_blocks == 1:
            visit(0)
        else:
            pl.loop(0, query_blocks)(visit)

    in_specs = [pl.BlockSpec((query_len, (3 if fused else 1) * PAIR), lambda j, n: (0, j))]
    args = [queries]
    if not fused:
        in_specs.append(pl.BlockSpec((key_len, 2 * PAIR), lambda j, n: (0, j)))
        args.append(memory)
    if bias is not None:
        in_specs.append(pl.BlockSpec((2,) + bias.shape[1:], lambda j, n: (j, 0, 0, 0)))
        args.append(bias)
    return pl.pallas_call(
        kernel,
        grid_spec=pltpu.PrefetchScalarGridSpec(
            num_scalar_prefetch=1,
            grid=(pairs,),
            in_specs=in_specs,
            out_specs=[
                pl.BlockSpec((query_len, PAIR), lambda j, n: (0, j)),
                pl.BlockSpec((1, 8, query_len), lambda j, n: (j, 0, 0)),
            ],
        ),
        out_shape=[
            jax.ShapeDtypeStruct((query_len, pairs * PAIR), BF16),
            jax.ShapeDtypeStruct((pairs, 8, query_len), F32),
        ],
        compiler_params=pltpu.CompilerParams(vmem_limit_bytes=40 << 20),
        cost_estimate=pl.CostEstimate(
            flops=pairs * 2 * query_len * key_len * PAIR * 4,
            transcendentals=pairs * 2 * query_len * key_len,
            bytes_accessed=pairs * PAIR * 2 * 2 * (query_len + key_len),
        ),
        name="attend_" + ("enc" if bias is not None else "dec" if fused else "cross"),
    )(limit, *args)


def attention_backward(queries, memory, limit, bias, causal, fused, context, lse, context_grad):
    query_len = queries.shape[0]
    key_len = query_len if fused else memory.shape[0]
    pairs = queries.shape[1] // ((3 if fused else 1) * PAIR)
    key_blocks, query_blocks = key_len // BLOCK, query_len // BLOCK
    spans = 2 * key_blocks - 1
    scale = (PAIR // 2) ** (-0.5)

    def kernel(limit_ref, q_ref, *refs):
        refs = list(refs)
        kv_ref = q_ref if fused else refs.pop(0)
        bias_ref = refs.pop(0) if bias is not None else None
        c_ref, lse_ref, dc_ref = refs[:3]
        refs = refs[3:]
        dq_ref = refs.pop(0)
        dkv_ref = dq_ref if fused else refs.pop(0)
        diag_ref = refs.pop(0) if bias is not None else None
        dk_acc, dv_acc = refs[:2]
        tile_acc = refs[2] if bias is not None else None
        k0 = PAIR if fused else 0
        keys = kv_ref[:, k0 : k0 + PAIR]
        values = kv_ref[:, k0 + PAIR : k0 + 2 * PAIR]
        key_a = [head_keys(keys, limit_ref[0], a) for a in range(2)]
        pure_key_a = [only_head(keys, a) for a in range(2)]
        value_a = [only_head(values, a) for a in range(2)]
        dk_acc[...] = jnp.zeros_like(dk_acc)
        dv_acc[...] = jnp.zeros_like(dv_acc)
        if bias is not None:
            tile_acc[...] = jnp.zeros_like(tile_acc)

        def visit(qb):
            rows = pl.ds(pl.multiple_of(qb * BLOCK, BLOCK), BLOCK)
            q = q_ref[rows, 0:PAIR]
            dc = dc_ref[rows, :]
            both = jnp.transpose(wide(dc) * wide(c_ref[rows, :]))
            dqt = jnp.zeros((PAIR, BLOCK), F32)
            for a in range(2):
                st = score_blocks(
                    key_a[a], head_queries(q, scale, a, 1.0), bias_ref, a, qb, key_blocks, causal
                )
                delta = jnp.sum(
                    both[a * (PAIR // 2) : (a + 1) * (PAIR // 2)], axis=0, keepdims=True
                )
                log_row = lse_ref[0, a : a + 1, rows]
                dc_a = only_head(dc, a)
                q_a = head_queries(q, scale, a, 0.0)
                for kb in range(key_blocks):
                    span = slice(kb * BLOCK, (kb + 1) * BLOCK)
                    p = jnp.exp(st[kb] - log_row)
                    dp = dot_nt(value_a[a][span], dc)
                    ds = p * (dp - delta)
                    dsb = bf(ds)
                    dv_acc[span, :] += dot_nn(bf(p), dc_a)
                    dk_acc[span, :] += dot_nn(dsb, q_a)
                    dqt = dqt + dot_tn(pure_key_a[a][span], dsb)
                    if bias is not None:
                        tile_acc[a, kb - qb + key_blocks - 1] += ds
            dq_ref[rows, 0:PAIR] = bf(jnp.transpose(dqt) * scale)

        if query_blocks == 1:
            visit(0)
        else:
            pl.loop(0, query_blocks)(visit)
        dkv_ref[:, k0 : k0 + PAIR] = bf(dk_acc[...])
        dkv_ref[:, k0 + PAIR : k0 + 2 * PAIR] = bf(dv_acc[...])
        if bias is not None:
            for a in range(2):
                for d in range(spans):
                    diag_ref[a, d : d + 1, :] = diagonal_sums(tile_acc[a, d])

    in_specs = [pl.BlockSpec((query_len, (3 if fused else 1) * PAIR), lambda j, n: (0, j))]
    args = [queries]
    if not fused:
        in_specs.append(pl.BlockSpec((key_len, 2 * PAIR), lambda j, n: (0, j)))
        args.append(memory)
    if bias is not None:
        in_specs.append(pl.BlockSpec((2,) + bias.shape[1:], lambda j, n: (j, 0, 0, 0)))
        args.append(bias)
    in_specs += [
        pl.BlockSpec((query_len, PAIR), lambda j, n: (0, j)),
        pl.BlockSpec((1, 8, query_len), lambda j, n: (j, 0, 0)),
        pl.BlockSpec((query_len, PAIR), lambda j, n: (0, j)),
    ]
    args += [context, lse, context_grad]
    out_specs = [pl.BlockSpec((query_len, (3 if fused else 1) * PAIR), lambda j, n: (0, j))]
    out_shape = [jax.ShapeDtypeStruct(queries.shape, BF16)]
    scratch = [pltpu.VMEM((key_len, PAIR), F32)] * 2
    if not fused:
        out_specs.append(pl.BlockSpec((key_len, 2 * PAIR), lambda j, n: (0, j)))
        out_shape.append(jax.ShapeDtypeStruct(memory.shape, BF16))
    if bias is not None:
        out_specs.append(pl.BlockSpec((2, 8, 2 * BLOCK), lambda j, n: (j, 0, 0)))
        out_shape.append(jax.ShapeDtypeStruct((2 * pairs, 8, 2 * BLOCK), F32))
        scratch.append(pltpu.VMEM((2, spans, BLOCK, BLOCK), F32))
    return pl.pallas_call(
        kernel,
        grid_spec=pltpu.PrefetchScalarGridSpec(
            num_scalar_prefetch=1,
            grid=(pairs,),
            in_specs=in_specs,
            out_specs=out_specs,
            scratch_shapes=scratch,
        ),
        out_shape=out_shape,
        compiler_params=pltpu.CompilerParams(vmem_limit_bytes=40 << 20),
        cost_estimate=pl.CostEstimate(
            flops=pairs * 2 * query_len * key_len * PAIR * 10,
            transcendentals=pairs * 2 * query_len * key_len,
            bytes_accessed=pairs * PAIR * 2 * 4 * (query_len + key_len),
        ),
        name="attend_back_" + ("enc" if bias is not None else "dec" if fused else "cross"),
    )(limit, *args)


def gelu(z):
    return z * (0.5 * (1.0 + lax.erf(z * ROOT_HALF)))


def gelu_slope(z):
    return 0.5 * (1.0 + lax.erf(z * ROOT_HALF)) + z * jnp.exp(-0.5 * z * z) * INV_ROOT_TAU


def norm_forward(values, gain, offset):
    center = values - jnp.mean(values, axis=-1, keepdims=True)
    inv = lax.rsqrt(jnp.mean(center * center, axis=-1, keepdims=True) + EPSILON)
    normed = center * inv
    return normed * gain + offset, normed, inv


def norm_backward(upstream, normed, inv, gain):
    scaled = upstream * gain
    inner = (
        scaled
        - jnp.mean(scaled, axis=-1, keepdims=True)
        - normed * jnp.mean(scaled * normed, axis=-1, keepdims=True)
    )
    return inv * inner, jnp.sum(upstream * normed, axis=0), jnp.sum(upstream, axis=0)


def update(master, moment, average, gradient, rate, frame_total):
    mean_grad = gradient / frame_total
    new_moment = MOMENTUM * moment + mean_grad
    new_master = master - rate * (mean_grad + MOMENTUM * new_moment)
    new_average = AVERAGING * average + (1.0 - AVERAGING) * new_master
    return mean_grad, new_master, new_moment, new_average


def both_cores(part):
    low = bf(part)
    return wide(low) + wide(swap_core(low))


def order_cols(v0, v1):
    return jnp.concatenate(
        [v0[..., :PAIR], v1[..., :PAIR], v0[..., PAIR:], v1[..., PAIR:]], axis=-1
    )


def group_cols(v):
    half = PAIR // 2
    return (
        jnp.concatenate([v[..., :PAIR], v[..., 2 * PAIR : 2 * PAIR + half]], axis=-1),
        jnp.concatenate([v[..., PAIR : 2 * PAIR], v[..., 2 * PAIR + half :]], axis=-1),
    )


QKV_PLAN = [(m, j) for j in range(3) for m in range(3)]
ENC_PLANS = [QKV_PLAN, [(3, j) for j in range(3)]]
DEC_PLANS = [
    QKV_PLAN,
    [(3, j) for j in range(3)],
    [(4, j) for j in range(3)],
    [(m, j) for j in range(3) for m in (5, 6)],
    [(7, j) for j in range(3)],
]


def local(
    frames,
    cotangent,
    lengths,
    attn_master,
    attn_moment,
    attn_average,
    ffn_master,
    ffn_moment,
    ffn_average,
    norm_vecs,
    norm_moment,
    norm_average,
    col_bias,
    col_moment,
    col_average,
    rel_table,
    rel_moment,
    rel_average,
    dec_frames,
    dec_cotangent,
    text_lengths,
    dec_attn_master,
    dec_attn_moment,
    dec_attn_average,
    dec_ffn_master,
    dec_ffn_moment,
    dec_ffn_average,
    dec_norm_vecs,
    dec_norm_moment,
    dec_norm_average,
    dec_col_bias,
    dec_col_moment,
    dec_col_average,
):
    n_dp = lax.axis_size("dp")
    z, s, m = lax.axis_index("dp"), lax.axis_index("seq"), lax.axis_index("mp")
    y = m // 2
    utt_count, half_len, width = frames.shape
    text_half = dec_frames.shape[1]
    full_len, text_full = 2 * half_len, 2 * text_half
    order = jnp.arange(n_dp, dtype=jnp.int32)
    zidx = order if n_dp > 4 else (z - order) % n_dp
    yidx = jnp.stack([y, 1 - y]).astype(jnp.int32)
    root_frames = float(utt_count * full_len * n_dp) ** 0.5

    attn_pieces = gather_chunk(pack_attn(bf(attn_master)))
    ffn_pieces = gather_chunk(bf(ffn_master))
    dec_attn_pieces = gather_chunk(pack_attn(bf(dec_attn_master)))
    dec_ffn_pieces = gather_chunk(bf(dec_ffn_master))
    w_qkv, w_o = assemble_attn(attn_pieces, ENC_PLANS, 4, zidx, yidx)
    w_one, w_two = assemble_ffn(ffn_pieces, zidx, yidx)
    d_qkv, d_o, c_q, c_kv, c_o = assemble_attn(dec_attn_pieces, DEC_PLANS, 8, zidx, yidx)
    dw_one, dw_two = assemble_ffn(dec_ffn_pieces, zidx, yidx)

    bucket_count, group_heads = rel_table.shape
    group_width = attn_master.shape[2]
    unit_count = ffn_master.shape[2]
    packed = jnp.concatenate([col_bias, dec_col_bias, rel_table.T.reshape(-1)])
    groups = [spread(packed, 0), None]
    groups[1] = swap_mp(groups[0], 1)
    enc_cols, dec_cols = col_bias.shape[0], dec_col_bias.shape[0]

    def cols_at(start):
        return order_cols(*[g[start : start + group_width] for g in groups])

    def units_at(start):
        return jnp.concatenate([g[start : start + unit_count] for g in groups])

    def qkv_bias(q, v):
        blank = jnp.zeros((PAIR,), F32)
        cut = [slice(j * PAIR, (j + 1) * PAIR) for j in range(3)]
        return jnp.concatenate([part for c in cut for part in (q[c], blank, v[c])])

    bias_qkv = qkv_bias(cols_at(0), cols_at(group_width))
    bias_one = units_at(2 * group_width)
    bias_dqkv = qkv_bias(cols_at(enc_cols), cols_at(enc_cols + group_width))
    bias_cq = cols_at(enc_cols + 2 * group_width)
    cv = cols_at(enc_cols + 3 * group_width)
    blank = jnp.zeros((PAIR,), F32)
    bias_ckv = jnp.concatenate(
        [part for j in range(3) for part in (blank, cv[j * PAIR : (j + 1) * PAIR])]
    )
    bias_done = units_at(enc_cols + 4 * group_width)
    tables = [
        g[enc_cols + dec_cols :].reshape(group_heads, bucket_count) for g in groups
    ]
    heads = jnp.stack(
        [tables[0][0], tables[0][1], tables[1][0], tables[1][1], tables[0][2], tables[1][2]]
    )
    max_dist = bucket_count // 2
    blocks = full_len // BLOCK
    before = blocks * BLOCK - max_dist + 1
    after = blocks * BLOCK - max_dist - 1
    line = jnp.pad(heads[:, ::-1], ((0, 0), (before, after)), mode="edge")
    bias = bias_tiles(line[:, None, :], blocks)

    def all_rows(parts):
        mine = lax.dynamic_index_in_dim(parts, m, 0, keepdims=False)
        other = swap_core(mine)
        first = jnp.where(s == 0, mine, other)
        last = jnp.where(s == 0, other, mine)
        return jnp.concatenate([first, last], axis=0)

    inputs = all_rows(frames)
    text_in = all_rows(dec_frames)
    upstream_in = all_rows(cotangent)
    text_upstream = all_rows(dec_cotangent)
    limit = lax.dynamic_slice_in_dim(lengths, m, 1)
    text_limit = lax.dynamic_slice_in_dim(text_lengths, m, 1)
    frame_total = sum_dp(jnp.broadcast_to(wide(jnp.sum(lengths)), (8, 128)))[0, 0]

    def to_owners(rows):
        count = rows.shape[0] // 2
        mine = lax.dynamic_slice_in_dim(rows, s * count, count, 0)
        cut = count // 2
        a, b = mine[:cut], mine[cut:]
        ax, by = swap_mp(a, 1), swap_mp(b, 2)
        ay, axy = swap_mp(a, 2), swap_mp(ax, 2)
        bx, byx = swap_mp(b, 1), swap_mp(by, 1)
        out = jnp.zeros((utt_count, count, width), rows.dtype)
        for bits, top, low in ((0, a, b), (1, ax, bx), (2, ay, by), (3, axy, byx)):
            out = lax.dynamic_update_slice(out, top[None], (m ^ bits, 0, 0))
            out = lax.dynamic_update_slice(out, low[None], (m ^ bits, cut, 0))
        return out

    qkv = bf(dot_nn(inputs, w_qkv) + bias_qkv)
    context, lse = attention_forward(qkv, None, limit, bias, False, True)
    attn_sum = both_cores(dot_nt(context, w_o))
    hidden_one, normed_one, inv_one = norm_forward(
        wide(inputs) + attn_sum + norm_vecs[4], norm_vecs[0], norm_vecs[1]
    )
    hidden_low = bf(hidden_one)
    gate_in = dot_nn(hidden_low, w_one) + bias_one
    activated = bf(gelu(gate_in))
    ffn_sum = both_cores(dot_nt(activated, w_two))
    result, normed_two, inv_two = norm_forward(
        hidden_one + ffn_sum + norm_vecs[5], norm_vecs[2], norm_vecs[3]
    )
    enc_low = bf(result)
    out_enc = to_owners(enc_low)

    dqkv = bf(dot_nn(text_in, d_qkv) + bias_dqkv)
    self_context, self_lse = attention_forward(dqkv, None, text_limit, None, True, True)
    self_sum = both_cores(dot_nt(self_context, d_o))
    dec_one, normed_d1, inv_d1 = norm_forward(
        wide(text_in) + self_sum + dec_norm_vecs[6], dec_norm_vecs[0], dec_norm_vecs[1]
    )
    dec_one_low = bf(dec_one)
    cross_q = bf(dot_nn(dec_one_low, c_q) + bias_cq)
    cross_kv = bf(dot_nn(enc_low, c_kv) + bias_ckv)
    cross_context, cross_lse = attention_forward(cross_q, cross_kv, limit, None, False, False)
    cross_sum = both_cores(dot_nt(cross_context, c_o))
    dec_two, normed_d2, inv_d2 = norm_forward(
        dec_one + cross_sum + dec_norm_vecs[7], dec_norm_vecs[2], dec_norm_vecs[3]
    )
    dec_two_low = bf(dec_two)
    dec_gate = dot_nn(dec_two_low, dw_one) + bias_done
    dec_act = bf(gelu(dec_gate))
    dec_ffn_sum = both_cores(dot_nt(dec_act, dw_two))
    dec_result, normed_d3, inv_d3 = norm_forward(
        dec_two + dec_ffn_sum + dec_norm_vecs[8], dec_norm_vecs[4], dec_norm_vecs[5]
    )
    out_dec = to_owners(bf(dec_result))

    text_places = lax.broadcasted_iota(jnp.int32, (text_full, 1), 0)
    dec_up = jnp.where(text_places < text_limit[0], wide(text_upstream), 0.0)
    grad_d3, gain_d3, shift_d3 = norm_backward(dec_up, normed_d3, inv_d3, dec_norm_vecs[4])
    dec_ffn_back = bf(grad_d3)
    dec_gate_grad = bf(dot_nn(dec_ffn_back, dw_two) * gelu_slope(dec_gate))
    grad_h2 = grad_d3 + both_cores(dot_nt(dec_gate_grad, dw_one))
    dec_ffn_grads = [
        bf(dot_tn(dec_two_low, dec_gate_grad)),
        bf(dot_tn(dec_ffn_back, dec_act)),
    ]
    dec_ffn_total = scatter_chunk(split_ffn(dec_ffn_grads, zidx, yidx))

    grad_d2, gain_d2, shift_d2 = norm_backward(grad_h2, normed_d2, inv_d2, dec_norm_vecs[2])
    cross_back = bf(grad_d2)
    cross_qg, cross_kvg = attention_backward(
        cross_q,
        cross_kv,
        limit,
        None,
        False,
        False,
        cross_context,
        cross_lse,
        bf(dot_nn(cross_back, c_o)),
    )
    memory_back = both_cores(dot_nt(cross_kvg, c_kv))
    grad_h1 = grad_d2 + both_cores(dot_nt(cross_qg, c_q))
    grad_d1, gain_d1, shift_d1 = norm_backward(grad_h1, normed_d1, inv_d1, dec_norm_vecs[0])
    self_back = bf(grad_d1)
    (self_g,) = attention_backward(
        dqkv,
        None,
        text_limit,
        None,
        True,
        True,
        self_context,
        self_lse,
        bf(dot_nn(self_back, d_o)),
    )
    text_grad = grad_d1 + both_cores(dot_nt(self_g, d_qkv))
    dec_attn_grads = [
        bf(dot_tn(text_in, self_g)),
        bf(dot_tn(self_back, self_context)),
        bf(dot_tn(dec_one_low, cross_qg)),
        bf(dot_tn(enc_low, cross_kvg)),
        bf(dot_tn(cross_back, cross_context)),
    ]
    dec_attn_total = unpack_attn(
        scatter_chunk(split_attn(dec_attn_grads, DEC_PLANS, 8, zidx, yidx)), 8
    )
    out_text_grad = to_owners(bf(text_grad))

    places = lax.broadcasted_iota(jnp.int32, (full_len, 1), 0)
    upstream = jnp.where(places < limit[0], wide(upstream_in), 0.0) + memory_back
    grad_two, gain_two, shift_two = norm_backward(upstream, normed_two, inv_two, norm_vecs[2])
    ffn_back = bf(grad_two)
    gate_grad = bf(dot_nn(ffn_back, w_two) * gelu_slope(gate_in))
    hidden_grad = grad_two + both_cores(dot_nt(gate_grad, w_one))
    ffn_grads = [bf(dot_tn(hidden_low, gate_grad)), bf(dot_tn(ffn_back, activated))]
    ffn_total = scatter_chunk(split_ffn(ffn_grads, zidx, yidx))
    grad_one, gain_one, shift_one = norm_backward(hidden_grad, normed_one, inv_one, norm_vecs[0])
    attn_back = bf(grad_one)
    enc_g, diag = attention_backward(
        qkv, None, limit, bias, False, True, context, lse, bf(dot_nn(attn_back, w_o))
    )
    input_grad = grad_one + both_cores(dot_nt(enc_g, w_qkv))
    attn_grads = [bf(dot_tn(inputs, enc_g)), bf(dot_tn(attn_back, context))]
    attn_total = unpack_attn(
        scatter_chunk(split_attn(attn_grads, ENC_PLANS, 4, zidx, yidx)), 4
    )
    out_input_grad = to_owners(bf(input_grad))

    def col_sum(a):
        return jnp.sum(a, axis=0, dtype=F32)

    def pick(v, stride, at):
        return jnp.concatenate(
            [v[(j * stride + at) * PAIR : (j * stride + at + 1) * PAIR] for j in range(3)]
        )

    enc_sum, dec_sum, kv_sum = col_sum(enc_g), col_sum(self_g), col_sum(cross_kvg)
    col_parts = [
        group_cols(pick(enc_sum, 3, 0)),
        group_cols(pick(enc_sum, 3, 2)),
        jnp.split(col_sum(gate_grad), 2),
        group_cols(pick(dec_sum, 3, 0)),
        group_cols(pick(dec_sum, 3, 2)),
        group_cols(col_sum(cross_qg)),
        group_cols(pick(kv_sum, 2, 1)),
        jnp.split(col_sum(dec_gate_grad), 2),
    ]
    turned = jnp.concatenate([diag[:, :, BLOCK:], diag[:, :, :BLOCK]], axis=-1)
    span_count = 2 * blocks - 1
    line_grad = sum(
        jnp.pad(
            turned[:, d],
            ((0, 0), ((span_count - 1 - d) * BLOCK, d * BLOCK)),
        )
        for d in range(span_count)
    )
    first_bucket = jnp.sum(line_grad[:, before + bucket_count :], axis=1, keepdims=True)
    last_bucket = jnp.sum(line_grad[:, :before], axis=1, keepdims=True)
    head_grad = line_grad[:, before : before + bucket_count][:, ::-1]
    head_grad = jnp.concatenate(
        [
            head_grad[:, :1] + first_bucket,
            head_grad[:, 1:-1],
            head_grad[:, -1:] + last_bucket,
        ],
        axis=1,
    )
    table_parts = (head_grad[jnp.array([0, 1, 4])], head_grad[jnp.array([2, 3, 5])])
    norm_local = jnp.stack(
        [gain_one, shift_one, gain_two, shift_two, jnp.sum(grad_one, 0), jnp.sum(grad_two, 0)]
    )
    dec_norm_local = jnp.stack(
        [
            gain_d1,
            shift_d1,
            gain_d2,
            shift_d2,
            gain_d3,
            shift_d3,
            jnp.sum(grad_d1, 0),
            jnp.sum(grad_d2, 0),
            jnp.sum(grad_d3, 0),
        ]
    )
    shared = jnp.concatenate([norm_local.reshape(-1), dec_norm_local.reshape(-1)])
    vectors = [
        jnp.concatenate([p[dx] for p in col_parts] + [table_parts[dx].reshape(-1), shared])
        for dx in range(2)
    ]
    small = unspread(vectors[0] + swap_mp(vectors[1], 1), 0)
    small = sum_dp(small + swap_core(small))
    cut = [enc_cols, dec_cols, group_heads * bucket_count, norm_vecs.size, dec_norm_vecs.size]
    ends = [sum(cut[: i + 1]) for i in range(len(cut))]
    col_total, dec_col_total, table_total, norm_total, dec_norm_total, _ = jnp.split(small, ends)
    table_total = table_total.reshape(group_heads, bucket_count).T
    norm_total = norm_total.reshape(norm_vecs.shape)
    dec_norm_total = dec_norm_total.reshape(dec_norm_vecs.shape)

    matrix_rate = MATRIX_RATE * root_frames
    vector_rate = VECTOR_RATE * root_frames
    attn_new = update(attn_master, attn_moment, attn_average, attn_total, matrix_rate, frame_total)
    ffn_new = update(ffn_master, ffn_moment, ffn_average, ffn_total, matrix_rate, frame_total)
    norm_new = update(norm_vecs, norm_moment, norm_average, norm_total, vector_rate, frame_total)
    col_new = update(col_bias, col_moment, col_average, col_total, vector_rate, frame_total)
    rel_new = update(rel_table, rel_moment, rel_average, table_total, vector_rate, frame_total)
    dattn_new = update(
        dec_attn_master, dec_attn_moment, dec_attn_average, dec_attn_total, matrix_rate, frame_total
    )
    dffn_new = update(
        dec_ffn_master, dec_ffn_moment, dec_ffn_average, dec_ffn_total, matrix_rate, frame_total
    )
    dnorm_new = update(
        dec_norm_vecs, dec_norm_moment, dec_norm_average, dec_norm_total, vector_rate, frame_total
    )
    dcol_new = update(
        dec_col_bias, dec_col_moment, dec_col_average, dec_col_total, vector_rate, frame_total
    )
    return (
        out_enc,
        out_input_grad,
        attn_new[0],
        ffn_new[0],
        *attn_new[1:],
        bf(attn_new[1]),
        *ffn_new[1:],
        bf(ffn_new[1]),
        *norm_new[1:],
        *col_new[1:],
        *rel_new[1:],
        out_dec,
        out_text_grad,
        dattn_new[0],
        dffn_new[0],
        *dattn_new[1:],
        bf(dattn_new[1]),
        *dffn_new[1:],
        bf(dffn_new[1]),
        *dnorm_new[1:],
        *dcol_new[1:],
    )


def solution(mesh):
    rows = P("dp", "seq", None)
    matrix = P(None, ("dp", "seq"), "mp")
    table = P(None, "mp")
    enc_params = [matrix] * 6 + [P()] * 3 + [P("mp")] * 3 + [table] * 3
    dec_params = [matrix] * 6 + [P()] * 3 + [P("mp")] * 3
    in_specs = (rows, rows, P("dp"), *enc_params, rows, rows, P("dp"), *dec_params)
    out_specs = (
        [rows, rows]
        + [matrix] * 10
        + [P()] * 3
        + [P("mp")] * 3
        + [table] * 3
        + [rows, rows]
        + [matrix] * 10
        + [P()] * 3
        + [P("mp")] * 3
    )
    return jax.shard_map(
        local, mesh=mesh, in_specs=in_specs, out_specs=tuple(out_specs), check_vma=False
    )
```

```python
import functools

import jax
import jax.numpy as jnp
from jax import lax
from jax.experimental import pallas as pl
from jax.experimental.pallas import tpu as pltpu
from jax.sharding import PartitionSpec as P

EPSILON = 1e-05
MOMENTUM = 0.9
AVERAGING = 0.75
MATRIX_RATE = 0.02
VECTOR_RATE = 0.2
MASK_VALUE = -1e30
ROOT_HALF = 0.7071067811865476
INV_ROOT_TAU = 0.3989422804014327
BLOCK = 256
PAIR = 128
BF16 = jnp.bfloat16
F32 = jnp.float32


def bf(a):
    return a.astype(BF16)


def wide(a):
    return a.astype(F32)


def dot_nn(left, right):
    return jnp.dot(left, right, preferred_element_type=F32)


def dot_nt(left, right):
    return lax.dot_general(left, right, (((1,), (1,)), ((), ())), preferred_element_type=F32)


def dot_tn(left, right):
    return lax.dot_general(left, right, (((0,), (0,)), ((), ())), preferred_element_type=F32)


def swap_core(v):
    return lax.ppermute(v, "seq", [(0, 1), (1, 0)])


def swap_mp(v, bits):
    return lax.ppermute(v, "mp", [(m, m ^ bits) for m in range(4)])


def spread_perm(dx, flip):
    pairs = [
        (s * 4 + y * 2 + x, y * 4 + (s ^ flip) * 2 + (x ^ dx))
        for s in range(2)
        for y in range(2)
        for x in range(2)
    ]
    return [(a, b) for a, b in pairs if a != b]


ROUTES = [(dx, flip) for dx in range(2) for flip in range(2)]


def spread(v, dx, flip):
    return lax.ppermute(v, ("seq", "mp"), spread_perm(dx, flip))


def unspread(v, dx, flip):
    return lax.ppermute(v, ("seq", "mp"), [(d, s) for s, d in spread_perm(dx, flip)])


def sum_dp(v):
    n = lax.axis_size("dp")
    if n != 4:
        return lax.psum(v, "dp")
    for bits in (1, 2):
        v = v + lax.ppermute(v, "dp", [(i, i ^ bits) for i in range(n)])
    return v


def stage(*values):
    return lax.optimization_barrier(values)


def after(values, *others):
    return lax.optimization_barrier((values, others))[0]


def gather_dp(shard):
    return lax.all_gather(shard, "dp", axis=0, tiled=False)


def scatter_dp(whole):
    return lax.psum_scatter(whole, "dp", scatter_dimension=0, tiled=False)


def gather_plane(v):
    return [v] + [spread(v, dx, flip) for dx, flip in ROUTES]


def scatter_plane(pieces):
    return [unspread(p, dx, flip) for p, (dx, flip) in zip(pieces, ROUTES)]


def sum_plane(pieces, back, own):
    first = jnp.where(own, wide(pieces[0]), wide(back[0]))
    return bf(first + sum(wide(b) for b in back[1:]))


def pack_attn(shard):
    main, rest = shard[:, :, :PAIR], shard[:, :, PAIR:]
    return jnp.concatenate([main, jnp.concatenate([rest[0::2], rest[1::2]], axis=-1)], axis=0)


def half_lanes(shape):
    return lax.broadcasted_iota(jnp.int32, shape, len(shape) - 1) < PAIR // 2


def half_roll(v):
    return bf(pltpu.roll(wide(v), PAIR // 2, 1))


def assemble_attn(pieces, plans, count, yidx):
    n, tiles, rows, _ = pieces[0].shape

    def kernel(yi, *refs):
        ins, outs = refs[:5], refs[5:]
        low = half_lanes((rows, PAIR))
        for a in range(2):
            side = yi[a]

            def tile(t, dx):
                val = ins[1 + dx * 2 + a][0, t]
                return jnp.where(yi[2] == 1, ins[0][0, t], val) if dx + a == 0 else val

            for out, plan in zip(outs, plans):
                for place, (mat, j) in enumerate(plan):
                    if j < 2:
                        val = tile(mat, j)
                    else:
                        t0, t1 = tile(count + mat // 2, 0), tile(count + mat // 2, 1)
                        if mat % 2 == 0:
                            val = jnp.where(low, t0, half_roll(t1))
                        else:
                            val = jnp.where(low, half_roll(t0), t1)
                    out[0, side, :, place * PAIR : (place + 1) * PAIR] = val

    outs = pl.pallas_call(
        kernel,
        grid_spec=pltpu.PrefetchScalarGridSpec(
            num_scalar_prefetch=1,
            grid=(n,),
            in_specs=[pl.BlockSpec((1, tiles, rows, PAIR), lambda k, yi: (k, 0, 0, 0))] * 5,
            out_specs=[
                pl.BlockSpec((1, 2, rows, PAIR * len(p)), lambda k, yi: (k, 0, 0, 0))
                for p in plans
            ],
        ),
        out_shape=[jax.ShapeDtypeStruct((n, 2, rows, PAIR * len(p)), BF16) for p in plans],
        cost_estimate=pl.CostEstimate(
            flops=0, transcendentals=0, bytes_accessed=9 * n * tiles * rows * PAIR * 2
        ),
        name="assemble_attn",
    )(yidx, *pieces)
    return [o.reshape(n * 2 * rows, -1) for o in outs]


def split_attn(mats, plans, count, n, yidx):
    tiles = count + count // 2
    rows = mats[0].shape[0] // (2 * n)
    ins = [m.reshape(n, 2, rows, -1) for m in mats]
    where = {}
    for i, plan in enumerate(plans):
        for place, key in enumerate(plan):
            where[key] = (i, place)

    def kernel(yi, *refs):
        srcs, outs = refs[: len(mats)], refs[len(mats) :]
        low = half_lanes((rows, PAIR))
        for a in range(2):
            side = yi[a]

            def get(mat, j):
                i, place = where[(mat, j)]
                return srcs[i][0, side, :, place * PAIR : (place + 1) * PAIR]

            for dx in range(2):
                for t in range(tiles):
                    if t < count:
                        val = get(t, dx)
                    else:
                        p = t - count
                        t0, t1 = get(2 * p, 2), get(2 * p + 1, 2)
                        if dx == 0:
                            val = jnp.where(low, t0, half_roll(t1))
                        else:
                            val = jnp.where(low, half_roll(t0), t1)
                    outs[dx * 2 + a][0, t] = val

    outs = pl.pallas_call(
        kernel,
        grid_spec=pltpu.PrefetchScalarGridSpec(
            num_scalar_prefetch=1,
            grid=(n,),
            in_specs=[
                pl.BlockSpec((1, 2, rows, m.shape[-1]), lambda k, yi: (k, 0, 0, 0))
                for m in ins
            ],
            out_specs=[pl.BlockSpec((1, tiles, rows, PAIR), lambda k, yi: (k, 0, 0, 0))] * 4,
        ),
        out_shape=[jax.ShapeDtypeStruct((n, tiles, rows, PAIR), BF16)] * 4,
        cost_estimate=pl.CostEstimate(
            flops=0, transcendentals=0, bytes_accessed=8 * n * tiles * rows * PAIR * 2
        ),
        name="split_attn",
    )(yidx, *ins)
    return outs


def assemble_ffn(pieces, yidx):
    n, _, rows, cols = pieces[0].shape

    def kernel(yi, *refs):
        ins, outs = refs[:5], refs[5:]
        for a in range(2):
            for h in range(2):
                for dx in range(2):
                    val = ins[1 + dx * 2 + a][0, h]
                    val = jnp.where(yi[2] == 1, ins[0][0, h], val) if dx + a == 0 else val
                    outs[h][0, yi[a], :, dx * cols : (dx + 1) * cols] = val

    outs = pl.pallas_call(
        kernel,
        grid_spec=pltpu.PrefetchScalarGridSpec(
            num_scalar_prefetch=1,
            grid=(n,),
            in_specs=[pl.BlockSpec((1, 2, rows, cols), lambda k, yi: (k, 0, 0, 0))] * 5,
            out_specs=[
                pl.BlockSpec((1, 2, rows, 2 * cols), lambda k, yi: (k, 0, 0, 0))
            ]
            * 2,
        ),
        out_shape=[jax.ShapeDtypeStruct((n, 2, rows, 2 * cols), BF16)] * 2,
        cost_estimate=pl.CostEstimate(
            flops=0, transcendentals=0, bytes_accessed=2 * 9 * n * rows * cols * 2
        ),
        name="assemble_ffn",
    )(yidx, *pieces)
    return [o.reshape(n * 2 * rows, 2 * cols) for o in outs]


def split_ffn(mats, n, yidx):
    rows = mats[0].shape[0] // (2 * n)
    cols = mats[0].shape[1] // 2
    ins = [m.reshape(n, 2, rows, 2 * cols) for m in mats]

    def kernel(yi, *refs):
        srcs, outs = refs[:2], refs[2:]
        for a in range(2):
            for h in range(2):
                for dx in range(2):
                    outs[dx * 2 + a][0, h] = srcs[h][0, yi[a], :, dx * cols : (dx + 1) * cols]

    return pl.pallas_call(
        kernel,
        grid_spec=pltpu.PrefetchScalarGridSpec(
            num_scalar_prefetch=1,
            grid=(n,),
            in_specs=[pl.BlockSpec((1, 2, rows, 2 * cols), lambda k, yi: (k, 0, 0, 0))] * 2,
            out_specs=[pl.BlockSpec((1, 2, rows, cols), lambda k, yi: (k, 0, 0, 0))] * 4,
        ),
        out_shape=[jax.ShapeDtypeStruct((n, 2, rows, cols), BF16)] * 4,
        cost_estimate=pl.CostEstimate(
            flops=0, transcendentals=0, bytes_accessed=2 * 8 * n * rows * cols * 2
        ),
        name="split_ffn",
    )(yidx, *ins)


def assemble_planes(planes, yidx):
    n = planes.shape[0]
    rows, cols = planes.shape[4:]

    def kernel(yi, src, *outs):
        for k in range(n):
            for a in range(2):
                for h in range(2):
                    outs[h][k, yi[a]] = src[k, 0, a, h]

    outs = pl.pallas_call(
        kernel,
        grid_spec=pltpu.PrefetchScalarGridSpec(
            num_scalar_prefetch=1,
            grid=(2,),
            in_specs=[pl.BlockSpec((n, 1, 2, 2, rows, cols), lambda d, yi: (0, d, 0, 0, 0, 0))],
            out_specs=[pl.BlockSpec((n, 2, rows, cols), lambda d, yi: (0, 0, 0, d))] * 2,
        ),
        compiler_params=pltpu.CompilerParams(vmem_limit_bytes=32 << 20),
        out_shape=[jax.ShapeDtypeStruct((n, 2, rows, 2 * cols), BF16)] * 2,
        cost_estimate=pl.CostEstimate(
            flops=0, transcendentals=0, bytes_accessed=2 * 8 * n * rows * cols * 2
        ),
        name="assemble_planes",
    )(yidx, planes)
    return [o.reshape(n * 2 * rows, 2 * cols) for o in outs]


def split_planes(mats, n, yidx):
    rows = mats[0].shape[0] // (2 * n)
    cols = mats[0].shape[1] // 2
    ins = [m.reshape(n, 2, rows, 2 * cols) for m in mats]

    def kernel(yi, *refs):
        for k in range(n):
            for a in range(2):
                for h in range(2):
                    refs[2][k, 0, a, h] = refs[h][k, yi[a]]

    return pl.pallas_call(
        kernel,
        grid_spec=pltpu.PrefetchScalarGridSpec(
            num_scalar_prefetch=1,
            grid=(2,),
            in_specs=[pl.BlockSpec((n, 2, rows, cols), lambda d, yi: (0, 0, 0, d))] * 2,
            out_specs=pl.BlockSpec((n, 1, 2, 2, rows, cols), lambda d, yi: (0, d, 0, 0, 0, 0)),
        ),
        compiler_params=pltpu.CompilerParams(vmem_limit_bytes=32 << 20),
        out_shape=jax.ShapeDtypeStruct((n, 2, 2, 2, rows, cols), BF16),
        cost_estimate=pl.CostEstimate(
            flops=0, transcendentals=0, bytes_accessed=2 * 8 * n * rows * cols * 2
        ),
        name="split_planes",
    )(yidx, *ins)


def bias_tiles(line, blocks):
    heads, _, length = line.shape
    spans = 2 * blocks - 1
    width = 2 * BLOCK

    def kernel(line_ref, out_ref):
        row = lax.broadcasted_iota(jnp.int32, (8, width), 0)
        for d in range(spans):
            start = (spans - 1 - d) * BLOCK
            window = line_ref[0, :, start : start + width]
            turned = jnp.concatenate([window[:, BLOCK:], window[:, :BLOCK]], axis=1)
            tile = jnp.broadcast_to(turned, (8, width))
            for bit in (1, 2, 4):
                tile = jnp.where((row & bit) != 0, pltpu.roll(tile, bit, 1), tile)
            size = 8
            while size < BLOCK:
                tile = jnp.concatenate([tile, pltpu.roll(tile, size, 1)], axis=0)
                size *= 2
            out_ref[0, d] = tile[:, :BLOCK]

    return pl.pallas_call(
        kernel,
        grid=(heads,),
        in_specs=[pl.BlockSpec((1, 1, length), lambda h: (h, 0, 0))],
        out_specs=pl.BlockSpec((1, spans, BLOCK, BLOCK), lambda h: (h, 0, 0, 0)),
        out_shape=jax.ShapeDtypeStruct((heads, spans, BLOCK, BLOCK), F32),
        cost_estimate=pl.CostEstimate(
            flops=heads * spans * BLOCK * BLOCK * 8,
            transcendentals=0,
            bytes_accessed=heads * spans * BLOCK * BLOCK * 4,
        ),
        name="bias_tiles",
    )(line)


def diagonal_sums(tile):
    width = 2 * BLOCK
    t = jnp.concatenate([tile, jnp.zeros_like(tile)], axis=1)
    size = BLOCK
    while size > 8:
        size //= 2
        t = t[:size] + pltpu.roll(t[size:], width - size, 1)
    row = lax.broadcasted_iota(jnp.int32, (8, width), 0)
    for bit in (1, 2, 4):
        t = jnp.where((row & bit) != 0, pltpu.roll(t, width - bit, 1), t)
    return jnp.sum(t, axis=0, keepdims=True)


def head_keys(keys, limit, a):
    lane = lax.broadcasted_iota(jnp.int32, keys.shape, 1)
    place = lax.broadcasted_iota(jnp.int32, keys.shape, 0)
    mine = (lane // (PAIR // 2)) == a
    flag = jnp.where(place < limit, 0.0, MASK_VALUE)
    other = jnp.where(lane == (1 - a) * (PAIR // 2), flag, 0.0)
    return bf(jnp.where(mine, wide(keys), other))


def head_queries(queries, scale, a, mark):
    lane = lax.broadcasted_iota(jnp.int32, queries.shape, 1)
    mine = (lane // (PAIR // 2)) == a
    other = jnp.where(lane == (1 - a) * (PAIR // 2), mark, 0.0)
    return bf(jnp.where(mine, wide(queries) * scale, other))


def only_head(values, a):
    lane = lax.broadcasted_iota(jnp.int32, values.shape, 1)
    return bf(jnp.where((lane // (PAIR // 2)) == a, wide(values), 0.0))


def score_blocks(key_a, query_a, bias_ref, a, qb, key_blocks, causal):
    out = []
    for kb in range(key_blocks):
        st = dot_nt(key_a[kb * BLOCK : (kb + 1) * BLOCK], query_a)
        if bias_ref is not None:
            st = st + bias_ref[a, kb - qb + key_blocks - 1]
        if causal:
            kpos = lax.broadcasted_iota(jnp.int32, st.shape, 0)
            qpos = lax.broadcasted_iota(jnp.int32, st.shape, 1)
            st = jnp.where(kpos <= qpos, st, MASK_VALUE)
        out.append(st)
    return out


def attention_forward(queries, memory, limit, bias, causal, fused):
    query_len = queries.shape[0]
    key_len = query_len if fused else memory.shape[0]
    pairs = queries.shape[1] // ((3 if fused else 1) * PAIR)
    key_blocks, query_blocks = key_len // BLOCK, query_len // BLOCK
    scale = (PAIR // 2) ** (-0.5)

    def kernel(limit_ref, q_ref, *refs):
        refs = list(refs)
        kv_ref = q_ref if fused else refs.pop(0)
        bias_ref = refs.pop(0) if bias is not None else None
        c_ref, lse_ref = refs
        k0 = PAIR if fused else 0
        keys = kv_ref[:, k0 : k0 + PAIR]
        values = kv_ref[:, k0 + PAIR : k0 + 2 * PAIR]
        key_a = [head_keys(keys, limit_ref[0], a) for a in range(2)]

        def visit(qb):
            rows = pl.ds(pl.multiple_of(qb * BLOCK, BLOCK), BLOCK)
            q = q_ref[rows, 0:PAIR]
            parts = []
            for a in range(2):
                st = score_blocks(
                    key_a[a], head_queries(q, scale, a, 1.0), bias_ref, a, qb, key_blocks, causal
                )
                top = functools.reduce(
                    jnp.maximum, [jnp.max(b, axis=0, keepdims=True) for b in st]
                )
                ex = [jnp.exp(b - top) for b in st]
                total = sum(jnp.sum(b, axis=0, keepdims=True) for b in ex)
                ct = sum(
                    dot_tn(values[kb * BLOCK : (kb + 1) * BLOCK], bf(ex[kb]))
                    for kb in range(key_blocks)
                )
                parts.append(ct[a * (PAIR // 2) : (a + 1) * (PAIR // 2)] * (1.0 / total))
                lse_ref[0, a : a + 1, rows] = top + jnp.log(total)
            c_ref[rows, :] = bf(jnp.transpose(jnp.concatenate(parts, axis=0)))

        if query_blocks == 1:
            visit(0)
        else:
            pl.loop(0, query_blocks)(visit)

    in_specs = [pl.BlockSpec((query_len, (3 if fused else 1) * PAIR), lambda j, n: (0, j))]
    args = [queries]
    if not fused:
        in_specs.append(pl.BlockSpec((key_len, 2 * PAIR), lambda j, n: (0, j)))
        args.append(memory)
    if bias is not None:
        in_specs.append(pl.BlockSpec((2,) + bias.shape[1:], lambda j, n: (j, 0, 0, 0)))
        args.append(bias)
    return pl.pallas_call(
        kernel,
        grid_spec=pltpu.PrefetchScalarGridSpec(
            num_scalar_prefetch=1,
            grid=(pairs,),
            in_specs=in_specs,
            out_specs=[
                pl.BlockSpec((query_len, PAIR), lambda j, n: (0, j)),
                pl.BlockSpec((1, 8, query_len), lambda j, n: (j, 0, 0)),
            ],
        ),
        out_shape=[
            jax.ShapeDtypeStruct((query_len, pairs * PAIR), BF16),
            jax.ShapeDtypeStruct((pairs, 8, query_len), F32),
        ],
        compiler_params=pltpu.CompilerParams(vmem_limit_bytes=40 << 20),
        cost_estimate=pl.CostEstimate(
            flops=pairs * 2 * query_len * key_len * PAIR * 4,
            transcendentals=pairs * 2 * query_len * key_len,
            bytes_accessed=pairs * PAIR * 2 * 2 * (query_len + key_len),
        ),
        name="attend_" + ("enc" if bias is not None else "dec" if fused else "cross"),
    )(limit, *args)


def attention_backward(queries, memory, limit, bias, causal, fused, context, lse, context_grad):
    query_len = queries.shape[0]
    key_len = query_len if fused else memory.shape[0]
    pairs = queries.shape[1] // ((3 if fused else 1) * PAIR)
    key_blocks, query_blocks = key_len // BLOCK, query_len // BLOCK
    spans = 2 * key_blocks - 1
    scale = (PAIR // 2) ** (-0.5)

    def kernel(limit_ref, q_ref, *refs):
        refs = list(refs)
        kv_ref = q_ref if fused else refs.pop(0)
        bias_ref = refs.pop(0) if bias is not None else None
        c_ref, lse_ref, dc_ref = refs[:3]
        refs = refs[3:]
        dq_ref = refs.pop(0)
        dkv_ref = dq_ref if fused else refs.pop(0)
        diag_ref = refs.pop(0) if bias is not None else None
        dk_acc, dv_acc = refs[:2]
        tile_acc = refs[2] if bias is not None else None
        k0 = PAIR if fused else 0
        keys = kv_ref[:, k0 : k0 + PAIR]
        values = kv_ref[:, k0 + PAIR : k0 + 2 * PAIR]
        key_a = [head_keys(keys, limit_ref[0], a) for a in range(2)]
        pure_key_a = [only_head(keys, a) for a in range(2)]
        value_a = [only_head(values, a) for a in range(2)]
        dk_acc[...] = jnp.zeros_like(dk_acc)
        dv_acc[...] = jnp.zeros_like(dv_acc)
        if bias is not None:
            tile_acc[...] = jnp.zeros_like(tile_acc)

        def visit(qb):
            rows = pl.ds(pl.multiple_of(qb * BLOCK, BLOCK), BLOCK)
            q = q_ref[rows, 0:PAIR]
            dc = dc_ref[rows, :]
            both = jnp.transpose(wide(dc) * wide(c_ref[rows, :]))
            dqt = jnp.zeros((PAIR, BLOCK), F32)
            for a in range(2):
                st = score_blocks(
                    key_a[a], head_queries(q, scale, a, 1.0), bias_ref, a, qb, key_blocks, causal
                )
                delta = jnp.sum(
                    both[a * (PAIR // 2) : (a + 1) * (PAIR // 2)], axis=0, keepdims=True
                )
                log_row = lse_ref[0, a : a + 1, rows]
                dc_a = only_head(dc, a)
                q_a = head_queries(q, scale, a, 0.0)
                for kb in range(key_blocks):
                    span = slice(kb * BLOCK, (kb + 1) * BLOCK)
                    p = jnp.exp(st[kb] - log_row)
                    dp = dot_nt(value_a[a][span], dc)
                    ds = p * (dp - delta)
                    dsb = bf(ds)
                    dv_acc[span, :] += dot_nn(bf(p), dc_a)
                    dk_acc[span, :] += dot_nn(dsb, q_a)
                    dqt = dqt + dot_tn(pure_key_a[a][span], dsb)
                    if bias is not None:
                        tile_acc[a, kb - qb + key_blocks - 1] += ds
            dq_ref[rows, 0:PAIR] = bf(jnp.transpose(dqt) * scale)

        if query_blocks == 1:
            visit(0)
        else:
            pl.loop(0, query_blocks)(visit)
        dkv_ref[:, k0 : k0 + PAIR] = bf(dk_acc[...])
        dkv_ref[:, k0 + PAIR : k0 + 2 * PAIR] = bf(dv_acc[...])
        if bias is not None:
            for a in range(2):
                for d in range(spans):
                    diag_ref[a, d : d + 1, :] = diagonal_sums(tile_acc[a, d])

    in_specs = [pl.BlockSpec((query_len, (3 if fused else 1) * PAIR), lambda j, n: (0, j))]
    args = [queries]
    if not fused:
        in_specs.append(pl.BlockSpec((key_len, 2 * PAIR), lambda j, n: (0, j)))
        args.append(memory)
    if bias is not None:
        in_specs.append(pl.BlockSpec((2,) + bias.shape[1:], lambda j, n: (j, 0, 0, 0)))
        args.append(bias)
    in_specs += [
        pl.BlockSpec((query_len, PAIR), lambda j, n: (0, j)),
        pl.BlockSpec((1, 8, query_len), lambda j, n: (j, 0, 0)),
        pl.BlockSpec((query_len, PAIR), lambda j, n: (0, j)),
    ]
    args += [context, lse, context_grad]
    out_specs = [pl.BlockSpec((query_len, (3 if fused else 1) * PAIR), lambda j, n: (0, j))]
    out_shape = [jax.ShapeDtypeStruct(queries.shape, BF16)]
    scratch = [pltpu.VMEM((key_len, PAIR), F32)] * 2
    if not fused:
        out_specs.append(pl.BlockSpec((key_len, 2 * PAIR), lambda j, n: (0, j)))
        out_shape.append(jax.ShapeDtypeStruct(memory.shape, BF16))
    if bias is not None:
        out_specs.append(pl.BlockSpec((2, 8, 2 * BLOCK), lambda j, n: (j, 0, 0)))
        out_shape.append(jax.ShapeDtypeStruct((2 * pairs, 8, 2 * BLOCK), F32))
        scratch.append(pltpu.VMEM((2, spans, BLOCK, BLOCK), F32))
    return pl.pallas_call(
        kernel,
        grid_spec=pltpu.PrefetchScalarGridSpec(
            num_scalar_prefetch=1,
            grid=(pairs,),
            in_specs=in_specs,
            out_specs=out_specs,
            scratch_shapes=scratch,
        ),
        out_shape=out_shape,
        compiler_params=pltpu.CompilerParams(vmem_limit_bytes=40 << 20),
        cost_estimate=pl.CostEstimate(
            flops=pairs * 2 * query_len * key_len * PAIR * 10,
            transcendentals=pairs * 2 * query_len * key_len,
            bytes_accessed=pairs * PAIR * 2 * 4 * (query_len + key_len),
        ),
        name="attend_back_" + ("enc" if bias is not None else "dec" if fused else "cross"),
    )(limit, *args)


def gelu(z):
    return z * (0.5 * (1.0 + lax.erf(z * ROOT_HALF)))


def gelu_slope(z):
    return 0.5 * (1.0 + lax.erf(z * ROOT_HALF)) + z * jnp.exp(-0.5 * z * z) * INV_ROOT_TAU


def norm_forward(values, gain, offset):
    center = values - jnp.mean(values, axis=-1, keepdims=True)
    inv = lax.rsqrt(jnp.mean(center * center, axis=-1, keepdims=True) + EPSILON)
    normed = center * inv
    return normed * gain + offset, normed, inv


def norm_backward(upstream, normed, inv, gain):
    scaled = upstream * gain
    inner = (
        scaled
        - jnp.mean(scaled, axis=-1, keepdims=True)
        - normed * jnp.mean(scaled * normed, axis=-1, keepdims=True)
    )
    return inv * inner, jnp.sum(upstream * normed, axis=0), jnp.sum(upstream, axis=0)


def update_matrices(sums, alternative, own, state, rate, inverse, packed):
    master = state[0]
    count, rows, cols = master.shape
    step = 2 if packed else 1
    arrays = list(sums) + ([alternative] if alternative is not None else [])

    def kernel(own_ref, inv_ref, *refs):
        if packed:
            groups = [refs[2 * i : 2 * i + 2] for i in range(len(arrays))]
            refs = refs[2 * len(arrays) :]
        else:
            groups = [refs[i : i + 1] for i in range(len(arrays))]
            refs = refs[len(arrays) :]
        state_refs, outs = refs[:3], refs[3:]
        inv = inv_ref[0]

        def total(part, i):
            vals = [wide(g[part][i]) for g in groups]
            if alternative is not None:
                vals = [jnp.where(own_ref[0] == 1, vals[-1], vals[0])] + vals[1:-1]
            return functools.reduce(jnp.add, vals)

        def advance(grad, i, span):
            mean_grad = grad * inv
            new_moment = MOMENTUM * state_refs[1][i, :, span] + mean_grad
            new_master = state_refs[0][i, :, span] - rate * (mean_grad + MOMENTUM * new_moment)
            outs[0][i, :, span] = mean_grad
            outs[1][i, :, span] = new_master
            outs[2][i, :, span] = new_moment
            outs[3][i, :, span] = (
                AVERAGING * state_refs[2][i, :, span] + (1.0 - AVERAGING) * new_master
            )
            outs[4][i, :, span] = bf(new_master)

        if packed:
            rest = total(1, 0)
            turned = pltpu.roll(rest, PAIR // 2, 1)
            for i in range(2):
                advance(total(0, i), i, slice(0, PAIR))
                advance((turned if i else rest)[:, : PAIR // 2], i, slice(PAIR, cols))
        else:
            advance(total(0, 0), 0, slice(0, cols))

    in_specs, args = [], []
    for a in arrays:
        in_specs.append(pl.BlockSpec((step, rows, a.shape[2]), lambda k, o: (k, 0, 0)))
        args.append(a)
        if packed:
            in_specs.append(pl.BlockSpec((1, rows, PAIR), lambda k, o: (count + k, 0, 0)))
            args.append(a)
    spec = pl.BlockSpec((step, rows, cols), lambda k, o: (k, 0, 0))
    return pl.pallas_call(
        kernel,
        grid_spec=pltpu.PrefetchScalarGridSpec(
            num_scalar_prefetch=1,
            grid=(count // step,),
            in_specs=[pl.BlockSpec(memory_space=pltpu.SMEM)] + in_specs + [spec] * 3,
            out_specs=[spec] * 5,
        ),
        out_shape=[jax.ShapeDtypeStruct(master.shape, F32)] * 4
        + [jax.ShapeDtypeStruct(master.shape, BF16)],
        cost_estimate=pl.CostEstimate(
            flops=12 * master.size, transcendentals=0, bytes_accessed=44 * master.size
        ),
        name="update_matrices",
    )(own, inverse, *args, *state)


def place_quarters(parts, index, cuts):
    rows, cols = parts[0].shape
    count = len(parts)

    def kernel(idx, *refs):
        outs = refs[count:]
        for k in range(count):

            @pl.when(pl.program_id(0) == k)
            def _():
                start = 0
                for out, cut in zip(outs, cuts):
                    out[0] = refs[k][start : start + cut]
                    start += cut

    return pl.pallas_call(
        kernel,
        grid_spec=pltpu.PrefetchScalarGridSpec(
            num_scalar_prefetch=1,
            grid=(count,),
            in_specs=[pl.BlockSpec((rows, cols), lambda g, idx: (0, 0))] * count,
            out_specs=[pl.BlockSpec((1, c, cols), lambda g, idx: (idx[g], 0, 0)) for c in cuts],
        ),
        out_shape=[jax.ShapeDtypeStruct((count, c, cols), parts[0].dtype) for c in cuts],
        cost_estimate=pl.CostEstimate(
            flops=0, transcendentals=0, bytes_accessed=4 * count * rows * cols
        ),
        name="place_quarters",
    )(index, *parts)


def update(master, moment, average, gradient, rate, frame_total):
    mean_grad = gradient / frame_total
    new_moment = MOMENTUM * moment + mean_grad
    new_master = master - rate * (mean_grad + MOMENTUM * new_moment)
    new_average = AVERAGING * average + (1.0 - AVERAGING) * new_master
    return mean_grad, new_master, new_moment, new_average


def both_cores(low):
    return wide(low) + wide(swap_core(low))


def order_cols(v0, v1):
    return jnp.concatenate(
        [v0[..., :PAIR], v1[..., :PAIR], v0[..., PAIR:], v1[..., PAIR:]], axis=-1
    )


def group_cols(v):
    half = PAIR // 2
    return (
        jnp.concatenate([v[..., :PAIR], v[..., 2 * PAIR : 2 * PAIR + half]], axis=-1),
        jnp.concatenate([v[..., PAIR : 2 * PAIR], v[..., 2 * PAIR + half :]], axis=-1),
    )


CROSS_PLANS = [
    [(0, j) for j in range(3)],
    [(m, j) for j in range(3) for m in (1, 2)],
    [(3, j) for j in range(3)],
]
QKV_PLAN = [(m, j) for j in range(3) for m in range(3)]
ENC_PLANS = [QKV_PLAN, [(3, j) for j in range(3)]]
DEC_PLANS = [
    QKV_PLAN,
    [(3, j) for j in range(3)],
    [(4, j) for j in range(3)],
    [(m, j) for j in range(3) for m in (5, 6)],
    [(7, j) for j in range(3)],
]


def local(
    frames,
    cotangent,
    lengths,
    attn_master,
    attn_moment,
    attn_average,
    ffn_master,
    ffn_moment,
    ffn_average,
    norm_vecs,
    norm_moment,
    norm_average,
    col_bias,
    col_moment,
    col_average,
    rel_table,
    rel_moment,
    rel_average,
    dec_frames,
    dec_cotangent,
    text_lengths,
    dec_attn_master,
    dec_attn_moment,
    dec_attn_average,
    dec_ffn_master,
    dec_ffn_moment,
    dec_ffn_average,
    dec_norm_vecs,
    dec_norm_moment,
    dec_norm_average,
    dec_col_bias,
    dec_col_moment,
    dec_col_average,
):
    n_dp = lax.axis_size("dp")
    z, s, m = lax.axis_index("dp"), lax.axis_index("seq"), lax.axis_index("mp")
    y = m // 2
    utt_count, half_len, width = frames.shape
    text_half = dec_frames.shape[1]
    full_len, text_full = 2 * half_len, 2 * text_half
    own = s == y
    yidx = jnp.stack([y, 1 - y, own.astype(jnp.int32)]).astype(jnp.int32)
    root_frames = float(utt_count * full_len * n_dp) ** 0.5

    mine = jnp.concatenate(
        [
            lax.dynamic_index_in_dim(parts, m, 0, keepdims=False)
            for parts in (frames, cotangent, dec_frames, dec_cotangent)
        ]
    )
    other = swap_core(mine)
    dffn_shard = bf(dec_ffn_master)
    dffn_parts = gather_plane(dffn_shard)
    attn_z = gather_dp(pack_attn(bf(attn_master)))
    packed = jnp.concatenate([col_bias, dec_col_bias, rel_table.T.reshape(-1)])
    groups = [jnp.where(own, packed, spread(packed, 0, 0)), spread(packed, 1, 0)]
    ffn_z = gather_dp(after(bf(ffn_master), attn_z))
    mine, other, dffn_parts, attn_z, groups = stage(mine, other, dffn_parts, attn_z, groups)
    attn_pieces = gather_plane(attn_z)

    bucket_count, group_heads = rel_table.shape
    group_width = attn_master.shape[2]
    unit_count = ffn_master.shape[2]
    enc_cols, dec_cols = col_bias.shape[0], dec_col_bias.shape[0]

    def cols_at(start):
        return order_cols(*[g[start : start + group_width] for g in groups])

    def units_at(start):
        return jnp.concatenate([g[start : start + unit_count] for g in groups])

    def qkv_bias(q, v):
        blank = jnp.zeros((PAIR,), F32)
        cut = [slice(j * PAIR, (j + 1) * PAIR) for j in range(3)]
        return jnp.concatenate([part for c in cut for part in (q[c], blank, v[c])])

    bias_qkv = qkv_bias(cols_at(0), cols_at(group_width))
    bias_one = units_at(2 * group_width)
    bias_dqkv = qkv_bias(cols_at(enc_cols), cols_at(enc_cols + group_width))
    bias_cq = cols_at(enc_cols + 2 * group_width)
    cv = cols_at(enc_cols + 3 * group_width)
    blank = jnp.zeros((PAIR,), F32)
    bias_ckv = jnp.concatenate(
        [part for j in range(3) for part in (blank, cv[j * PAIR : (j + 1) * PAIR])]
    )
    bias_done = units_at(enc_cols + 4 * group_width)
    tables = [
        g[enc_cols + dec_cols :].reshape(group_heads, bucket_count) for g in groups
    ]
    heads = jnp.stack(
        [tables[0][0], tables[0][1], tables[1][0], tables[1][1], tables[0][2], tables[1][2]]
    )
    max_dist = bucket_count // 2
    blocks = full_len // BLOCK
    lead = blocks * BLOCK - max_dist + 1
    tail = blocks * BLOCK - max_dist - 1
    line = jnp.pad(heads[:, ::-1], ((0, 0), (lead, tail)), mode="edge")
    bias = bias_tiles(line[:, None, :], blocks)

    def all_rows(start, count):
        ours, theirs = mine[start : start + count], other[start : start + count]
        return jnp.concatenate([jnp.where(s == 0, ours, theirs), jnp.where(s == 0, theirs, ours)])

    inputs = all_rows(0, half_len)
    upstream_in = all_rows(half_len, half_len)
    text_in = all_rows(2 * half_len, text_half)
    text_upstream = all_rows(2 * half_len + text_half, text_half)
    limit = lax.dynamic_slice_in_dim(lengths, m, 1)
    text_limit = lax.dynamic_slice_in_dim(text_lengths, m, 1)
    own_flag = own.astype(jnp.int32).reshape(1)

    def my_half(rows):
        count = rows.shape[0] // 2
        return lax.dynamic_slice_in_dim(rows, s * count, count, 0)

    def to_owners(mine):
        return [mine] + [swap_mp(mine, bits) for bits in range(1, 4)]

    owners = m ^ jnp.arange(4, dtype=jnp.int32)

    attn_pieces, ffn_z, bias, bias_qkv, inputs, dattn_shard, dffn_plane = stage(
        attn_pieces,
        ffn_z,
        bias,
        bias_qkv,
        inputs,
        pack_attn(bf(dec_attn_master)),
        jnp.stack([jnp.where(own, dffn_parts[0], dffn_parts[1]), *dffn_parts[2:]]),
    )
    ffn_pieces = gather_plane(ffn_z)
    dattn_z = gather_dp(dattn_shard)
    dffn_planes = gather_dp(after(dffn_plane, dattn_z).reshape((2, 2) + dffn_shard.shape))
    w_qkv, w_o = assemble_attn(attn_pieces, ENC_PLANS, 4, yidx)
    qkv = bf(dot_nn(inputs, w_qkv) + bias_qkv)
    context, lse = attention_forward(qkv, None, limit, bias, False, True)
    part = bf(dot_nt(context, w_o))
    ffn_pieces, dattn_z, part = stage(ffn_pieces, dattn_z, part)
    dattn_pieces = gather_plane(dattn_z)
    attn_sum = both_cores(part)
    hidden_one, normed_one, inv_one = norm_forward(
        wide(inputs) + attn_sum + norm_vecs[4], norm_vecs[0], norm_vecs[1]
    )
    hidden_low = bf(hidden_one)
    w_one, w_two = assemble_ffn(ffn_pieces, yidx)
    gate_in = dot_nn(hidden_low, w_one) + bias_one
    activated = bf(gelu(gate_in))
    part = bf(dot_nt(activated, w_two))
    dattn_pieces, part, lengths_sum = stage(
        dattn_pieces, part, jnp.broadcast_to(wide(jnp.sum(lengths)), (8, 128))
    )
    ffn_sum = both_cores(part)
    result, normed_two, inv_two = norm_forward(
        hidden_one + ffn_sum + norm_vecs[5], norm_vecs[2], norm_vecs[3]
    )
    enc_low = bf(result)
    out_enc = lax.all_gather(after(my_half(enc_low), dffn_planes), "mp", axis=0, tiled=False)

    frame_total = sum_dp(lengths_sum)[0, 0]
    inverse = (1.0 / frame_total).reshape(1)
    d_qkv, d_o, c_q, c_kv, c_o = assemble_attn(dattn_pieces, DEC_PLANS, 8, yidx)
    dw_one, dw_two = assemble_planes(dffn_planes, yidx)
    dqkv = bf(dot_nn(text_in, d_qkv) + bias_dqkv)
    self_context, self_lse = attention_forward(dqkv, None, text_limit, None, True, True)
    self_sum = both_cores(bf(dot_nt(self_context, d_o)))
    dec_one, normed_d1, inv_d1 = norm_forward(
        wide(text_in) + self_sum + dec_norm_vecs[6], dec_norm_vecs[0], dec_norm_vecs[1]
    )
    dec_one_low = bf(dec_one)
    cross_q = bf(dot_nn(dec_one_low, c_q) + bias_cq)
    cross_kv = bf(dot_nn(enc_low, c_kv) + bias_ckv)
    cross_context, cross_lse = attention_forward(cross_q, cross_kv, limit, None, False, False)
    cross_sum = both_cores(bf(dot_nt(cross_context, c_o)))
    dec_two, normed_d2, inv_d2 = norm_forward(
        dec_one + cross_sum + dec_norm_vecs[7], dec_norm_vecs[2], dec_norm_vecs[3]
    )
    dec_two_low = bf(dec_two)
    dec_gate = dot_nn(dec_two_low, dw_one) + bias_done
    dec_act = bf(gelu(dec_gate))
    dec_ffn_sum = both_cores(bf(dot_nt(dec_act, dw_two)))
    dec_result, normed_d3, inv_d3 = norm_forward(
        dec_two + dec_ffn_sum + dec_norm_vecs[8], dec_norm_vecs[4], dec_norm_vecs[5]
    )

    text_places = lax.broadcasted_iota(jnp.int32, (text_full, 1), 0)
    dec_up = jnp.where(text_places < text_limit[0], wide(text_upstream), 0.0)
    grad_d3, gain_d3, shift_d3 = norm_backward(dec_up, normed_d3, inv_d3, dec_norm_vecs[4])
    dec_ffn_back = bf(grad_d3)
    dec_gate_grad = bf(dot_nn(dec_ffn_back, dw_two) * gelu_slope(dec_gate))
    part = bf(dot_nt(dec_gate_grad, dw_one))
    dec_ffn_grads = [
        bf(dot_tn(dec_two_low, dec_gate_grad)),
        bf(dot_tn(dec_ffn_back, dec_act)),
    ]
    dec_ffn_planes, part, sent, inverse = stage(
        split_planes(dec_ffn_grads, n_dp, yidx), part, my_half(bf(dec_result)), inverse
    )
    dec_ffn_plane = scatter_dp(dec_ffn_planes)
    out_dec = to_owners(sent)
    grad_h2 = grad_d3 + both_cores(part)

    grad_d2, gain_d2, shift_d2 = norm_backward(grad_h2, normed_d2, inv_d2, dec_norm_vecs[2])
    cross_back = bf(grad_d2)
    cross_qg, cross_kvg = attention_backward(
        cross_q,
        cross_kv,
        limit,
        None,
        False,
        False,
        cross_context,
        cross_lse,
        bf(dot_nn(cross_back, c_o)),
    )
    cross_grads = [
        bf(dot_tn(dec_one_low, cross_qg)),
        bf(dot_tn(enc_low, cross_kvg)),
        bf(dot_tn(cross_back, cross_context)),
    ]
    query_part, memory_part, cross_parts, out_dec = stage(
        bf(dot_nt(cross_qg, c_q)),
        bf(dot_nt(cross_kvg, c_kv)),
        split_attn(cross_grads, CROSS_PLANS, 4, n_dp, yidx),
        out_dec,
    )
    (out_dec,) = place_quarters(out_dec, owners, [text_half])
    cross_plane_back = scatter_plane(cross_parts)
    memory_back = both_cores(memory_part)
    grad_h1 = grad_d2 + both_cores(query_part)
    grad_d1, gain_d1, shift_d1 = norm_backward(grad_h1, normed_d1, inv_d1, dec_norm_vecs[0])
    self_back = bf(grad_d1)
    (self_g,) = attention_backward(
        dqkv,
        None,
        text_limit,
        None,
        True,
        True,
        self_context,
        self_lse,
        bf(dot_nn(self_back, d_o)),
    )
    text_part = bf(dot_nt(self_g, d_qkv))
    self_grads = [bf(dot_tn(text_in, self_g)), bf(dot_tn(self_back, self_context))]
    self_parts = split_attn(self_grads, ENC_PLANS, 4, n_dp, yidx)

    places = lax.broadcasted_iota(jnp.int32, (full_len, 1), 0)
    upstream = jnp.where(places < limit[0], wide(upstream_in), 0.0) + memory_back
    grad_two, gain_two, shift_two = norm_backward(upstream, normed_two, inv_two, norm_vecs[2])
    ffn_back = bf(grad_two)
    gate_grad = bf(dot_nn(ffn_back, w_two) * gelu_slope(gate_in))
    ffn_grads = [bf(dot_tn(hidden_low, gate_grad)), bf(dot_tn(ffn_back, activated))]
    part, text_part, self_parts, cross_parts, cross_plane_back, ffn_parts = stage(
        bf(dot_nt(gate_grad, w_one)),
        text_part,
        self_parts,
        cross_parts,
        cross_plane_back,
        split_ffn(ffn_grads, n_dp, yidx),
    )
    cross_total = scatter_dp(sum_plane(cross_parts, cross_plane_back, own))
    ffn_plane_back = scatter_plane(ffn_parts)
    hidden_grad = grad_two + both_cores(part)
    grad_one, gain_one, shift_one = norm_backward(hidden_grad, normed_one, inv_one, norm_vecs[0])
    attn_back = bf(grad_one)
    enc_g, diag = attention_backward(
        qkv, None, limit, bias, False, True, context, lse, bf(dot_nn(attn_back, w_o))
    )
    self_parts, ffn_parts, ffn_plane_back, part, enc_g, diag, text_part, dec_ffn_plane = stage(
        self_parts,
        ffn_parts,
        ffn_plane_back,
        bf(dot_nt(enc_g, w_qkv)),
        enc_g,
        diag,
        text_part,
        dec_ffn_plane,
    )
    ffn_total = scatter_dp(sum_plane(ffn_parts, ffn_plane_back, own))
    self_plane_back = scatter_plane(self_parts)
    plane_parts = [dec_ffn_plane[dx, a] for dx, a in ROUTES]
    dec_ffn_sums = scatter_plane(plane_parts)
    input_grad = grad_one + both_cores(part)
    attn_grads = [bf(dot_tn(inputs, enc_g)), bf(dot_tn(attn_back, context))]
    attn_parts = split_attn(attn_grads, ENC_PLANS, 4, n_dp, yidx)
    def col_sum(a):
        return jnp.sum(a, axis=0, dtype=F32)

    def pick(v, stride, at):
        return jnp.concatenate(
            [v[(j * stride + at) * PAIR : (j * stride + at + 1) * PAIR] for j in range(3)]
        )

    enc_sum, dec_sum, kv_sum = col_sum(enc_g), col_sum(self_g), col_sum(cross_kvg)
    col_parts = [
        group_cols(pick(enc_sum, 3, 0)),
        group_cols(pick(enc_sum, 3, 2)),
        jnp.split(col_sum(gate_grad), 2),
        group_cols(pick(dec_sum, 3, 0)),
        group_cols(pick(dec_sum, 3, 2)),
        group_cols(col_sum(cross_qg)),
        group_cols(pick(kv_sum, 2, 1)),
        jnp.split(col_sum(dec_gate_grad), 2),
    ]
    turned = jnp.concatenate([diag[:, :, BLOCK:], diag[:, :, :BLOCK]], axis=-1)
    span_count = 2 * blocks - 1
    line_grad = sum(
        jnp.pad(
            turned[:, d],
            ((0, 0), ((span_count - 1 - d) * BLOCK, d * BLOCK)),
        )
        for d in range(span_count)
    )
    first_bucket = jnp.sum(line_grad[:, lead + bucket_count :], axis=1, keepdims=True)
    last_bucket = jnp.sum(line_grad[:, :lead], axis=1, keepdims=True)
    head_grad = line_grad[:, lead : lead + bucket_count][:, ::-1]
    head_grad = jnp.concatenate(
        [
            head_grad[:, :1] + first_bucket,
            head_grad[:, 1:-1],
            head_grad[:, -1:] + last_bucket,
        ],
        axis=1,
    )
    table_parts = (head_grad[jnp.array([0, 1, 4])], head_grad[jnp.array([2, 3, 5])])
    norm_local = jnp.stack(
        [gain_one, shift_one, gain_two, shift_two, jnp.sum(grad_one, 0), jnp.sum(grad_two, 0)]
    )
    dec_norm_local = jnp.stack(
        [
            gain_d1,
            shift_d1,
            gain_d2,
            shift_d2,
            gain_d3,
            shift_d3,
            jnp.sum(grad_d1, 0),
            jnp.sum(grad_d2, 0),
            jnp.sum(grad_d3, 0),
        ]
    )
    shared = jnp.concatenate([norm_local.reshape(-1), dec_norm_local.reshape(-1)])
    vectors = [
        jnp.concatenate([p[dx] for p in col_parts] + [table_parts[dx].reshape(-1), shared])
        for dx in range(2)
    ]
    self_parts, self_plane_back, attn_parts, input_grad, vectors, text_part, dec_ffn_sums = stage(
        self_parts, self_plane_back, attn_parts, input_grad, vectors, text_part, dec_ffn_sums
    )
    self_total = scatter_dp(sum_plane(self_parts, self_plane_back, own))
    attn_plane_back = scatter_plane(attn_parts)
    text_grad = grad_d1 + both_cores(text_part)
    small = vectors[0] + swap_mp(vectors[1], 1)
    small = jnp.where(own, small, unspread(small, 0, 0))
    small = small + swap_core(small)
    attn_parts, attn_plane_back, small, input_grad, text_grad = stage(
        attn_parts, attn_plane_back, small, input_grad, text_grad
    )
    attn_total = scatter_dp(sum_plane(attn_parts, attn_plane_back, own))
    held_back = to_owners(jnp.concatenate([my_half(bf(input_grad)), my_half(bf(text_grad))]))
    out_input_grad, out_text_grad = place_quarters(held_back, owners, [half_len, text_half])
    dec_attn_total = jnp.concatenate(
        [self_total[:4], cross_total[:4], self_total[4:], cross_total[4:]]
    )
    small = sum_dp(small)
    cut = [enc_cols, dec_cols, group_heads * bucket_count, norm_vecs.size, dec_norm_vecs.size]
    ends = [sum(cut[: i + 1]) for i in range(len(cut))]
    col_total, dec_col_total, table_total, norm_total, dec_norm_total, _ = jnp.split(small, ends)
    table_total = table_total.reshape(group_heads, bucket_count).T
    norm_total = norm_total.reshape(norm_vecs.shape)
    dec_norm_total = dec_norm_total.reshape(dec_norm_vecs.shape)

    matrix_rate = MATRIX_RATE * root_frames
    vector_rate = VECTOR_RATE * root_frames
    attn_new = update_matrices(
        [attn_total],
        None,
        own_flag,
        (attn_master, attn_moment, attn_average),
        matrix_rate,
        inverse,
        True,
    )
    ffn_new = update_matrices(
        [ffn_total],
        None,
        own_flag,
        (ffn_master, ffn_moment, ffn_average),
        matrix_rate,
        inverse,
        False,
    )
    dattn_new = update_matrices(
        [dec_attn_total],
        None,
        own_flag,
        (dec_attn_master, dec_attn_moment, dec_attn_average),
        matrix_rate,
        inverse,
        True,
    )
    dffn_new = update_matrices(
        dec_ffn_sums,
        plane_parts[0],
        own_flag,
        (dec_ffn_master, dec_ffn_moment, dec_ffn_average),
        matrix_rate,
        inverse,
        False,
    )
    norm_new = update(norm_vecs, norm_moment, norm_average, norm_total, vector_rate, frame_total)
    col_new = update(col_bias, col_moment, col_average, col_total, vector_rate, frame_total)
    rel_new = update(rel_table, rel_moment, rel_average, table_total, vector_rate, frame_total)
    dnorm_new = update(
        dec_norm_vecs, dec_norm_moment, dec_norm_average, dec_norm_total, vector_rate, frame_total
    )
    dcol_new = update(
        dec_col_bias, dec_col_moment, dec_col_average, dec_col_total, vector_rate, frame_total
    )
    return (
        out_enc,
        out_input_grad,
        attn_new[0],
        ffn_new[0],
        *attn_new[1:],
        *ffn_new[1:],
        *norm_new[1:],
        *col_new[1:],
        *rel_new[1:],
        out_dec,
        out_text_grad,
        dattn_new[0],
        dffn_new[0],
        *dattn_new[1:],
        *dffn_new[1:],
        *dnorm_new[1:],
        *dcol_new[1:],
    )


def solution(mesh):
    rows = P("dp", "seq", None)
    matrix = P(None, ("dp", "seq"), "mp")
    table = P(None, "mp")
    enc_params = [matrix] * 6 + [P()] * 3 + [P("mp")] * 3 + [table] * 3
    dec_params = [matrix] * 6 + [P()] * 3 + [P("mp")] * 3
    in_specs = (rows, rows, P("dp"), *enc_params, rows, rows, P("dp"), *dec_params)
    out_specs = (
        [rows, rows]
        + [matrix] * 10
        + [P()] * 3
        + [P("mp")] * 3
        + [table] * 3
        + [rows, rows]
        + [matrix] * 10
        + [P()] * 3
        + [P("mp")] * 3
    )
    return jax.shard_map(
        local, mesh=mesh, in_specs=in_specs, out_specs=tuple(out_specs), check_vma=False
    )
```

```python
import functools

import jax
import jax.numpy as jnp
from jax import lax
from jax.experimental import pallas as pl
from jax.experimental.pallas import tpu as pltpu
from jax.sharding import PartitionSpec as P

EPSILON = 1e-05
MOMENTUM = 0.9
AVERAGING = 0.75
MATRIX_RATE = 0.02
VECTOR_RATE = 0.2
MASK_VALUE = -1e30
ROOT_HALF = 0.7071067811865476
INV_ROOT_TAU = 0.3989422804014327
BLOCK = 256
PAIR = 128
BF16 = jnp.bfloat16
F32 = jnp.float32
ON_CHIP = pl.BlockSpec(memory_space=pltpu.VMEM)
SCALARS = pl.BlockSpec(memory_space=pltpu.SMEM)


def bf(a):
    return a.astype(BF16)


def wide(a):
    return a.astype(F32)


def dot_nn(left, right):
    return jnp.dot(left, right, preferred_element_type=F32)


def dot_nt(left, right):
    return lax.dot_general(left, right, (((1,), (1,)), ((), ())), preferred_element_type=F32)


def dot_tn(left, right):
    return lax.dot_general(left, right, (((0,), (0,)), ((), ())), preferred_element_type=F32)


def swap_core(v):
    return lax.ppermute(v, "seq", [(0, 1), (1, 0)])


def swap_mp(v, bits):
    return lax.ppermute(v, "mp", [(m, m ^ bits) for m in range(4)])


def spread_perm(dx, flip):
    pairs = [
        (s * 4 + y * 2 + x, y * 4 + (s ^ flip) * 2 + (x ^ dx))
        for s in range(2)
        for y in range(2)
        for x in range(2)
    ]
    return [(a, b) for a, b in pairs if a != b]


ROUTES = [(dx, flip) for dx in range(2) for flip in range(2)]


def spread(v, dx, flip):
    return lax.ppermute(v, ("seq", "mp"), spread_perm(dx, flip))


def unspread(v, dx, flip):
    return lax.ppermute(v, ("seq", "mp"), [(d, s) for s, d in spread_perm(dx, flip)])


def sum_dp(v):
    n = lax.axis_size("dp")
    if n != 4:
        return lax.psum(v, "dp")
    for bits in (1, 2):
        v = v + lax.ppermute(v, "dp", [(i, i ^ bits) for i in range(n)])
    return v


def stage(*values):
    return lax.optimization_barrier(values)


def after(values, *others):
    return lax.optimization_barrier((values, others))[0]


def gather_dp(shard):
    return lax.all_gather(shard, "dp", axis=0, tiled=False)


def scatter_dp(whole):
    return lax.psum_scatter(whole, "dp", scatter_dimension=0, tiled=False)


def gather_plane(v):
    return [v] + [spread(v, dx, flip) for dx, flip in ROUTES]


def scatter_plane(pieces):
    return [unspread(p, dx, flip) for p, (dx, flip) in zip(pieces, ROUTES)]


def sum_plane(pieces, back, own):
    first = jnp.where(own, wide(pieces[0]), wide(back[0]))
    return bf(first + sum(wide(b) for b in back[1:]))


def pack_attn(shard):
    main, rest = shard[:, :, :PAIR], shard[:, :, PAIR:]
    return jnp.concatenate([main, jnp.concatenate([rest[0::2], rest[1::2]], axis=-1)], axis=0)


def half_lanes(shape):
    return lax.broadcasted_iota(jnp.int32, shape, len(shape) - 1) < PAIR // 2


def half_roll(v):
    return bf(pltpu.roll(wide(v), PAIR // 2, 1))


def assemble_attn(pieces, plans, count, yidx):
    n, tiles, rows, _ = pieces[0].shape

    def kernel(yi, *refs):
        ins, outs = refs[:5], refs[5:]
        low = half_lanes((rows, PAIR))
        for k in range(n):
            for a in range(2):
                side = yi[a]

                def tile(t, dx):
                    val = ins[1 + dx * 2 + a][k, t]
                    return jnp.where(yi[2] == 1, ins[0][k, t], val) if dx + a == 0 else val

                for out, plan in zip(outs, plans):
                    for place, (mat, j) in enumerate(plan):
                        if j < 2:
                            val = tile(mat, j)
                        else:
                            t0, t1 = tile(count + mat // 2, 0), tile(count + mat // 2, 1)
                            if mat % 2 == 0:
                                val = jnp.where(low, t0, half_roll(t1))
                            else:
                                val = jnp.where(low, half_roll(t0), t1)
                        out[k, side, :, place * PAIR : (place + 1) * PAIR] = val

    outs = pl.pallas_call(
        kernel,
        in_specs=[SCALARS] + [ON_CHIP] * 5,
        out_specs=[ON_CHIP] * len(plans),
        out_shape=[jax.ShapeDtypeStruct((n, 2, rows, PAIR * len(p)), BF16) for p in plans],
        cost_estimate=pl.CostEstimate(
            flops=0, transcendentals=0, bytes_accessed=9 * n * tiles * rows * PAIR * 2
        ),
        name="assemble_attn",
    )(yidx, *pieces)
    return [o.reshape(n * 2 * rows, -1) for o in outs]


def split_attn(mats, plans, count, n, yidx):
    tiles = count + count // 2
    rows = mats[0].shape[0] // (2 * n)
    ins = [m.reshape(n, 2, rows, -1) for m in mats]
    where = {}
    for i, plan in enumerate(plans):
        for place, key in enumerate(plan):
            where[key] = (i, place)

    def kernel(yi, *refs):
        srcs, outs = refs[: len(mats)], refs[len(mats) :]
        low = half_lanes((rows, PAIR))
        for k in range(n):
            for a in range(2):
                side = yi[a]

                def get(mat, j):
                    i, place = where[(mat, j)]
                    return srcs[i][k, side, :, place * PAIR : (place + 1) * PAIR]

                for dx in range(2):
                    for t in range(tiles):
                        if t < count:
                            val = get(t, dx)
                        else:
                            p = t - count
                            t0, t1 = get(2 * p, 2), get(2 * p + 1, 2)
                            if dx == 0:
                                val = jnp.where(low, t0, half_roll(t1))
                            else:
                                val = jnp.where(low, half_roll(t0), t1)
                        outs[dx * 2 + a][k, t] = val

    return pl.pallas_call(
        kernel,
        in_specs=[SCALARS] + [ON_CHIP] * len(ins),
        out_specs=[ON_CHIP] * 4,
        out_shape=[jax.ShapeDtypeStruct((n, tiles, rows, PAIR), BF16)] * 4,
        cost_estimate=pl.CostEstimate(
            flops=0, transcendentals=0, bytes_accessed=8 * n * tiles * rows * PAIR * 2
        ),
        name="split_attn",
    )(yidx, *ins)


def assemble_ffn(pieces, yidx):
    n, _, rows, cols = pieces[0].shape

    def kernel(yi, *refs):
        ins, outs = refs[:5], refs[5:]
        for k in range(n):
            for a in range(2):
                for h in range(2):
                    for dx in range(2):
                        val = ins[1 + dx * 2 + a][k, h]
                        val = jnp.where(yi[2] == 1, ins[0][k, h], val) if dx + a == 0 else val
                        outs[h][k, yi[a], :, dx * cols : (dx + 1) * cols] = val

    outs = pl.pallas_call(
        kernel,
        in_specs=[SCALARS] + [ON_CHIP] * 5,
        out_specs=[ON_CHIP] * 2,
        out_shape=[jax.ShapeDtypeStruct((n, 2, rows, 2 * cols), BF16)] * 2,
        cost_estimate=pl.CostEstimate(
            flops=0, transcendentals=0, bytes_accessed=2 * 9 * n * rows * cols * 2
        ),
        name="assemble_ffn",
    )(yidx, *pieces)
    return [o.reshape(n * 2 * rows, 2 * cols) for o in outs]


def split_ffn(mats, n, yidx):
    rows = mats[0].shape[0] // (2 * n)
    cols = mats[0].shape[1] // 2
    ins = [m.reshape(n, 2, rows, 2 * cols) for m in mats]

    def kernel(yi, *refs):
        srcs, outs = refs[:2], refs[2:]
        for k in range(n):
            for a in range(2):
                for h in range(2):
                    for dx in range(2):
                        outs[dx * 2 + a][k, h] = srcs[h][
                            k, yi[a], :, dx * cols : (dx + 1) * cols
                        ]

    return pl.pallas_call(
        kernel,
        in_specs=[SCALARS] + [ON_CHIP] * 2,
        out_specs=[ON_CHIP] * 4,
        out_shape=[jax.ShapeDtypeStruct((n, 2, rows, cols), BF16)] * 4,
        cost_estimate=pl.CostEstimate(
            flops=0, transcendentals=0, bytes_accessed=2 * 8 * n * rows * cols * 2
        ),
        name="split_ffn",
    )(yidx, *ins)


def assemble_planes(planes, yidx):
    n = planes.shape[0]
    rows, cols = planes.shape[4:]

    def kernel(yi, src, *outs):
        for k in range(n):
            for a in range(2):
                for h in range(2):
                    outs[h][k, yi[a]] = src[k, 0, a, h]

    outs = pl.pallas_call(
        kernel,
        grid_spec=pltpu.PrefetchScalarGridSpec(
            num_scalar_prefetch=1,
            grid=(2,),
            in_specs=[pl.BlockSpec((n, 1, 2, 2, rows, cols), lambda d, yi: (0, d, 0, 0, 0, 0))],
            out_specs=[pl.BlockSpec((n, 2, rows, cols), lambda d, yi: (0, 0, 0, d))] * 2,
        ),
        compiler_params=pltpu.CompilerParams(vmem_limit_bytes=32 << 20),
        out_shape=[jax.ShapeDtypeStruct((n, 2, rows, 2 * cols), BF16)] * 2,
        cost_estimate=pl.CostEstimate(
            flops=0, transcendentals=0, bytes_accessed=2 * 8 * n * rows * cols * 2
        ),
        name="assemble_planes",
    )(yidx, planes)
    return [o.reshape(n * 2 * rows, 2 * cols) for o in outs]


def split_planes(mats, n, yidx):
    rows = mats[0].shape[0] // (2 * n)
    cols = mats[0].shape[1] // 2
    ins = [m.reshape(n, 2, rows, 2 * cols) for m in mats]

    def kernel(yi, *refs):
        for k in range(n):
            for a in range(2):
                for h in range(2):
                    refs[2][k, 0, a, h] = refs[h][k, yi[a]]

    return pl.pallas_call(
        kernel,
        grid_spec=pltpu.PrefetchScalarGridSpec(
            num_scalar_prefetch=1,
            grid=(2,),
            in_specs=[pl.BlockSpec((n, 2, rows, cols), lambda d, yi: (0, 0, 0, d))] * 2,
            out_specs=pl.BlockSpec((n, 1, 2, 2, rows, cols), lambda d, yi: (0, d, 0, 0, 0, 0)),
        ),
        compiler_params=pltpu.CompilerParams(vmem_limit_bytes=32 << 20),
        out_shape=jax.ShapeDtypeStruct((n, 2, 2, 2, rows, cols), BF16),
        cost_estimate=pl.CostEstimate(
            flops=0, transcendentals=0, bytes_accessed=2 * 8 * n * rows * cols * 2
        ),
        name="split_planes",
    )(yidx, *ins)


def bias_tiles(line, blocks):
    heads, _, length = line.shape
    spans = 2 * blocks - 1
    width = 2 * BLOCK

    def kernel(line_ref, out_ref):
        row = lax.broadcasted_iota(jnp.int32, (8, width), 0)
        for d in range(spans):
            start = (spans - 1 - d) * BLOCK
            window = line_ref[0, :, start : start + width]
            turned = jnp.concatenate([window[:, BLOCK:], window[:, :BLOCK]], axis=1)
            tile = jnp.broadcast_to(turned, (8, width))
            for bit in (1, 2, 4):
                tile = jnp.where((row & bit) != 0, pltpu.roll(tile, bit, 1), tile)
            size = 8
            while size < BLOCK:
                tile = jnp.concatenate([tile, pltpu.roll(tile, size, 1)], axis=0)
                size *= 2
            out_ref[0, d] = tile[:, :BLOCK]

    return pl.pallas_call(
        kernel,
        grid=(heads,),
        in_specs=[pl.BlockSpec((1, 1, length), lambda h: (h, 0, 0))],
        out_specs=pl.BlockSpec((1, spans, BLOCK, BLOCK), lambda h: (h, 0, 0, 0)),
        out_shape=jax.ShapeDtypeStruct((heads, spans, BLOCK, BLOCK), F32),
        cost_estimate=pl.CostEstimate(
            flops=heads * spans * BLOCK * BLOCK * 8,
            transcendentals=0,
            bytes_accessed=heads * spans * BLOCK * BLOCK * 4,
        ),
        name="bias_tiles",
    )(line)


def diagonal_sums(tile):
    width = 2 * BLOCK
    t = jnp.concatenate([tile, jnp.zeros_like(tile)], axis=1)
    size = BLOCK
    while size > 8:
        size //= 2
        t = t[:size] + pltpu.roll(t[size:], width - size, 1)
    row = lax.broadcasted_iota(jnp.int32, (8, width), 0)
    for bit in (1, 2, 4):
        t = jnp.where((row & bit) != 0, pltpu.roll(t, width - bit, 1), t)
    return jnp.sum(t, axis=0, keepdims=True)


def head_keys(keys, limit, a):
    lane = lax.broadcasted_iota(jnp.int32, keys.shape, 1)
    place = lax.broadcasted_iota(jnp.int32, keys.shape, 0)
    mine = (lane // (PAIR // 2)) == a
    flag = jnp.where(place < limit, 0.0, MASK_VALUE)
    other = jnp.where(lane == (1 - a) * (PAIR // 2), flag, 0.0)
    return bf(jnp.where(mine, wide(keys), other))


def head_queries(queries, scale, a, mark):
    lane = lax.broadcasted_iota(jnp.int32, queries.shape, 1)
    mine = (lane // (PAIR // 2)) == a
    other = jnp.where(lane == (1 - a) * (PAIR // 2), mark, 0.0)
    return bf(jnp.where(mine, wide(queries) * scale, other))


def only_head(values, a):
    lane = lax.broadcasted_iota(jnp.int32, values.shape, 1)
    return bf(jnp.where((lane // (PAIR // 2)) == a, wide(values), 0.0))


def score_blocks(key_a, query_a, bias_ref, a, qb, key_blocks, causal):
    out = []
    for kb in range(key_blocks):
        st = dot_nt(key_a[kb * BLOCK : (kb + 1) * BLOCK], query_a)
        if bias_ref is not None:
            st = st + bias_ref[a, kb - qb + key_blocks - 1]
        if causal:
            kpos = lax.broadcasted_iota(jnp.int32, st.shape, 0)
            qpos = lax.broadcasted_iota(jnp.int32, st.shape, 1)
            st = jnp.where(kpos <= qpos, st, MASK_VALUE)
        out.append(st)
    return out


def attention_forward(queries, memory, limit, bias, causal, fused):
    query_len = queries.shape[0]
    key_len = query_len if fused else memory.shape[0]
    pairs = queries.shape[1] // ((3 if fused else 1) * PAIR)
    key_blocks, query_blocks = key_len // BLOCK, query_len // BLOCK
    scale = (PAIR // 2) ** (-0.5)

    def kernel(limit_ref, q_ref, *refs):
        refs = list(refs)
        kv_ref = q_ref if fused else refs.pop(0)
        bias_ref = refs.pop(0) if bias is not None else None
        c_ref, lse_ref = refs
        k0 = PAIR if fused else 0
        keys = kv_ref[:, k0 : k0 + PAIR]
        values = kv_ref[:, k0 + PAIR : k0 + 2 * PAIR]
        key_a = [head_keys(keys, limit_ref[0], a) for a in range(2)]

        def visit(qb):
            rows = pl.ds(pl.multiple_of(qb * BLOCK, BLOCK), BLOCK)
            q = q_ref[rows, 0:PAIR]
            parts = []
            for a in range(2):
                st = score_blocks(
                    key_a[a], head_queries(q, scale, a, 1.0), bias_ref, a, qb, key_blocks, causal
                )
                top = functools.reduce(
                    jnp.maximum, [jnp.max(b, axis=0, keepdims=True) for b in st]
                )
                ex = [jnp.exp(b - top) for b in st]
                total = sum(jnp.sum(b, axis=0, keepdims=True) for b in ex)
                ct = sum(
                    dot_tn(values[kb * BLOCK : (kb + 1) * BLOCK], bf(ex[kb]))
                    for kb in range(key_blocks)
                )
                parts.append(ct[a * (PAIR // 2) : (a + 1) * (PAIR // 2)] * (1.0 / total))
                lse_ref[0, a : a + 1, rows] = top + jnp.log(total)
            c_ref[rows, :] = bf(jnp.transpose(jnp.concatenate(parts, axis=0)))

        if query_blocks == 1:
            visit(0)
        else:
            pl.loop(0, query_blocks)(visit)

    in_specs = [pl.BlockSpec((query_len, (3 if fused else 1) * PAIR), lambda j, n: (0, j))]
    args = [queries]
    if not fused:
        in_specs.append(pl.BlockSpec((key_len, 2 * PAIR), lambda j, n: (0, j)))
        args.append(memory)
    if bias is not None:
        in_specs.append(pl.BlockSpec((2,) + bias.shape[1:], lambda j, n: (j, 0, 0, 0)))
        args.append(pltpu.with_memory_space_constraint(bias, pltpu.HBM))
    return pl.pallas_call(
        kernel,
        grid_spec=pltpu.PrefetchScalarGridSpec(
            num_scalar_prefetch=1,
            grid=(pairs,),
            in_specs=in_specs,
            out_specs=[
                pl.BlockSpec((query_len, PAIR), lambda j, n: (0, j)),
                pl.BlockSpec((1, 8, query_len), lambda j, n: (j, 0, 0)),
            ],
        ),
        out_shape=[
            jax.ShapeDtypeStruct((query_len, pairs * PAIR), BF16),
            jax.ShapeDtypeStruct((pairs, 8, query_len), F32),
        ],
        compiler_params=pltpu.CompilerParams(vmem_limit_bytes=40 << 20),
        cost_estimate=pl.CostEstimate(
            flops=pairs * 2 * query_len * key_len * PAIR * 4,
            transcendentals=pairs * 2 * query_len * key_len,
            bytes_accessed=pairs * PAIR * 2 * 2 * (query_len + key_len),
        ),
        name="attend_" + ("enc" if bias is not None else "dec" if fused else "cross"),
    )(limit, *args)


def attention_backward(queries, memory, limit, bias, causal, fused, context, lse, context_grad):
    query_len = queries.shape[0]
    key_len = query_len if fused else memory.shape[0]
    pairs = queries.shape[1] // ((3 if fused else 1) * PAIR)
    key_blocks, query_blocks = key_len // BLOCK, query_len // BLOCK
    spans = 2 * key_blocks - 1
    scale = (PAIR // 2) ** (-0.5)

    def kernel(limit_ref, q_ref, *refs):
        refs = list(refs)
        kv_ref = q_ref if fused else refs.pop(0)
        bias_ref = refs.pop(0) if bias is not None else None
        c_ref, lse_ref, dc_ref = refs[:3]
        refs = refs[3:]
        dq_ref = refs.pop(0)
        dkv_ref = dq_ref if fused else refs.pop(0)
        dq_sum = refs.pop(0)
        dkv_sum = dq_sum if fused else refs.pop(0)
        diag_ref = refs.pop(0) if bias is not None else None
        dk_acc, dv_acc = refs[:2]
        tile_acc = refs[2] if bias is not None else None
        k0 = PAIR if fused else 0
        keys = kv_ref[:, k0 : k0 + PAIR]
        values = kv_ref[:, k0 + PAIR : k0 + 2 * PAIR]
        key_a = [head_keys(keys, limit_ref[0], a) for a in range(2)]
        pure_key_a = [only_head(keys, a) for a in range(2)]
        value_a = [only_head(values, a) for a in range(2)]
        dq_sum[...] = jnp.zeros_like(dq_sum)
        dk_acc[...] = jnp.zeros_like(dk_acc)
        dv_acc[...] = jnp.zeros_like(dv_acc)
        if bias is not None:
            tile_acc[...] = jnp.zeros_like(tile_acc)

        def visit(qb):
            rows = pl.ds(pl.multiple_of(qb * BLOCK, BLOCK), BLOCK)
            q = q_ref[rows, 0:PAIR]
            dc = dc_ref[rows, :]
            both = jnp.transpose(wide(dc) * wide(c_ref[rows, :]))
            dqt = jnp.zeros((PAIR, BLOCK), F32)
            for a in range(2):
                st = score_blocks(
                    key_a[a], head_queries(q, scale, a, 1.0), bias_ref, a, qb, key_blocks, causal
                )
                delta = jnp.sum(
                    both[a * (PAIR // 2) : (a + 1) * (PAIR // 2)], axis=0, keepdims=True
                )
                log_row = lse_ref[0, a : a + 1, rows]
                dc_a = only_head(dc, a)
                q_a = head_queries(q, scale, a, 0.0)
                for kb in range(key_blocks):
                    span = slice(kb * BLOCK, (kb + 1) * BLOCK)
                    p = jnp.exp(st[kb] - log_row)
                    dp = dot_nt(value_a[a][span], dc)
                    ds = p * (dp - delta)
                    dsb = bf(ds)
                    dv_acc[span, :] += dot_nn(bf(p), dc_a)
                    dk_acc[span, :] += dot_nn(dsb, q_a)
                    dqt = dqt + dot_tn(pure_key_a[a][span], dsb)
                    if bias is not None:
                        tile_acc[a, kb - qb + key_blocks - 1] += ds
            dq = bf(jnp.transpose(dqt) * scale)
            dq_ref[rows, 0:PAIR] = dq
            dq_sum[0:1, 0:PAIR] += jnp.sum(wide(dq), axis=0, keepdims=True)

        if query_blocks == 1:
            visit(0)
        else:
            pl.loop(0, query_blocks)(visit)
        dkv_ref[:, k0 : k0 + PAIR] = bf(dk_acc[...])
        dv = bf(dv_acc[...])
        dkv_ref[:, k0 + PAIR : k0 + 2 * PAIR] = dv
        dkv_sum[0:1, k0 + PAIR : k0 + 2 * PAIR] = jnp.sum(wide(dv), axis=0, keepdims=True)
        if bias is not None:
            for a in range(2):
                for d in range(spans):
                    diag_ref[a, d : d + 1, :] = diagonal_sums(tile_acc[a, d])

    in_specs = [pl.BlockSpec((query_len, (3 if fused else 1) * PAIR), lambda j, n: (0, j))]
    args = [queries]
    if not fused:
        in_specs.append(pl.BlockSpec((key_len, 2 * PAIR), lambda j, n: (0, j)))
        args.append(memory)
    if bias is not None:
        in_specs.append(pl.BlockSpec((2,) + bias.shape[1:], lambda j, n: (j, 0, 0, 0)))
        args.append(pltpu.with_memory_space_constraint(bias, pltpu.HBM))
    in_specs += [
        pl.BlockSpec((query_len, PAIR), lambda j, n: (0, j)),
        pl.BlockSpec((1, 8, query_len), lambda j, n: (j, 0, 0)),
        pl.BlockSpec((query_len, PAIR), lambda j, n: (0, j)),
    ]
    args += [context, lse, context_grad]
    out_specs = [pl.BlockSpec((query_len, (3 if fused else 1) * PAIR), lambda j, n: (0, j))]
    out_shape = [jax.ShapeDtypeStruct(queries.shape, BF16)]
    scratch = [pltpu.VMEM((key_len, PAIR), F32)] * 2
    if not fused:
        out_specs.append(pl.BlockSpec((key_len, 2 * PAIR), lambda j, n: (0, j)))
        out_shape.append(jax.ShapeDtypeStruct(memory.shape, BF16))
    for array, tiles in ((queries, 3 if fused else 1), (memory, 2)):
        if array is not None:
            out_specs.append(pl.BlockSpec((8, tiles * PAIR), lambda j, n: (0, j)))
            out_shape.append(jax.ShapeDtypeStruct((8, array.shape[1]), F32))
    if bias is not None:
        out_specs.append(pl.BlockSpec((2, 8, 2 * BLOCK), lambda j, n: (j, 0, 0)))
        out_shape.append(jax.ShapeDtypeStruct((2 * pairs, 8, 2 * BLOCK), F32))
        scratch.append(pltpu.VMEM((2, spans, BLOCK, BLOCK), F32))
    return pl.pallas_call(
        kernel,
        grid_spec=pltpu.PrefetchScalarGridSpec(
            num_scalar_prefetch=1,
            grid=(pairs,),
            in_specs=in_specs,
            out_specs=out_specs,
            scratch_shapes=scratch,
        ),
        out_shape=out_shape,
        compiler_params=pltpu.CompilerParams(vmem_limit_bytes=40 << 20),
        cost_estimate=pl.CostEstimate(
            flops=pairs * 2 * query_len * key_len * PAIR * 10,
            transcendentals=pairs * 2 * query_len * key_len,
            bytes_accessed=pairs * PAIR * 2 * 4 * (query_len + key_len),
        ),
        name="attend_back_" + ("enc" if bias is not None else "dec" if fused else "cross"),
    )(limit, *args)


def gelu(z):
    return z * (0.5 * (1.0 + lax.erf(z * ROOT_HALF)))


def gelu_slope(z):
    return 0.5 * (1.0 + lax.erf(z * ROOT_HALF)) + z * jnp.exp(-0.5 * z * z) * INV_ROOT_TAU


ROWS = 128


def row_steps(count, body):
    @pl.loop(0, count // ROWS)
    def _(step):
        body(pl.ds(pl.multiple_of(step * ROWS, ROWS), ROWS), step)


def add_norm(residual, own_part, other_part, vecs, bias, gain, shift):
    source, affine = residual if isinstance(residual, tuple) else (residual, None)
    count, width = source.shape

    def kernel(x_ref, p_ref, q_ref, v_ref, low_ref, normed_ref, inv_ref):
        def body(rows, step):
            base = wide(x_ref[rows])
            if affine is not None:
                base = base * v_ref[affine[0] : affine[0] + 1] + v_ref[affine[1] : affine[1] + 1]
            values = base + (wide(p_ref[rows]) + wide(q_ref[rows])) + v_ref[bias : bias + 1]
            center = values - jnp.sum(values, axis=-1, keepdims=True) * (1.0 / width)
            square = jnp.sum(center * center, axis=-1, keepdims=True)
            inv = lax.rsqrt(square * (1.0 / width) + EPSILON)
            normed = center * inv
            low_ref[rows] = bf(normed * v_ref[gain : gain + 1] + v_ref[shift : shift + 1])
            normed_ref[rows] = normed
            inv_ref[rows] = jnp.broadcast_to(inv, (ROWS, PAIR))

        row_steps(count, body)

    return pl.pallas_call(
        kernel,
        in_specs=[ON_CHIP] * 4,
        out_specs=[ON_CHIP] * 3,
        out_shape=[
            jax.ShapeDtypeStruct((count, width), BF16),
            jax.ShapeDtypeStruct((count, width), F32),
            jax.ShapeDtypeStruct((count, PAIR), F32),
        ],
        cost_estimate=pl.CostEstimate(
            flops=12 * count * width, transcendentals=count, bytes_accessed=14 * count * width
        ),
        name="add_norm",
    )(source, own_part, other_part, vecs)


def norm_back(terms, limit, normed, inv, vecs, gain):
    count, width = normed.shape
    use = limit is not None

    def kernel(*refs):
        refs = list(refs)
        limit_ref = refs.pop(0) if use else None
        ins, (n_ref, inv_ref, v_ref, grad_ref, low_ref, sum_ref) = refs[:-6], refs[-6:]
        sum_ref[...] = jnp.zeros_like(sum_ref)

        def body(rows, step):
            up = wide(ins[0][rows])
            if use:
                place = step * ROWS + lax.broadcasted_iota(jnp.int32, up.shape, 0)
                up = jnp.where(place < limit_ref[0], up, 0.0)
            rest = [wide(r[rows]) for r in ins[1:]]
            if rest:
                up = up + (rest[0] + rest[1])
            values = n_ref[rows]
            scaled = up * v_ref[gain : gain + 1]
            mean = jnp.sum(scaled, axis=-1, keepdims=True) * (1.0 / width)
            along = jnp.sum(scaled * values, axis=-1, keepdims=True) * (1.0 / width)
            grad = inv_ref[rows, :1] * (scaled - mean - values * along)
            grad_ref[rows] = grad
            low_ref[rows] = bf(grad)
            sum_ref[0:1] += jnp.sum(up * values, axis=0, keepdims=True)
            sum_ref[1:2] += jnp.sum(up, axis=0, keepdims=True)
            sum_ref[2:3] += jnp.sum(grad, axis=0, keepdims=True)

        row_steps(count, body)

    smem = [pl.BlockSpec(memory_space=pltpu.SMEM)] if use else []
    return pl.pallas_call(
        kernel,
        in_specs=smem + [ON_CHIP] * (len(terms) + 3),
        out_specs=[ON_CHIP] * 3,
        out_shape=[
            jax.ShapeDtypeStruct((count, width), F32),
            jax.ShapeDtypeStruct((count, width), BF16),
            jax.ShapeDtypeStruct((8, width), F32),
        ],
        cost_estimate=pl.CostEstimate(
            flops=16 * count * width, transcendentals=0, bytes_accessed=20 * count * width
        ),
        name="norm_back",
    )(*([limit] if use else []), *terms, normed, inv, vecs)


NORM_ROWS = 15


def pack_small(norm_sums, enc_sum, dec_sum, query_sum, memory_sum, unit_sums, diag, buckets):
    width = norm_sums[0].shape[1]
    heads, _, span = diag.shape
    spans = 2 * (span // BLOCK) + 1
    length = (spans + 1) * BLOCK

    def kernel(*refs):
        one, two, d_one, d_two, d_three = refs[:5]
        enc_ref, dec_ref, query_ref, memory_ref, unit_ref, dec_unit_ref, diag_ref = refs[5:12]
        outs, line = refs[12:14], refs[14]
        norms = [(one, 0), (one, 1), (two, 0), (two, 1), (one, 2), (two, 2)]
        norms += [(r, i) for r in (d_one, d_two, d_three) for i in range(2)]
        norms += [(r, 2) for r in (d_one, d_two, d_three)]
        tiles = [(enc_ref, 3, 0), (enc_ref, 3, 2), (dec_ref, 3, 0)]
        tiles += [(dec_ref, 3, 2), (query_ref, 1, 0), (memory_ref, 2, 1)]
        line[...] = jnp.zeros_like(line)
        for h in range(heads):
            for d in range(spans):
                row = diag_ref[h, d : d + 1, :]
                start = (spans - 1 - d) * BLOCK
                line[h : h + 1, start : start + BLOCK] += row[:, BLOCK:]
                line[h : h + 1, start + BLOCK : start + 2 * BLOCK] += row[:, :BLOCK]
        wide_table = -(-buckets // PAIR) * PAIR
        dist = length // 2 - lax.broadcasted_iota(jnp.int32, (length, wide_table), 0)
        bucket = jnp.clip(dist, -(buckets // 2), buckets // 2 - 1) + buckets // 2
        hot = jnp.where(
            bucket == lax.broadcasted_iota(jnp.int32, (length, wide_table), 1), 1.0, 0.0
        )
        table = jnp.dot(
            line[...], hot, precision=lax.Precision.HIGHEST, preferred_element_type=F32
        )
        for dx, out in enumerate(outs):
            out[...] = jnp.zeros_like(out)
            for i, (ref, r) in enumerate(norms):
                out[i : i + 1, :] = ref[r : r + 1, :]
            for i, (ref, stride, at) in enumerate(tiles):
                row, lane = NORM_ROWS + i // 3, (i % 3) * 2 * PAIR
                part = [ref[0:1, (j * stride + at) * PAIR : (j * stride + at + 1) * PAIR] for j in range(3)]
                out[row : row + 1, lane : lane + PAIR] = part[dx]
                both = jnp.broadcast_to(part[2], (8, PAIR))
                both = pltpu.roll(both, PAIR // 2, 1) if dx else both
                out[row : row + 1, lane + PAIR : lane + 2 * PAIR] = both[0:1]
            for i, ref in enumerate((unit_ref, dec_unit_ref)):
                out[NORM_ROWS + 2 + i : NORM_ROWS + 3 + i, :] = ref[0:1, dx * width : (dx + 1) * width]
            for i, h in enumerate(((0, 1, 4), (2, 3, 5))[dx]):
                out[NORM_ROWS + 4 + i : NORM_ROWS + 5 + i, 0:wide_table] = table[h : h + 1]

    return pl.pallas_call(
        kernel,
        out_shape=[jax.ShapeDtypeStruct((24, width), F32)] * 2,
        scratch_shapes=[pltpu.VMEM((8, length), F32)],
        compiler_params=pltpu.CompilerParams(vmem_limit_bytes=32 << 20),
        name="pack_small",
    )(*norm_sums, enc_sum, dec_sum, query_sum, memory_sum, *unit_sums, diag)


def update_matrices(sums, alternative, own, state, rate, inverse, packed):
    master = state[0]
    count, rows, cols = master.shape
    step = 2 if packed else 1
    arrays = list(sums) + ([alternative] if alternative is not None else [])

    def kernel(own_ref, inv_ref, *refs):
        if packed:
            groups = [refs[2 * i : 2 * i + 2] for i in range(len(arrays))]
            refs = refs[2 * len(arrays) :]
        else:
            groups = [refs[i : i + 1] for i in range(len(arrays))]
            refs = refs[len(arrays) :]
        state_refs, outs = refs[:3], refs[3:]
        inv = inv_ref[0]

        def total(part, i):
            vals = [wide(g[part][i]) for g in groups]
            if alternative is not None:
                vals = [jnp.where(own_ref[0] == 1, vals[-1], vals[0])] + vals[1:-1]
            return functools.reduce(jnp.add, vals)

        def advance(grad, i, span):
            mean_grad = grad * inv
            new_moment = MOMENTUM * state_refs[1][i, :, span] + mean_grad
            new_master = state_refs[0][i, :, span] - rate * (mean_grad + MOMENTUM * new_moment)
            outs[0][i, :, span] = mean_grad
            outs[1][i, :, span] = new_master
            outs[2][i, :, span] = new_moment
            outs[3][i, :, span] = (
                AVERAGING * state_refs[2][i, :, span] + (1.0 - AVERAGING) * new_master
            )
            outs[4][i, :, span] = bf(new_master)

        if packed:
            rest = total(1, 0)
            turned = pltpu.roll(rest, PAIR // 2, 1)
            for i in range(2):
                advance(total(0, i), i, slice(0, PAIR))
                advance((turned if i else rest)[:, : PAIR // 2], i, slice(PAIR, cols))
        else:
            advance(total(0, 0), 0, slice(0, cols))

    in_specs, args = [], []
    for a in arrays:
        in_specs.append(pl.BlockSpec((step, rows, a.shape[2]), lambda k, o: (k, 0, 0)))
        args.append(a)
        if packed:
            in_specs.append(pl.BlockSpec((1, rows, PAIR), lambda k, o: (count + k, 0, 0)))
            args.append(a)
    spec = pl.BlockSpec((step, rows, cols), lambda k, o: (k, 0, 0))
    return pl.pallas_call(
        kernel,
        grid_spec=pltpu.PrefetchScalarGridSpec(
            num_scalar_prefetch=1,
            grid=(count // step,),
            in_specs=[pl.BlockSpec(memory_space=pltpu.SMEM)] + in_specs + [spec] * 3,
            out_specs=[spec] * 5,
        ),
        out_shape=[jax.ShapeDtypeStruct(master.shape, F32)] * 4
        + [jax.ShapeDtypeStruct(master.shape, BF16)],
        cost_estimate=pl.CostEstimate(
            flops=12 * master.size, transcendentals=0, bytes_accessed=44 * master.size
        ),
        name="update_matrices",
    )(own, inverse, *args, *state)


def place_quarters(parts, index):
    count = len(parts)

    def kernel(idx, *refs):
        out, sem = refs[count], refs[count + 1]
        copies = [
            pltpu.make_async_copy(refs[k], out.at[idx[k]], sem.at[k]) for k in range(count)
        ]
        for copy in copies:
            copy.start()
        for copy in copies:
            copy.wait()

    return pl.pallas_call(
        kernel,
        in_specs=[pl.BlockSpec(memory_space=pltpu.SMEM)] + [ON_CHIP] * count,
        out_specs=pl.BlockSpec(memory_space=pl.ANY),
        out_shape=jax.ShapeDtypeStruct((count,) + parts[0].shape, parts[0].dtype),
        scratch_shapes=[pltpu.SemaphoreType.DMA((count,))],
        cost_estimate=pl.CostEstimate(
            flops=0, transcendentals=0, bytes_accessed=4 * count * parts[0].size
        ),
        name="place_quarters",
    )(index, *parts)


def update(master, moment, average, gradient, rate, frame_total):
    mean_grad = gradient / frame_total
    new_moment = MOMENTUM * moment + mean_grad
    new_master = master - rate * (mean_grad + MOMENTUM * new_moment)
    new_average = AVERAGING * average + (1.0 - AVERAGING) * new_master
    return mean_grad, new_master, new_moment, new_average


def order_cols(v0, v1):
    return jnp.concatenate(
        [v0[..., :PAIR], v1[..., :PAIR], v0[..., PAIR:], v1[..., PAIR:]], axis=-1
    )


CROSS_PLANS = [
    [(0, j) for j in range(3)],
    [(m, j) for j in range(3) for m in (1, 2)],
    [(3, j) for j in range(3)],
]
QKV_PLAN = [(m, j) for j in range(3) for m in range(3)]
ENC_PLANS = [QKV_PLAN, [(3, j) for j in range(3)]]

def local(
    frames,
    cotangent,
    lengths,
    attn_master,
    attn_moment,
    attn_average,
    ffn_master,
    ffn_moment,
    ffn_average,
    norm_vecs,
    norm_moment,
    norm_average,
    col_bias,
    col_moment,
    col_average,
    rel_table,
    rel_moment,
    rel_average,
    dec_frames,
    dec_cotangent,
    text_lengths,
    dec_attn_master,
    dec_attn_moment,
    dec_attn_average,
    dec_ffn_master,
    dec_ffn_moment,
    dec_ffn_average,
    dec_norm_vecs,
    dec_norm_moment,
    dec_norm_average,
    dec_col_bias,
    dec_col_moment,
    dec_col_average,
):
    n_dp = lax.axis_size("dp")
    z, s, m = lax.axis_index("dp"), lax.axis_index("seq"), lax.axis_index("mp")
    y = m // 2
    utt_count, half_len, width = frames.shape
    text_half = dec_frames.shape[1]
    full_len, text_full = 2 * half_len, 2 * text_half
    own = s == y
    yidx = jnp.stack([y, 1 - y, own.astype(jnp.int32)]).astype(jnp.int32)
    root_frames = float(utt_count * full_len * n_dp) ** 0.5

    mine = jnp.concatenate(
        [
            lax.dynamic_index_in_dim(parts, m, 0, keepdims=False)
            for parts in (frames, cotangent, dec_frames, dec_cotangent)
        ]
    )
    other = swap_core(mine)
    dffn_shard = bf(dec_ffn_master)
    dffn_parts = gather_plane(dffn_shard)
    attn_z = gather_dp(pack_attn(bf(attn_master)))
    packed = jnp.concatenate([col_bias, dec_col_bias, rel_table.T.reshape(-1)])
    groups = [jnp.where(own, packed, spread(packed, 0, 0)), spread(packed, 1, 0)]
    ffn_z = gather_dp(after(bf(ffn_master), attn_z))
    mine, other, dffn_parts, attn_z, groups, dattn_low, lengths = stage(
        mine, other, dffn_parts, attn_z, groups, dec_attn_master, lengths
    )
    dattn_low = bf(dattn_low)
    attn_pieces = gather_plane(attn_z)

    bucket_count, group_heads = rel_table.shape
    group_width = attn_master.shape[2]
    unit_count = ffn_master.shape[2]
    enc_cols, dec_cols = col_bias.shape[0], dec_col_bias.shape[0]

    def cols_at(start):
        return order_cols(*[g[start : start + group_width] for g in groups])

    def units_at(start):
        return jnp.concatenate([g[start : start + unit_count] for g in groups])

    def qkv_bias(q, v):
        blank = jnp.zeros((PAIR,), F32)
        cut = [slice(j * PAIR, (j + 1) * PAIR) for j in range(3)]
        return jnp.concatenate([part for c in cut for part in (q[c], blank, v[c])])

    bias_qkv = qkv_bias(cols_at(0), cols_at(group_width))
    bias_one = units_at(2 * group_width)
    bias_dqkv = qkv_bias(cols_at(enc_cols), cols_at(enc_cols + group_width))
    bias_cq = cols_at(enc_cols + 2 * group_width)
    cv = cols_at(enc_cols + 3 * group_width)
    blank = jnp.zeros((PAIR,), F32)
    bias_ckv = jnp.concatenate(
        [part for j in range(3) for part in (blank, cv[j * PAIR : (j + 1) * PAIR])]
    )
    bias_done = units_at(enc_cols + 4 * group_width)
    tables = [
        g[enc_cols + dec_cols :].reshape(group_heads, bucket_count) for g in groups
    ]
    heads = jnp.stack(
        [tables[0][0], tables[0][1], tables[1][0], tables[1][1], tables[0][2], tables[1][2]]
    )
    max_dist = bucket_count // 2
    blocks = full_len // BLOCK
    lead = blocks * BLOCK - max_dist + 1
    tail = blocks * BLOCK - max_dist - 1
    line = jnp.pad(heads[:, ::-1], ((0, 0), (lead, tail)), mode="edge")
    bias = bias_tiles(line[:, None, :], blocks)

    def all_rows(start, count):
        ours, theirs = mine[start : start + count], other[start : start + count]
        return jnp.concatenate([jnp.where(s == 0, ours, theirs), jnp.where(s == 0, theirs, ours)])

    inputs = all_rows(0, half_len)
    upstream_in = all_rows(half_len, half_len)
    text_in = all_rows(2 * half_len, text_half)
    text_upstream = all_rows(2 * half_len + text_half, text_half)
    limit = lax.dynamic_slice_in_dim(lengths, m, 1)
    text_limit = lax.dynamic_slice_in_dim(text_lengths, m, 1)
    own_flag = own.astype(jnp.int32).reshape(1)

    def my_half(rows):
        count = rows.shape[0] // 2
        return lax.dynamic_slice_in_dim(rows, s * count, count, 0)

    def to_owners(mine):
        return [mine] + [swap_mp(mine, bits) for bits in range(1, 4)]

    owners = m ^ jnp.arange(4, dtype=jnp.int32)

    frame_count = jnp.sum(lengths)
    digit_row = lax.broadcasted_iota(jnp.int32, (1,) + dec_attn_master.shape[1:2] + (PAIR,), 1)
    digits = bf(jnp.where(digit_row == 0, frame_count // 256, frame_count % 256))

    attn_pieces, ffn_z, bias, bias_qkv, inputs, dattn_shard, dffn_plane = stage(
        attn_pieces,
        ffn_z,
        bias,
        bias_qkv,
        inputs,
        jnp.concatenate(
            [pack_attn(dattn_low[:4]), pack_attn(dattn_low[4:]), digits]
        ),
        jnp.stack([jnp.where(own, dffn_parts[0], dffn_parts[1]), *dffn_parts[2:]]),
    )
    ffn_pieces = gather_plane(ffn_z)
    dattn_z = gather_dp(dattn_shard)
    w_qkv, w_o = assemble_attn(attn_pieces, ENC_PLANS, 4, yidx)
    qkv = bf(dot_nn(inputs, w_qkv) + bias_qkv)
    context, lse = attention_forward(qkv, None, limit, bias, False, True)
    part = bf(dot_nt(context, w_o))
    ffn_pieces, dattn_z, part, dffn_plane = stage(ffn_pieces, dattn_z, part, dffn_plane)
    tiles = dattn_z.shape[1] // 2
    frame_total = jnp.sum(wide(dattn_z[:, -1, 0, 0]) * 256.0 + wide(dattn_z[:, -1, 1, 0]))
    inverse = (1.0 / frame_total).reshape(1)
    cross_z = dattn_z[:, tiles : 2 * tiles]
    self_pieces = gather_plane(dattn_z[:, :tiles])
    dffn_planes = gather_dp(dffn_plane.reshape((2, 2) + dffn_shard.shape))
    hidden_low, normed_one, inv_one = add_norm(
        inputs, part, swap_core(part), norm_vecs, 4, 0, 1
    )
    w_one, w_two = assemble_ffn(ffn_pieces, yidx)
    gate_in = dot_nn(hidden_low, w_one) + bias_one
    activated, slope = bf(gelu(gate_in)), bf(gelu_slope(gate_in))
    part = bf(dot_nt(activated, w_two))
    self_pieces, cross_z, part, activated, slope = stage(
        self_pieces, cross_z, part, activated, slope
    )
    cross_pieces = gather_plane(cross_z)
    enc_low, normed_two, inv_two = add_norm(
        (normed_one, (0, 1)), part, swap_core(part), norm_vecs, 5, 2, 3
    )
    out_enc = lax.all_gather(after(my_half(enc_low), dffn_planes), "mp", axis=0, tiled=False)

    d_qkv, d_o = assemble_attn(self_pieces, ENC_PLANS, 4, yidx)
    dqkv = bf(dot_nn(text_in, d_qkv) + bias_dqkv)
    self_context, self_lse = attention_forward(dqkv, None, text_limit, None, True, True)
    part, cross_pieces = stage(bf(dot_nt(self_context, d_o)), cross_pieces)
    c_q, c_kv, c_o = assemble_attn(cross_pieces, CROSS_PLANS, 4, yidx)
    dw_one, dw_two = assemble_planes(dffn_planes, yidx)
    dec_one_low, normed_d1, inv_d1 = add_norm(
        text_in, part, swap_core(part), dec_norm_vecs, 6, 0, 1
    )
    cross_q = bf(dot_nn(dec_one_low, c_q) + bias_cq)
    cross_kv = bf(dot_nn(enc_low, c_kv) + bias_ckv)
    cross_context, cross_lse = attention_forward(cross_q, cross_kv, limit, None, False, False)
    part = bf(dot_nt(cross_context, c_o))
    dec_two_low, normed_d2, inv_d2 = add_norm(
        (normed_d1, (0, 1)), part, swap_core(part), dec_norm_vecs, 7, 2, 3
    )
    dec_gate = dot_nn(dec_two_low, dw_one) + bias_done
    dec_act, dec_slope = bf(gelu(dec_gate)), bf(gelu_slope(dec_gate))
    part, dec_act, dec_slope = stage(bf(dot_nt(dec_act, dw_two)), dec_act, dec_slope)
    dec_low, normed_d3, inv_d3 = add_norm(
        (normed_d2, (2, 3)), part, swap_core(part), dec_norm_vecs, 8, 4, 5
    )
    grad_d3, dec_ffn_back, sums_d3 = norm_back(
        [text_upstream], text_limit, normed_d3, inv_d3, dec_norm_vecs, 4
    )
    dec_gate_grad = bf(dot_nn(dec_ffn_back, dw_two) * wide(dec_slope))
    part = bf(dot_nt(dec_gate_grad, dw_one))
    dec_ffn_grads = [
        bf(dot_tn(dec_two_low, dec_gate_grad)),
        bf(dot_tn(dec_ffn_back, dec_act)),
    ]
    dec_ffn_planes, part, sent, out_enc = stage(
        split_planes(dec_ffn_grads, n_dp, yidx), part, my_half(dec_low), out_enc
    )
    dec_ffn_plane = scatter_dp(dec_ffn_planes)
    out_dec = to_owners(sent)

    grad_d2, cross_back, sums_d2 = norm_back(
        [grad_d3, part, swap_core(part)], None, normed_d2, inv_d2, dec_norm_vecs, 2
    )
    cross_qg, cross_kvg, query_sum, memory_sum = attention_backward(
        cross_q,
        cross_kv,
        limit,
        None,
        False,
        False,
        cross_context,
        cross_lse,
        bf(dot_nn(cross_back, c_o)),
    )
    cross_grads = [
        bf(dot_tn(dec_one_low, cross_qg)),
        bf(dot_tn(enc_low, cross_kvg)),
        bf(dot_tn(cross_back, cross_context)),
    ]
    query_part, memory_part, cross_parts, out_dec = stage(
        bf(dot_nt(cross_qg, c_q)),
        bf(dot_nt(cross_kvg, c_kv)),
        split_attn(cross_grads, CROSS_PLANS, 4, n_dp, yidx),
        out_dec,
    )
    out_dec = place_quarters(out_dec, owners)
    cross_plane_back = scatter_plane(cross_parts)
    memory_other = swap_core(memory_part)
    grad_d1, self_back, sums_d1 = norm_back(
        [grad_d2, query_part, swap_core(query_part)], None, normed_d1, inv_d1, dec_norm_vecs, 0
    )
    self_g, dec_sum = attention_backward(
        dqkv,
        None,
        text_limit,
        None,
        True,
        True,
        self_context,
        self_lse,
        bf(dot_nn(self_back, d_o)),
    )
    text_part = bf(dot_nt(self_g, d_qkv))
    self_grads = [bf(dot_tn(text_in, self_g)), bf(dot_tn(self_back, self_context))]
    self_parts = split_attn(self_grads, ENC_PLANS, 4, n_dp, yidx)

    self_parts, memory_part, memory_other, cross_parts, cross_plane_back, text_part = stage(
        self_parts, memory_part, memory_other, cross_parts, cross_plane_back, text_part
    )
    self_plane_back = scatter_plane(self_parts)
    text_other = swap_core(text_part)
    cross_total = scatter_dp(sum_plane(cross_parts, cross_plane_back, own))
    grad_two, ffn_back, sums_two = norm_back(
        [upstream_in, memory_part, memory_other], limit, normed_two, inv_two, norm_vecs, 2
    )
    gate_grad = bf(dot_nn(ffn_back, w_two) * wide(slope))
    ffn_grads = [bf(dot_tn(hidden_low, gate_grad)), bf(dot_tn(ffn_back, activated))]
    part, self_parts, self_plane_back, ffn_parts, text_other = stage(
        bf(dot_nt(gate_grad, w_one)),
        self_parts,
        self_plane_back,
        split_ffn(ffn_grads, n_dp, yidx),
        text_other,
    )
    text_grad = my_half(grad_d1) + (wide(my_half(text_part)) + wide(my_half(text_other)))
    self_total = scatter_dp(sum_plane(self_parts, self_plane_back, own))
    ffn_plane_back = scatter_plane(ffn_parts)
    grad_one, attn_back, sums_one = norm_back(
        [grad_two, part, swap_core(part)], None, normed_one, inv_one, norm_vecs, 0
    )
    enc_g, enc_sum, diag = attention_backward(
        qkv, None, limit, bias, False, True, context, lse, bf(dot_nn(attn_back, w_o))
    )
    ffn_parts, ffn_plane_back, part, enc_g, diag, text_low, dec_ffn_plane = stage(
        ffn_parts,
        ffn_plane_back,
        bf(dot_nt(enc_g, w_qkv)),
        enc_g,
        diag,
        bf(text_grad),
        dec_ffn_plane,
    )
    out_text_grad = to_owners(text_low)
    ffn_total = scatter_dp(sum_plane(ffn_parts, ffn_plane_back, own))
    plane_parts = [dec_ffn_plane[dx, a] for dx, a in ROUTES]
    dec_ffn_sums = scatter_plane(plane_parts)
    input_grad = my_half(grad_one) + (wide(my_half(part)) + wide(my_half(swap_core(part))))
    attn_grads = [bf(dot_tn(inputs, enc_g)), bf(dot_tn(attn_back, context))]
    attn_parts = split_attn(attn_grads, ENC_PLANS, 4, n_dp, yidx)
    def col_sum(a):
        return dot_nn(jnp.ones((8, a.shape[0]), BF16), a)

    vectors = pack_small(
        [sums_one, sums_two, sums_d1, sums_d2, sums_d3],
        enc_sum,
        dec_sum,
        query_sum,
        memory_sum,
        [col_sum(gate_grad), col_sum(dec_gate_grad)],
        diag,
        bucket_count,
    )
    attn_parts, input_grad, vectors, out_text_grad, dec_ffn_sums = stage(
        attn_parts, input_grad, vectors, out_text_grad, dec_ffn_sums
    )
    out_text_grad = place_quarters(out_text_grad, owners)
    attn_plane_back = scatter_plane(attn_parts)
    small = vectors[0] + swap_mp(vectors[1], 1)
    small = jnp.where(own, small, unspread(small, 0, 0))
    dec_attn_total = jnp.concatenate(
        [self_total[:4], cross_total[:4], self_total[4:], cross_total[4:]]
    )
    matrix_rate = MATRIX_RATE * root_frames
    vector_rate = VECTOR_RATE * root_frames
    ffn_new = update_matrices(
        [ffn_total],
        None,
        own_flag,
        (ffn_master, ffn_moment, ffn_average),
        matrix_rate,
        inverse,
        False,
    )
    dattn_new = update_matrices(
        [dec_attn_total],
        None,
        own_flag,
        (dec_attn_master, dec_attn_moment, dec_attn_average),
        matrix_rate,
        inverse,
        True,
    )
    dffn_new = update_matrices(
        dec_ffn_sums,
        plane_parts[0],
        own_flag,
        (dec_ffn_master, dec_ffn_moment, dec_ffn_average),
        matrix_rate,
        inverse,
        False,
    )
    small, out_dec, out_text_grad, *_ = stage(
        small, out_dec, out_text_grad, ffn_new[4], dattn_new[4], dffn_new[4]
    )
    small = small + swap_core(small)
    attn_parts, attn_plane_back, small, input_grad = stage(
        attn_parts, attn_plane_back, small, input_grad
    )
    attn_total = scatter_dp(sum_plane(attn_parts, attn_plane_back, own))
    out_input_grad = place_quarters(to_owners(bf(input_grad)), owners)
    small = sum_dp(small)
    def head_bias(i):
        row, lane = NORM_ROWS + i // 3, (i % 3) * 2 * PAIR
        return small[row, lane : lane + group_width]

    norm_total = small[: norm_vecs.shape[0]]
    dec_norm_total = small[norm_vecs.shape[0] : NORM_ROWS]
    col_total = jnp.concatenate([head_bias(0), head_bias(1), small[NORM_ROWS + 2]])
    dec_col_total = jnp.concatenate([head_bias(i) for i in range(2, 6)] + [small[NORM_ROWS + 3]])
    table_total = small[NORM_ROWS + 4 : NORM_ROWS + 4 + group_heads, :bucket_count].T

    attn_new = update_matrices(
        [attn_total],
        None,
        own_flag,
        (attn_master, attn_moment, attn_average),
        matrix_rate,
        inverse,
        True,
    )
    norm_new = update(norm_vecs, norm_moment, norm_average, norm_total, vector_rate, frame_total)
    col_new = update(col_bias, col_moment, col_average, col_total, vector_rate, frame_total)
    rel_new = update(rel_table, rel_moment, rel_average, table_total, vector_rate, frame_total)
    dnorm_new = update(
        dec_norm_vecs, dec_norm_moment, dec_norm_average, dec_norm_total, vector_rate, frame_total
    )
    dcol_new = update(
        dec_col_bias, dec_col_moment, dec_col_average, dec_col_total, vector_rate, frame_total
    )
    return (
        out_enc,
        out_input_grad,
        attn_new[0],
        ffn_new[0],
        *attn_new[1:],
        *ffn_new[1:],
        *norm_new[1:],
        *col_new[1:],
        *rel_new[1:],
        out_dec,
        out_text_grad,
        dattn_new[0],
        dffn_new[0],
        *dattn_new[1:],
        *dffn_new[1:],
        *dnorm_new[1:],
        *dcol_new[1:],
    )


def solution(mesh):
    rows = P("dp", "seq", None)
    matrix = P(None, ("dp", "seq"), "mp")
    table = P(None, "mp")
    enc_params = [matrix] * 6 + [P()] * 3 + [P("mp")] * 3 + [table] * 3
    dec_params = [matrix] * 6 + [P()] * 3 + [P("mp")] * 3
    in_specs = (rows, rows, P("dp"), *enc_params, rows, rows, P("dp"), *dec_params)
    out_specs = (
        [rows, rows]
        + [matrix] * 10
        + [P()] * 3
        + [P("mp")] * 3
        + [table] * 3
        + [rows, rows]
        + [matrix] * 10
        + [P()] * 3
        + [P("mp")] * 3
    )
    return jax.shard_map(
        local, mesh=mesh, in_specs=in_specs, out_specs=tuple(out_specs), check_vma=False
    )
```

```python
import functools

import jax
import jax.numpy as jnp
from jax import lax
from jax.experimental import pallas as pl
from jax.experimental.pallas import tpu as pltpu
from jax.sharding import PartitionSpec as P

EPSILON = 1e-05
MOMENTUM = 0.9
AVERAGING = 0.75
MATRIX_RATE = 0.02
VECTOR_RATE = 0.2
MASK_VALUE = -1e30
ROOT_HALF = 0.7071067811865476
INV_ROOT_TAU = 0.3989422804014327
BLOCK = 256
PAIR = 128
BF16 = jnp.bfloat16
F32 = jnp.float32
ON_CHIP = pl.BlockSpec(memory_space=pltpu.VMEM)
SCALARS = pl.BlockSpec(memory_space=pltpu.SMEM)


def bf(a):
    return a.astype(BF16)


def wide(a):
    return a.astype(F32)


def dot_nn(left, right):
    return jnp.dot(left, right, preferred_element_type=F32)


def dot_nt(left, right):
    return lax.dot_general(left, right, (((1,), (1,)), ((), ())), preferred_element_type=F32)


def dot_tn(left, right):
    return lax.dot_general(left, right, (((0,), (0,)), ((), ())), preferred_element_type=F32)


def swap_core(v):
    return lax.ppermute(v, "seq", [(0, 1), (1, 0)])


def swap_mp(v, bits):
    return lax.ppermute(v, "mp", [(m, m ^ bits) for m in range(4)])


def spread_perm(dx, flip):
    pairs = [
        (s * 4 + y * 2 + x, y * 4 + (s ^ flip) * 2 + (x ^ dx))
        for s in range(2)
        for y in range(2)
        for x in range(2)
    ]
    return [(a, b) for a, b in pairs if a != b]


ROUTES = [(dx, flip) for dx in range(2) for flip in range(2)]


def spread(v, dx, flip):
    return lax.ppermute(v, ("seq", "mp"), spread_perm(dx, flip))


def unspread(v, dx, flip):
    return lax.ppermute(v, ("seq", "mp"), [(d, s) for s, d in spread_perm(dx, flip)])


def sum_dp(v):
    n = lax.axis_size("dp")
    if n != 4:
        return lax.psum(v, "dp")
    for bits in (1, 2):
        v = v + lax.ppermute(v, "dp", [(i, i ^ bits) for i in range(n)])
    return v


def stage(*values):
    return lax.optimization_barrier(values)


def after(values, *others):
    return lax.optimization_barrier((values, others))[0]


def gather_dp(shard):
    return lax.all_gather(shard, "dp", axis=0, tiled=False)


def scatter_dp(whole):
    return lax.psum_scatter(whole, "dp", scatter_dimension=0, tiled=False)


def gather_plane(v):
    return [v] + [spread(v, dx, flip) for dx, flip in ROUTES]


def scatter_plane(pieces):
    return [unspread(p, dx, flip) for p, (dx, flip) in zip(pieces, ROUTES)]


def sum_plane(pieces, back, own):
    first = jnp.where(own, wide(pieces[0]), wide(back[0]))
    return bf(first + sum(wide(b) for b in back[1:]))


def pack_attn(shard):
    main, rest = shard[:, :, :PAIR], shard[:, :, PAIR:]
    return jnp.concatenate([main, jnp.concatenate([rest[0::2], rest[1::2]], axis=-1)], axis=0)


def half_lanes(shape):
    return lax.broadcasted_iota(jnp.int32, shape, len(shape) - 1) < PAIR // 2


def half_roll(v):
    return bf(pltpu.roll(wide(v), PAIR // 2, 1))


def assemble_attn(pieces, plans, count, yidx):
    n, tiles, rows, _ = pieces[0].shape

    def kernel(yi, *refs):
        ins, outs = refs[:5], refs[5:]
        low = half_lanes((rows, PAIR))
        for k in range(n):
            for a in range(2):
                side = yi[a]

                def tile(t, dx):
                    val = ins[1 + dx * 2 + a][k, t]
                    return jnp.where(yi[2] == 1, ins[0][k, t], val) if dx + a == 0 else val

                for out, plan in zip(outs, plans):
                    for place, (mat, j) in enumerate(plan):
                        if j < 2:
                            val = tile(mat, j)
                        else:
                            t0, t1 = tile(count + mat // 2, 0), tile(count + mat // 2, 1)
                            if mat % 2 == 0:
                                val = jnp.where(low, t0, half_roll(t1))
                            else:
                                val = jnp.where(low, half_roll(t0), t1)
                        out[k, side, :, place * PAIR : (place + 1) * PAIR] = val

    outs = pl.pallas_call(
        kernel,
        in_specs=[SCALARS] + [ON_CHIP] * 5,
        out_specs=[ON_CHIP] * len(plans),
        out_shape=[jax.ShapeDtypeStruct((n, 2, rows, PAIR * len(p)), BF16) for p in plans],
        cost_estimate=pl.CostEstimate(
            flops=0, transcendentals=0, bytes_accessed=9 * n * tiles * rows * PAIR * 2
        ),
        compiler_params=pltpu.CompilerParams(vmem_limit_bytes=12 << 20),
        name="assemble_attn",
    )(yidx, *pieces)
    return [o.reshape(n * 2 * rows, -1) for o in outs]


def split_attn(mats, plans, count, n, yidx):
    tiles = count + count // 2
    rows = mats[0].shape[0] // (2 * n)
    ins = [m.reshape(n, 2, rows, -1) for m in mats]
    where = {}
    for i, plan in enumerate(plans):
        for place, key in enumerate(plan):
            where[key] = (i, place)

    def kernel(yi, *refs):
        srcs, outs = refs[: len(mats)], refs[len(mats) :]
        low = half_lanes((rows, PAIR))
        for k in range(n):
            for a in range(2):
                side = yi[a]

                def get(mat, j):
                    i, place = where[(mat, j)]
                    return srcs[i][k, side, :, place * PAIR : (place + 1) * PAIR]

                for dx in range(2):
                    for t in range(tiles):
                        if t < count:
                            val = get(t, dx)
                        else:
                            p = t - count
                            t0, t1 = get(2 * p, 2), get(2 * p + 1, 2)
                            if dx == 0:
                                val = jnp.where(low, t0, half_roll(t1))
                            else:
                                val = jnp.where(low, half_roll(t0), t1)
                        outs[dx * 2 + a][k, t] = val

    return pl.pallas_call(
        kernel,
        in_specs=[SCALARS] + [ON_CHIP] * len(ins),
        out_specs=[ON_CHIP] * 4,
        out_shape=[jax.ShapeDtypeStruct((n, tiles, rows, PAIR), BF16)] * 4,
        cost_estimate=pl.CostEstimate(
            flops=0, transcendentals=0, bytes_accessed=8 * n * tiles * rows * PAIR * 2
        ),
        compiler_params=pltpu.CompilerParams(vmem_limit_bytes=12 << 20),
        name="split_attn",
    )(yidx, *ins)


def assemble_ffn(pieces, yidx):
    n, _, rows, cols = pieces[0].shape

    def kernel(yi, *refs):
        ins, outs = refs[:5], refs[5:]
        for k in range(n):
            for a in range(2):
                for h in range(2):
                    for dx in range(2):
                        val = ins[1 + dx * 2 + a][k, h]
                        val = jnp.where(yi[2] == 1, ins[0][k, h], val) if dx + a == 0 else val
                        outs[h][k, yi[a], :, dx * cols : (dx + 1) * cols] = val

    outs = pl.pallas_call(
        kernel,
        in_specs=[SCALARS] + [ON_CHIP] * 5,
        out_specs=[ON_CHIP] * 2,
        out_shape=[jax.ShapeDtypeStruct((n, 2, rows, 2 * cols), BF16)] * 2,
        cost_estimate=pl.CostEstimate(
            flops=0, transcendentals=0, bytes_accessed=2 * 9 * n * rows * cols * 2
        ),
        compiler_params=pltpu.CompilerParams(vmem_limit_bytes=16 << 20),
        name="assemble_ffn",
    )(yidx, *pieces)
    return [o.reshape(n * 2 * rows, 2 * cols) for o in outs]


def split_ffn(mats, n, yidx):
    rows = mats[0].shape[0] // (2 * n)
    cols = mats[0].shape[1] // 2
    ins = [m.reshape(n, 2, rows, 2 * cols) for m in mats]

    def kernel(yi, *refs):
        srcs, outs = refs[:2], refs[2:]
        for k in range(n):
            for a in range(2):
                for h in range(2):
                    for dx in range(2):
                        outs[dx * 2 + a][k, h] = srcs[h][
                            k, yi[a], :, dx * cols : (dx + 1) * cols
                        ]

    return pl.pallas_call(
        kernel,
        in_specs=[SCALARS] + [ON_CHIP] * 2,
        out_specs=[ON_CHIP] * 4,
        out_shape=[jax.ShapeDtypeStruct((n, 2, rows, cols), BF16)] * 4,
        cost_estimate=pl.CostEstimate(
            flops=0, transcendentals=0, bytes_accessed=2 * 8 * n * rows * cols * 2
        ),
        compiler_params=pltpu.CompilerParams(vmem_limit_bytes=16 << 20),
        name="split_ffn",
    )(yidx, *ins)


def assemble_planes(planes, yidx):
    n = planes.shape[0]
    rows, cols = planes.shape[4:]

    def kernel(yi, src, *outs):
        for k in range(n):
            for a in range(2):
                for h in range(2):
                    outs[h][k, yi[a]] = src[k, 0, a, h]

    outs = pl.pallas_call(
        kernel,
        grid_spec=pltpu.PrefetchScalarGridSpec(
            num_scalar_prefetch=1,
            grid=(2,),
            in_specs=[pl.BlockSpec((n, 1, 2, 2, rows, cols), lambda d, yi: (0, d, 0, 0, 0, 0))],
            out_specs=[pl.BlockSpec((n, 2, rows, cols), lambda d, yi: (0, 0, 0, d))] * 2,
        ),
        out_shape=[jax.ShapeDtypeStruct((n, 2, rows, 2 * cols), BF16)] * 2,
        cost_estimate=pl.CostEstimate(
            flops=0, transcendentals=0, bytes_accessed=2 * 8 * n * rows * cols * 2
        ),
        compiler_params=pltpu.CompilerParams(vmem_limit_bytes=24 << 20),
        name="assemble_planes",
    )(yidx, planes)
    return [o.reshape(n * 2 * rows, 2 * cols) for o in outs]


def split_planes(mats, n, yidx):
    rows = mats[0].shape[0] // (2 * n)
    cols = mats[0].shape[1] // 2
    ins = [m.reshape(n, 2, rows, 2 * cols) for m in mats]

    def kernel(yi, *refs):
        for k in range(n):
            for a in range(2):
                for h in range(2):
                    refs[2][k, 0, a, h] = refs[h][k, yi[a]]

    return pl.pallas_call(
        kernel,
        grid_spec=pltpu.PrefetchScalarGridSpec(
            num_scalar_prefetch=1,
            grid=(2,),
            in_specs=[pl.BlockSpec((n, 2, rows, cols), lambda d, yi: (0, 0, 0, d))] * 2,
            out_specs=pl.BlockSpec((n, 1, 2, 2, rows, cols), lambda d, yi: (0, d, 0, 0, 0, 0)),
        ),
        out_shape=jax.ShapeDtypeStruct((n, 2, 2, 2, rows, cols), BF16),
        cost_estimate=pl.CostEstimate(
            flops=0, transcendentals=0, bytes_accessed=2 * 8 * n * rows * cols * 2
        ),
        compiler_params=pltpu.CompilerParams(vmem_limit_bytes=24 << 20),
        name="split_planes",
    )(yidx, *ins)


def bias_tiles(line, blocks):
    heads, _, length = line.shape
    spans = 2 * blocks - 1
    width = 2 * BLOCK

    def kernel(line_ref, out_ref):
        row = lax.broadcasted_iota(jnp.int32, (8, width), 0)
        for d in range(spans):
            start = (spans - 1 - d) * BLOCK
            window = line_ref[0, :, start : start + width]
            turned = jnp.concatenate([window[:, BLOCK:], window[:, :BLOCK]], axis=1)
            tile = jnp.broadcast_to(turned, (8, width))
            for bit in (1, 2, 4):
                tile = jnp.where((row & bit) != 0, pltpu.roll(tile, bit, 1), tile)
            size = 8
            while size < BLOCK:
                tile = jnp.concatenate([tile, pltpu.roll(tile, size, 1)], axis=0)
                size *= 2
            out_ref[0, d] = tile[:, :BLOCK]

    return pl.pallas_call(
        kernel,
        grid=(heads,),
        in_specs=[pl.BlockSpec((1, 1, length), lambda h: (h, 0, 0))],
        out_specs=pl.BlockSpec((1, spans, BLOCK, BLOCK), lambda h: (h, 0, 0, 0)),
        out_shape=jax.ShapeDtypeStruct((heads, spans, BLOCK, BLOCK), F32),
        cost_estimate=pl.CostEstimate(
            flops=heads * spans * BLOCK * BLOCK * 8,
            transcendentals=0,
            bytes_accessed=heads * spans * BLOCK * BLOCK * 4,
        ),
        compiler_params=pltpu.CompilerParams(vmem_limit_bytes=8 << 20),
        name="bias_tiles",
    )(line)


def diagonal_sums(tile):
    width = 2 * BLOCK
    t = jnp.concatenate([tile, jnp.zeros_like(tile)], axis=1)
    size = BLOCK
    while size > 8:
        size //= 2
        t = t[:size] + pltpu.roll(t[size:], width - size, 1)
    row = lax.broadcasted_iota(jnp.int32, (8, width), 0)
    for bit in (1, 2, 4):
        t = jnp.where((row & bit) != 0, pltpu.roll(t, width - bit, 1), t)
    return jnp.sum(t, axis=0, keepdims=True)


def head_keys(keys, limit, a):
    lane = lax.broadcasted_iota(jnp.int32, keys.shape, 1)
    place = lax.broadcasted_iota(jnp.int32, keys.shape, 0)
    mine = (lane // (PAIR // 2)) == a
    flag = jnp.where(place < limit, 0.0, MASK_VALUE)
    other = jnp.where(lane == (1 - a) * (PAIR // 2), flag, 0.0)
    return bf(jnp.where(mine, wide(keys), other))


def head_queries(queries, scale, a, mark):
    lane = lax.broadcasted_iota(jnp.int32, queries.shape, 1)
    mine = (lane // (PAIR // 2)) == a
    other = jnp.where(lane == (1 - a) * (PAIR // 2), mark, 0.0)
    return bf(jnp.where(mine, wide(queries) * scale, other))


def only_head(values, a):
    lane = lax.broadcasted_iota(jnp.int32, values.shape, 1)
    return bf(jnp.where((lane // (PAIR // 2)) == a, wide(values), 0.0))


def score_blocks(key_a, query_a, bias_ref, a, qb, key_blocks, causal):
    out = []
    for kb in range(key_blocks):
        st = dot_nt(key_a[kb * BLOCK : (kb + 1) * BLOCK], query_a)
        if bias_ref is not None:
            st = st + bias_ref[a, kb - qb + key_blocks - 1]
        if causal:
            kpos = lax.broadcasted_iota(jnp.int32, st.shape, 0)
            qpos = lax.broadcasted_iota(jnp.int32, st.shape, 1)
            st = jnp.where(kpos <= qpos, st, MASK_VALUE)
        out.append(st)
    return out


def attention_forward(queries, memory, limit, bias, causal, fused):
    query_len = queries.shape[0]
    key_len = query_len if fused else memory.shape[0]
    pairs = queries.shape[1] // ((3 if fused else 1) * PAIR)
    key_blocks, query_blocks = key_len // BLOCK, query_len // BLOCK
    scale = (PAIR // 2) ** (-0.5)

    def kernel(limit_ref, q_ref, *refs):
        refs = list(refs)
        kv_ref = q_ref if fused else refs.pop(0)
        bias_ref = refs.pop(0) if bias is not None else None
        c_ref, lse_ref = refs
        k0 = PAIR if fused else 0
        keys = kv_ref[:, k0 : k0 + PAIR]
        values = kv_ref[:, k0 + PAIR : k0 + 2 * PAIR]
        key_a = [head_keys(keys, limit_ref[0], a) for a in range(2)]

        def visit(qb):
            rows = pl.ds(pl.multiple_of(qb * BLOCK, BLOCK), BLOCK)
            q = q_ref[rows, 0:PAIR]
            parts = []
            for a in range(2):
                st = score_blocks(
                    key_a[a], head_queries(q, scale, a, 1.0), bias_ref, a, qb, key_blocks, causal
                )
                top = functools.reduce(
                    jnp.maximum, [jnp.max(b, axis=0, keepdims=True) for b in st]
                )
                ex = [jnp.exp(b - top) for b in st]
                total = sum(jnp.sum(b, axis=0, keepdims=True) for b in ex)
                ct = sum(
                    dot_tn(values[kb * BLOCK : (kb + 1) * BLOCK], bf(ex[kb]))
                    for kb in range(key_blocks)
                )
                parts.append(ct[a * (PAIR // 2) : (a + 1) * (PAIR // 2)] * (1.0 / total))
                lse_ref[0, a : a + 1, rows] = top + jnp.log(total)
            c_ref[rows, :] = bf(jnp.transpose(jnp.concatenate(parts, axis=0)))

        if query_blocks == 1:
            visit(0)
        else:
            pl.loop(0, query_blocks)(visit)

    in_specs = [pl.BlockSpec((query_len, (3 if fused else 1) * PAIR), lambda j, n: (0, j))]
    args = [queries]
    if not fused:
        in_specs.append(pl.BlockSpec((key_len, 2 * PAIR), lambda j, n: (0, j)))
        args.append(memory)
    if bias is not None:
        in_specs.append(pl.BlockSpec((2,) + bias.shape[1:], lambda j, n: (j, 0, 0, 0)))
        args.append(pltpu.with_memory_space_constraint(bias, pltpu.HBM))
    return pl.pallas_call(
        kernel,
        grid_spec=pltpu.PrefetchScalarGridSpec(
            num_scalar_prefetch=1,
            grid=(pairs,),
            in_specs=in_specs,
            out_specs=[
                pl.BlockSpec((query_len, PAIR), lambda j, n: (0, j)),
                pl.BlockSpec((1, 8, query_len), lambda j, n: (j, 0, 0)),
            ],
        ),
        out_shape=[
            jax.ShapeDtypeStruct((query_len, pairs * PAIR), BF16),
            jax.ShapeDtypeStruct((pairs, 8, query_len), F32),
        ],
        compiler_params=pltpu.CompilerParams(vmem_limit_bytes=26 << 20),
        cost_estimate=pl.CostEstimate(
            flops=pairs * 2 * query_len * key_len * PAIR * 4,
            transcendentals=pairs * 2 * query_len * key_len,
            bytes_accessed=pairs * PAIR * 2 * 2 * (query_len + key_len),
        ),
        name="attend_" + ("enc" if bias is not None else "dec" if fused else "cross"),
    )(limit, *args)


def attention_backward(queries, memory, limit, bias, causal, fused, context, lse, context_grad):
    query_len = queries.shape[0]
    key_len = query_len if fused else memory.shape[0]
    pairs = queries.shape[1] // ((3 if fused else 1) * PAIR)
    key_blocks, query_blocks = key_len // BLOCK, query_len // BLOCK
    spans = 2 * key_blocks - 1
    scale = (PAIR // 2) ** (-0.5)

    def kernel(limit_ref, q_ref, *refs):
        refs = list(refs)
        kv_ref = q_ref if fused else refs.pop(0)
        bias_ref = refs.pop(0) if bias is not None else None
        c_ref, lse_ref, dc_ref = refs[:3]
        refs = refs[3:]
        dq_ref = refs.pop(0)
        dkv_ref = dq_ref if fused else refs.pop(0)
        dq_sum = refs.pop(0)
        dkv_sum = dq_sum if fused else refs.pop(0)
        diag_ref = refs.pop(0) if bias is not None else None
        dk_acc, dv_acc = refs[:2]
        tile_acc = refs[2] if bias is not None else None
        k0 = PAIR if fused else 0
        keys = kv_ref[:, k0 : k0 + PAIR]
        values = kv_ref[:, k0 + PAIR : k0 + 2 * PAIR]
        key_a = [head_keys(keys, limit_ref[0], a) for a in range(2)]
        pure_key_a = [only_head(keys, a) for a in range(2)]
        value_a = [only_head(values, a) for a in range(2)]
        dq_sum[...] = jnp.zeros_like(dq_sum)
        dk_acc[...] = jnp.zeros_like(dk_acc)
        dv_acc[...] = jnp.zeros_like(dv_acc)
        if bias is not None:
            tile_acc[...] = jnp.zeros_like(tile_acc)

        def visit(qb):
            rows = pl.ds(pl.multiple_of(qb * BLOCK, BLOCK), BLOCK)
            q = q_ref[rows, 0:PAIR]
            dc = dc_ref[rows, :]
            both = jnp.transpose(wide(dc) * wide(c_ref[rows, :]))
            dqt = jnp.zeros((PAIR, BLOCK), F32)
            for a in range(2):
                st = score_blocks(
                    key_a[a], head_queries(q, scale, a, 1.0), bias_ref, a, qb, key_blocks, causal
                )
                delta = jnp.sum(
                    both[a * (PAIR // 2) : (a + 1) * (PAIR // 2)], axis=0, keepdims=True
                )
                log_row = lse_ref[0, a : a + 1, rows]
                dc_a = only_head(dc, a)
                q_a = head_queries(q, scale, a, 0.0)
                for kb in range(key_blocks):
                    span = slice(kb * BLOCK, (kb + 1) * BLOCK)
                    p = jnp.exp(st[kb] - log_row)
                    dp = dot_nt(value_a[a][span], dc)
                    ds = p * (dp - delta)
                    dsb = bf(ds)
                    dv_acc[span, :] += dot_nn(bf(p), dc_a)
                    dk_acc[span, :] += dot_nn(dsb, q_a)
                    dqt = dqt + dot_tn(pure_key_a[a][span], dsb)
                    if bias is not None:
                        tile_acc[a, kb - qb + key_blocks - 1] += ds
            dq = bf(jnp.transpose(dqt) * scale)
            dq_ref[rows, 0:PAIR] = dq
            dq_sum[0:1, 0:PAIR] += jnp.sum(wide(dq), axis=0, keepdims=True)

        if query_blocks == 1:
            visit(0)
        else:
            pl.loop(0, query_blocks)(visit)
        dkv_ref[:, k0 : k0 + PAIR] = bf(dk_acc[...])
        dv = bf(dv_acc[...])
        dkv_ref[:, k0 + PAIR : k0 + 2 * PAIR] = dv
        dkv_sum[0:1, k0 + PAIR : k0 + 2 * PAIR] = jnp.sum(wide(dv), axis=0, keepdims=True)
        if bias is not None:
            for a in range(2):
                for d in range(spans):
                    diag_ref[a, d : d + 1, :] = diagonal_sums(tile_acc[a, d])

    in_specs = [pl.BlockSpec((query_len, (3 if fused else 1) * PAIR), lambda j, n: (0, j))]
    args = [queries]
    if not fused:
        in_specs.append(pl.BlockSpec((key_len, 2 * PAIR), lambda j, n: (0, j)))
        args.append(memory)
    if bias is not None:
        in_specs.append(pl.BlockSpec((2,) + bias.shape[1:], lambda j, n: (j, 0, 0, 0)))
        args.append(pltpu.with_memory_space_constraint(bias, pltpu.HBM))
    in_specs += [
        pl.BlockSpec((query_len, PAIR), lambda j, n: (0, j)),
        pl.BlockSpec((1, 8, query_len), lambda j, n: (j, 0, 0)),
        pl.BlockSpec((query_len, PAIR), lambda j, n: (0, j)),
    ]
    args += [context, lse, context_grad]
    out_specs = [pl.BlockSpec((query_len, (3 if fused else 1) * PAIR), lambda j, n: (0, j))]
    out_shape = [jax.ShapeDtypeStruct(queries.shape, BF16)]
    scratch = [pltpu.VMEM((key_len, PAIR), F32)] * 2
    if not fused:
        out_specs.append(pl.BlockSpec((key_len, 2 * PAIR), lambda j, n: (0, j)))
        out_shape.append(jax.ShapeDtypeStruct(memory.shape, BF16))
    for array, tiles in ((queries, 3 if fused else 1), (memory, 2)):
        if array is not None:
            out_specs.append(pl.BlockSpec((8, tiles * PAIR), lambda j, n: (0, j)))
            out_shape.append(jax.ShapeDtypeStruct((8, array.shape[1]), F32))
    if bias is not None:
        out_specs.append(pl.BlockSpec((2, 8, 2 * BLOCK), lambda j, n: (j, 0, 0)))
        out_shape.append(jax.ShapeDtypeStruct((2 * pairs, 8, 2 * BLOCK), F32))
        scratch.append(pltpu.VMEM((2, spans, BLOCK, BLOCK), F32))
    return pl.pallas_call(
        kernel,
        grid_spec=pltpu.PrefetchScalarGridSpec(
            num_scalar_prefetch=1,
            grid=(pairs,),
            in_specs=in_specs,
            out_specs=out_specs,
            scratch_shapes=scratch,
        ),
        out_shape=out_shape,
        compiler_params=pltpu.CompilerParams(vmem_limit_bytes=26 << 20),
        cost_estimate=pl.CostEstimate(
            flops=pairs * 2 * query_len * key_len * PAIR * 10,
            transcendentals=pairs * 2 * query_len * key_len,
            bytes_accessed=pairs * PAIR * 2 * 4 * (query_len + key_len),
        ),
        name="attend_back_" + ("enc" if bias is not None else "dec" if fused else "cross"),
    )(limit, *args)


def gelu(z):
    return z * (0.5 * (1.0 + lax.erf(z * ROOT_HALF)))


def gelu_slope(z):
    return 0.5 * (1.0 + lax.erf(z * ROOT_HALF)) + z * jnp.exp(-0.5 * z * z) * INV_ROOT_TAU


ROWS = 128


def row_steps(count, body):
    @pl.loop(0, count // ROWS)
    def _(step):
        body(pl.ds(pl.multiple_of(step * ROWS, ROWS), ROWS), step)


def add_norm(residual, own_part, other_part, vecs, bias, gain, shift):
    source, affine = residual if isinstance(residual, tuple) else (residual, None)
    count, width = source.shape

    def kernel(x_ref, p_ref, q_ref, v_ref, low_ref, normed_ref, inv_ref):
        def body(rows, step):
            base = wide(x_ref[rows])
            if affine is not None:
                base = base * v_ref[affine[0] : affine[0] + 1] + v_ref[affine[1] : affine[1] + 1]
            values = base + (wide(p_ref[rows]) + wide(q_ref[rows])) + v_ref[bias : bias + 1]
            center = values - jnp.sum(values, axis=-1, keepdims=True) * (1.0 / width)
            square = jnp.sum(center * center, axis=-1, keepdims=True)
            inv = lax.rsqrt(square * (1.0 / width) + EPSILON)
            normed = center * inv
            low_ref[rows] = bf(normed * v_ref[gain : gain + 1] + v_ref[shift : shift + 1])
            normed_ref[rows] = normed
            inv_ref[rows] = jnp.broadcast_to(inv, (ROWS, PAIR))

        row_steps(count, body)

    return pl.pallas_call(
        kernel,
        in_specs=[ON_CHIP] * 4,
        out_specs=[ON_CHIP] * 3,
        out_shape=[
            jax.ShapeDtypeStruct((count, width), BF16),
            jax.ShapeDtypeStruct((count, width), F32),
            jax.ShapeDtypeStruct((count, PAIR), F32),
        ],
        cost_estimate=pl.CostEstimate(
            flops=12 * count * width, transcendentals=count, bytes_accessed=14 * count * width
        ),
        compiler_params=pltpu.CompilerParams(vmem_limit_bytes=14 << 20),
        name="add_norm",
    )(source, own_part, other_part, vecs)


def norm_back(terms, limit, normed, inv, vecs, gain):
    count, width = normed.shape
    use = limit is not None

    def kernel(*refs):
        refs = list(refs)
        limit_ref = refs.pop(0) if use else None
        ins, (n_ref, inv_ref, v_ref, grad_ref, low_ref, sum_ref) = refs[:-6], refs[-6:]
        sum_ref[...] = jnp.zeros_like(sum_ref)

        def body(rows, step):
            up = wide(ins[0][rows])
            if use:
                place = step * ROWS + lax.broadcasted_iota(jnp.int32, up.shape, 0)
                up = jnp.where(place < limit_ref[0], up, 0.0)
            rest = [wide(r[rows]) for r in ins[1:]]
            if rest:
                up = up + (rest[0] + rest[1])
            values = n_ref[rows]
            scaled = up * v_ref[gain : gain + 1]
            mean = jnp.sum(scaled, axis=-1, keepdims=True) * (1.0 / width)
            along = jnp.sum(scaled * values, axis=-1, keepdims=True) * (1.0 / width)
            grad = inv_ref[rows, :1] * (scaled - mean - values * along)
            grad_ref[rows] = grad
            low_ref[rows] = bf(grad)
            sum_ref[0:1] += jnp.sum(up * values, axis=0, keepdims=True)
            sum_ref[1:2] += jnp.sum(up, axis=0, keepdims=True)
            sum_ref[2:3] += jnp.sum(grad, axis=0, keepdims=True)

        row_steps(count, body)

    smem = [pl.BlockSpec(memory_space=pltpu.SMEM)] if use else []
    return pl.pallas_call(
        kernel,
        in_specs=smem + [ON_CHIP] * (len(terms) + 3),
        out_specs=[ON_CHIP] * 3,
        out_shape=[
            jax.ShapeDtypeStruct((count, width), F32),
            jax.ShapeDtypeStruct((count, width), BF16),
            jax.ShapeDtypeStruct((8, width), F32),
        ],
        cost_estimate=pl.CostEstimate(
            flops=16 * count * width, transcendentals=0, bytes_accessed=20 * count * width
        ),
        compiler_params=pltpu.CompilerParams(vmem_limit_bytes=18 << 20),
        name="norm_back",
    )(*([limit] if use else []), *terms, normed, inv, vecs)


NORM_ROWS = 15


def pack_small(norm_sums, enc_sum, dec_sum, query_sum, memory_sum, unit_sums, diag, buckets):
    width = norm_sums[0].shape[1]
    heads, _, span = diag.shape
    spans = 2 * (span // BLOCK) + 1
    length = (spans + 1) * BLOCK

    def kernel(*refs):
        one, two, d_one, d_two, d_three = refs[:5]
        enc_ref, dec_ref, query_ref, memory_ref, unit_ref, dec_unit_ref, diag_ref = refs[5:12]
        outs, line = refs[12:14], refs[14]
        norms = [(one, 0), (one, 1), (two, 0), (two, 1), (one, 2), (two, 2)]
        norms += [(r, i) for r in (d_one, d_two, d_three) for i in range(2)]
        norms += [(r, 2) for r in (d_one, d_two, d_three)]
        tiles = [(enc_ref, 3, 0), (enc_ref, 3, 2), (dec_ref, 3, 0)]
        tiles += [(dec_ref, 3, 2), (query_ref, 1, 0), (memory_ref, 2, 1)]
        line[...] = jnp.zeros_like(line)
        for h in range(heads):
            for d in range(spans):
                row = diag_ref[h, d : d + 1, :]
                start = (spans - 1 - d) * BLOCK
                line[h : h + 1, start : start + BLOCK] += row[:, BLOCK:]
                line[h : h + 1, start + BLOCK : start + 2 * BLOCK] += row[:, :BLOCK]
        wide_table = -(-buckets // PAIR) * PAIR
        dist = length // 2 - lax.broadcasted_iota(jnp.int32, (length, wide_table), 0)
        bucket = jnp.clip(dist, -(buckets // 2), buckets // 2 - 1) + buckets // 2
        hot = jnp.where(
            bucket == lax.broadcasted_iota(jnp.int32, (length, wide_table), 1), 1.0, 0.0
        )
        table = jnp.dot(
            line[...], hot, precision=lax.Precision.HIGHEST, preferred_element_type=F32
        )
        for dx, out in enumerate(outs):
            out[...] = jnp.zeros_like(out)
            for i, (ref, r) in enumerate(norms):
                out[i : i + 1, :] = ref[r : r + 1, :]
            for i, (ref, stride, at) in enumerate(tiles):
                row, lane = NORM_ROWS + i // 3, (i % 3) * 2 * PAIR
                part = [ref[0:1, (j * stride + at) * PAIR : (j * stride + at + 1) * PAIR] for j in range(3)]
                out[row : row + 1, lane : lane + PAIR] = part[dx]
                both = jnp.broadcast_to(part[2], (8, PAIR))
                both = pltpu.roll(both, PAIR // 2, 1) if dx else both
                out[row : row + 1, lane + PAIR : lane + 2 * PAIR] = both[0:1]
            for i, ref in enumerate((unit_ref, dec_unit_ref)):
                out[NORM_ROWS + 2 + i : NORM_ROWS + 3 + i, :] = ref[0:1, dx * width : (dx + 1) * width]
            for i, h in enumerate(((0, 1, 4), (2, 3, 5))[dx]):
                out[NORM_ROWS + 4 + i : NORM_ROWS + 5 + i, 0:wide_table] = table[h : h + 1]

    return pl.pallas_call(
        kernel,
        out_shape=[jax.ShapeDtypeStruct((24, width), F32)] * 2,
        scratch_shapes=[pltpu.VMEM((8, length), F32)],
        compiler_params=pltpu.CompilerParams(vmem_limit_bytes=12 << 20),
        name="pack_small",
    )(*norm_sums, enc_sum, dec_sum, query_sum, memory_sum, *unit_sums, diag)


def update_matrices(sums, alternative, own, state, rate, inverse, packed):
    master = state[0]
    count, rows, cols = master.shape
    step = 2 if packed else 1
    arrays = list(sums) + ([alternative] if alternative is not None else [])

    def kernel(own_ref, inv_ref, *refs):
        if packed:
            groups = [refs[2 * i : 2 * i + 2] for i in range(len(arrays))]
            refs = refs[2 * len(arrays) :]
        else:
            groups = [refs[i : i + 1] for i in range(len(arrays))]
            refs = refs[len(arrays) :]
        state_refs, outs = refs[:3], refs[3:]
        inv = inv_ref[0]

        def total(part, i):
            vals = [wide(g[part][i]) for g in groups]
            if alternative is not None:
                vals = [jnp.where(own_ref[0] == 1, vals[-1], vals[0])] + vals[1:-1]
            return functools.reduce(jnp.add, vals)

        def advance(grad, i, span):
            mean_grad = grad * inv
            new_moment = MOMENTUM * state_refs[1][i, :, span] + mean_grad
            new_master = state_refs[0][i, :, span] - rate * (mean_grad + MOMENTUM * new_moment)
            outs[0][i, :, span] = mean_grad
            outs[1][i, :, span] = new_master
            outs[2][i, :, span] = new_moment
            outs[3][i, :, span] = (
                AVERAGING * state_refs[2][i, :, span] + (1.0 - AVERAGING) * new_master
            )
            outs[4][i, :, span] = bf(new_master)

        if packed:
            rest = total(1, 0)
            turned = pltpu.roll(rest, PAIR // 2, 1)
            for i in range(2):
                advance(total(0, i), i, slice(0, PAIR))
                advance((turned if i else rest)[:, : PAIR // 2], i, slice(PAIR, cols))
        else:
            advance(total(0, 0), 0, slice(0, cols))

    in_specs, args = [], []
    for a in arrays:
        in_specs.append(pl.BlockSpec((step, rows, a.shape[2]), lambda k, o: (k, 0, 0)))
        args.append(a)
        if packed:
            in_specs.append(pl.BlockSpec((1, rows, PAIR), lambda k, o: (count + k, 0, 0)))
            args.append(a)
    spec = pl.BlockSpec((step, rows, cols), lambda k, o: (k, 0, 0))
    return pl.pallas_call(
        kernel,
        grid_spec=pltpu.PrefetchScalarGridSpec(
            num_scalar_prefetch=1,
            grid=(count // step,),
            in_specs=[pl.BlockSpec(memory_space=pltpu.SMEM)] + in_specs + [spec] * 3,
            out_specs=[spec] * 5,
        ),
        out_shape=[jax.ShapeDtypeStruct(master.shape, F32)] * 4
        + [jax.ShapeDtypeStruct(master.shape, BF16)],
        cost_estimate=pl.CostEstimate(
            flops=12 * master.size, transcendentals=0, bytes_accessed=44 * master.size
        ),
        compiler_params=pltpu.CompilerParams(vmem_limit_bytes=8 << 20),
        name="update_matrices",
    )(own, inverse, *args, *state)


def place_quarters(parts, index, cuts):
    count, outputs = len(parts), len(cuts)
    starts = [sum(cuts[:i]) for i in range(outputs)]

    def kernel(idx, *refs):
        outs, sem = refs[count : count + outputs], refs[-1]
        copies = [
            pltpu.make_async_copy(
                refs[k].at[starts[i] : starts[i] + cuts[i]], outs[i].at[idx[k]], sem.at[k, i]
            )
            for k in range(count)
            for i in range(outputs)
        ]
        for copy in copies:
            copy.start()
        for copy in copies:
            copy.wait()

    return pl.pallas_call(
        kernel,
        in_specs=[SCALARS] + [ON_CHIP] * count,
        out_specs=[pl.BlockSpec(memory_space=pl.ANY)] * outputs,
        out_shape=[
            jax.ShapeDtypeStruct((count, c) + parts[0].shape[1:], parts[0].dtype) for c in cuts
        ],
        scratch_shapes=[pltpu.SemaphoreType.DMA((count, outputs))],
        cost_estimate=pl.CostEstimate(
            flops=0, transcendentals=0, bytes_accessed=4 * count * parts[0].size
        ),
        compiler_params=pltpu.CompilerParams(vmem_limit_bytes=8 << 20),
        name="place_quarters",
    )(index, *parts)


def update(master, moment, average, gradient, rate, frame_total):
    mean_grad = gradient / frame_total
    new_moment = MOMENTUM * moment + mean_grad
    new_master = master - rate * (mean_grad + MOMENTUM * new_moment)
    new_average = AVERAGING * average + (1.0 - AVERAGING) * new_master
    return mean_grad, new_master, new_moment, new_average


def order_cols(v0, v1):
    return jnp.concatenate(
        [v0[..., :PAIR], v1[..., :PAIR], v0[..., PAIR:], v1[..., PAIR:]], axis=-1
    )


CROSS_PLANS = [
    [(0, j) for j in range(3)],
    [(m, j) for j in range(3) for m in (1, 2)],
    [(3, j) for j in range(3)],
]
QKV_PLAN = [(m, j) for j in range(3) for m in range(3)]
ENC_PLANS = [QKV_PLAN, [(3, j) for j in range(3)]]

def local(
    frames,
    cotangent,
    lengths,
    attn_master,
    attn_moment,
    attn_average,
    ffn_master,
    ffn_moment,
    ffn_average,
    norm_vecs,
    norm_moment,
    norm_average,
    col_bias,
    col_moment,
    col_average,
    rel_table,
    rel_moment,
    rel_average,
    dec_frames,
    dec_cotangent,
    text_lengths,
    dec_attn_master,
    dec_attn_moment,
    dec_attn_average,
    dec_ffn_master,
    dec_ffn_moment,
    dec_ffn_average,
    dec_norm_vecs,
    dec_norm_moment,
    dec_norm_average,
    dec_col_bias,
    dec_col_moment,
    dec_col_average,
):
    n_dp = lax.axis_size("dp")
    z, s, m = lax.axis_index("dp"), lax.axis_index("seq"), lax.axis_index("mp")
    y = m // 2
    utt_count, half_len, width = frames.shape
    text_half = dec_frames.shape[1]
    full_len, text_full = 2 * half_len, 2 * text_half
    own = s == y
    yidx = jnp.stack([y, 1 - y, own.astype(jnp.int32)]).astype(jnp.int32)
    root_frames = float(utt_count * full_len * n_dp) ** 0.5

    mine = jnp.concatenate(
        [
            lax.dynamic_index_in_dim(parts, m, 0, keepdims=False)
            for parts in (frames, cotangent, dec_frames, dec_cotangent)
        ]
    )
    other = swap_core(mine)
    dffn_shard = bf(dec_ffn_master)
    dffn_parts = gather_plane(dffn_shard)
    attn_z = gather_dp(pack_attn(bf(attn_master)))
    packed = jnp.concatenate([col_bias, dec_col_bias, rel_table.T.reshape(-1)])
    groups = [jnp.where(own, packed, spread(packed, 0, 0)), spread(packed, 1, 0)]
    ffn_z = gather_dp(after(bf(ffn_master), attn_z))
    mine, other, dffn_parts, attn_z, groups, dattn_low, lengths = stage(
        mine, other, dffn_parts, attn_z, groups, dec_attn_master, lengths
    )
    dattn_low = bf(dattn_low)
    attn_pieces = gather_plane(attn_z)

    bucket_count, group_heads = rel_table.shape
    group_width = attn_master.shape[2]
    unit_count = ffn_master.shape[2]
    enc_cols, dec_cols = col_bias.shape[0], dec_col_bias.shape[0]

    def cols_at(start):
        return order_cols(*[g[start : start + group_width] for g in groups])

    def units_at(start):
        return jnp.concatenate([g[start : start + unit_count] for g in groups])

    def qkv_bias(q, v):
        blank = jnp.zeros((PAIR,), F32)
        cut = [slice(j * PAIR, (j + 1) * PAIR) for j in range(3)]
        return jnp.concatenate([part for c in cut for part in (q[c], blank, v[c])])

    bias_qkv = qkv_bias(cols_at(0), cols_at(group_width))
    bias_one = units_at(2 * group_width)
    bias_dqkv = qkv_bias(cols_at(enc_cols), cols_at(enc_cols + group_width))
    bias_cq = cols_at(enc_cols + 2 * group_width)
    cv = cols_at(enc_cols + 3 * group_width)
    blank = jnp.zeros((PAIR,), F32)
    bias_ckv = jnp.concatenate(
        [part for j in range(3) for part in (blank, cv[j * PAIR : (j + 1) * PAIR])]
    )
    bias_done = units_at(enc_cols + 4 * group_width)
    tables = [
        g[enc_cols + dec_cols :].reshape(group_heads, bucket_count) for g in groups
    ]
    heads = jnp.stack(
        [tables[0][0], tables[0][1], tables[1][0], tables[1][1], tables[0][2], tables[1][2]]
    )
    max_dist = bucket_count // 2
    blocks = full_len // BLOCK
    lead = blocks * BLOCK - max_dist + 1
    tail = blocks * BLOCK - max_dist - 1
    line = jnp.pad(heads[:, ::-1], ((0, 0), (lead, tail)), mode="edge")
    bias = bias_tiles(line[:, None, :], blocks)

    def all_rows(start, count):
        ours, theirs = mine[start : start + count], other[start : start + count]
        return jnp.concatenate([jnp.where(s == 0, ours, theirs), jnp.where(s == 0, theirs, ours)])

    inputs = all_rows(0, half_len)
    upstream_in = all_rows(half_len, half_len)
    text_in = all_rows(2 * half_len, text_half)
    text_upstream = all_rows(2 * half_len + text_half, text_half)
    limit = lax.dynamic_slice_in_dim(lengths, m, 1)
    text_limit = lax.dynamic_slice_in_dim(text_lengths, m, 1)
    own_flag = own.astype(jnp.int32).reshape(1)

    def my_half(rows):
        count = rows.shape[0] // 2
        return lax.dynamic_slice_in_dim(rows, s * count, count, 0)

    def to_owners(mine):
        return [mine] + [swap_mp(mine, bits) for bits in range(1, 4)]

    owners = m ^ jnp.arange(4, dtype=jnp.int32)

    frame_count = jnp.sum(lengths)
    digit_row = lax.broadcasted_iota(jnp.int32, (1,) + dec_attn_master.shape[1:2] + (PAIR,), 1)
    digits = bf(jnp.where(digit_row == 0, frame_count // 256, frame_count % 256))

    attn_pieces, ffn_z, bias, bias_qkv, inputs, dattn_shard, dffn_plane = stage(
        attn_pieces,
        ffn_z,
        bias,
        bias_qkv,
        inputs,
        jnp.concatenate(
            [pack_attn(dattn_low[:4]), pack_attn(dattn_low[4:]), digits]
        ),
        jnp.stack([jnp.where(own, dffn_parts[0], dffn_parts[1]), *dffn_parts[2:]]),
    )
    ffn_pieces = gather_plane(ffn_z)
    dattn_z = gather_dp(dattn_shard)
    w_qkv, w_o = assemble_attn(attn_pieces, ENC_PLANS, 4, yidx)
    qkv = bf(dot_nn(inputs, w_qkv) + bias_qkv)
    context, lse = attention_forward(qkv, None, limit, bias, False, True)
    part = bf(dot_nt(context, w_o))
    ffn_pieces, dattn_z, part, dffn_plane = stage(ffn_pieces, dattn_z, part, dffn_plane)
    tiles = dattn_z.shape[1] // 2
    frame_total = jnp.sum(wide(dattn_z[:, -1, 0, 0]) * 256.0 + wide(dattn_z[:, -1, 1, 0]))
    cross_z = dattn_z[:, tiles : 2 * tiles]
    self_pieces = gather_plane(dattn_z[:, :tiles])
    dffn_planes = gather_dp(dffn_plane.reshape((2, 2) + dffn_shard.shape))
    hidden_low, normed_one, inv_one = add_norm(
        inputs, part, swap_core(part), norm_vecs, 4, 0, 1
    )
    w_one, w_two = assemble_ffn(ffn_pieces, yidx)
    gate_in = dot_nn(hidden_low, w_one) + bias_one
    activated, slope = bf(gelu(gate_in)), bf(gelu_slope(gate_in))
    part = bf(dot_nt(activated, w_two))
    self_pieces, cross_z, part, activated, slope, frame_total = stage(
        self_pieces, cross_z, part, activated, slope, frame_total
    )
    inverse = (1.0 / frame_total).reshape(1)
    cross_pieces = gather_plane(cross_z)
    enc_low, normed_two, inv_two = add_norm(
        (normed_one, (0, 1)), part, swap_core(part), norm_vecs, 5, 2, 3
    )

    d_qkv, d_o = assemble_attn(self_pieces, ENC_PLANS, 4, yidx)
    dqkv = bf(dot_nn(text_in, d_qkv) + bias_dqkv)
    self_context, self_lse = attention_forward(dqkv, None, text_limit, None, True, True)
    part, cross_pieces = stage(bf(dot_nt(self_context, d_o)), cross_pieces)
    c_q, c_kv, c_o = assemble_attn(cross_pieces, CROSS_PLANS, 4, yidx)
    dw_one, dw_two = assemble_planes(dffn_planes, yidx)
    dec_one_low, normed_d1, inv_d1 = add_norm(
        text_in, part, swap_core(part), dec_norm_vecs, 6, 0, 1
    )
    cross_q = bf(dot_nn(dec_one_low, c_q) + bias_cq)
    cross_kv = bf(dot_nn(enc_low, c_kv) + bias_ckv)
    cross_context, cross_lse = attention_forward(cross_q, cross_kv, limit, None, False, False)
    part = bf(dot_nt(cross_context, c_o))
    dec_two_low, normed_d2, inv_d2 = add_norm(
        (normed_d1, (0, 1)), part, swap_core(part), dec_norm_vecs, 7, 2, 3
    )
    dec_gate = dot_nn(dec_two_low, dw_one) + bias_done
    dec_act, dec_slope = bf(gelu(dec_gate)), bf(gelu_slope(dec_gate))
    part, dec_act, dec_slope = stage(bf(dot_nt(dec_act, dw_two)), dec_act, dec_slope)
    dec_low, normed_d3, inv_d3 = add_norm(
        (normed_d2, (2, 3)), part, swap_core(part), dec_norm_vecs, 8, 4, 5
    )
    grad_d3, dec_ffn_back, sums_d3 = norm_back(
        [text_upstream], text_limit, normed_d3, inv_d3, dec_norm_vecs, 4
    )
    dec_gate_grad = bf(dot_nn(dec_ffn_back, dw_two) * wide(dec_slope))
    dec_gate_sum = jnp.sum(dec_gate_grad, axis=0, dtype=F32)[None]
    part = bf(dot_nt(dec_gate_grad, dw_one))
    dec_ffn_grads = [
        bf(dot_tn(dec_two_low, dec_gate_grad)),
        bf(dot_tn(dec_ffn_back, dec_act)),
    ]
    dec_ffn_planes, part, sent = stage(
        split_planes(dec_ffn_grads, n_dp, yidx),
        part,
        jnp.concatenate([my_half(enc_low), my_half(dec_low)]),
    )
    dec_ffn_plane = scatter_dp(dec_ffn_planes)
    held = to_owners(sent)

    grad_d2, cross_back, sums_d2 = norm_back(
        [grad_d3, part, swap_core(part)], None, normed_d2, inv_d2, dec_norm_vecs, 2
    )
    cross_qg, cross_kvg, query_sum, memory_sum = attention_backward(
        cross_q,
        cross_kv,
        limit,
        None,
        False,
        False,
        cross_context,
        cross_lse,
        bf(dot_nn(cross_back, c_o)),
    )
    cross_grads = [
        bf(dot_tn(dec_one_low, cross_qg)),
        bf(dot_tn(enc_low, cross_kvg)),
        bf(dot_tn(cross_back, cross_context)),
    ]
    query_part, memory_part, cross_parts, held = stage(
        bf(dot_nt(cross_qg, c_q)),
        bf(dot_nt(cross_kvg, c_kv)),
        split_attn(cross_grads, CROSS_PLANS, 4, n_dp, yidx),
        held,
    )
    cross_plane_back = scatter_plane(cross_parts)
    memory_other = swap_core(memory_part)
    grad_d1, self_back, sums_d1 = norm_back(
        [grad_d2, query_part, swap_core(query_part)], None, normed_d1, inv_d1, dec_norm_vecs, 0
    )
    self_g, dec_sum = attention_backward(
        dqkv,
        None,
        text_limit,
        None,
        True,
        True,
        self_context,
        self_lse,
        bf(dot_nn(self_back, d_o)),
    )
    text_part = bf(dot_nt(self_g, d_qkv))
    self_grads = [bf(dot_tn(text_in, self_g)), bf(dot_tn(self_back, self_context))]
    self_parts = split_attn(self_grads, ENC_PLANS, 4, n_dp, yidx)

    grad_two, ffn_back, sums_two = norm_back(
        [upstream_in, memory_part, memory_other], limit, normed_two, inv_two, norm_vecs, 2
    )
    gate_grad = bf(dot_nn(ffn_back, w_two) * wide(slope))
    gate_sum = jnp.sum(gate_grad, axis=0, dtype=F32)[None]
    self_parts, gate_grad, ffn_back, cross_parts, cross_plane_back, text_part = stage(
        self_parts, gate_grad, ffn_back, cross_parts, cross_plane_back, text_part
    )
    self_plane_back = scatter_plane(self_parts)
    text_other = swap_core(text_part)
    cross_total = scatter_dp(sum_plane(cross_parts, cross_plane_back, own))
    ffn_grads = [bf(dot_tn(hidden_low, gate_grad)), bf(dot_tn(ffn_back, activated))]
    part, self_parts, self_plane_back, ffn_parts, text_other = stage(
        bf(dot_nt(gate_grad, w_one)),
        self_parts,
        self_plane_back,
        split_ffn(ffn_grads, n_dp, yidx),
        text_other,
    )
    text_grad = my_half(grad_d1) + (wide(my_half(text_part)) + wide(my_half(text_other)))
    self_total = scatter_dp(sum_plane(self_parts, self_plane_back, own))
    ffn_plane_back = scatter_plane(ffn_parts)
    grad_one, attn_back, sums_one = norm_back(
        [grad_two, part, swap_core(part)], None, normed_one, inv_one, norm_vecs, 0
    )
    enc_g, enc_sum, diag = attention_backward(
        qkv, None, limit, bias, False, True, context, lse, bf(dot_nn(attn_back, w_o))
    )
    ffn_parts, ffn_plane_back, part, enc_g, diag, text_low, dec_ffn_plane = stage(
        ffn_parts,
        ffn_plane_back,
        bf(dot_nt(enc_g, w_qkv)),
        enc_g,
        diag,
        bf(text_grad),
        dec_ffn_plane,
    )
    ffn_total = scatter_dp(sum_plane(ffn_parts, ffn_plane_back, own))
    plane_parts = [dec_ffn_plane[dx, a] for dx, a in ROUTES]
    dec_ffn_sums = scatter_plane(plane_parts)
    out_text_grad = to_owners(text_low)
    input_grad = my_half(grad_one) + (wide(my_half(part)) + wide(my_half(swap_core(part))))
    attn_grads = [bf(dot_tn(inputs, enc_g)), bf(dot_tn(attn_back, context))]
    attn_parts = split_attn(attn_grads, ENC_PLANS, 4, n_dp, yidx)
    vectors = pack_small(
        [sums_one, sums_two, sums_d1, sums_d2, sums_d3],
        enc_sum,
        dec_sum,
        query_sum,
        memory_sum,
        [gate_sum, dec_gate_sum],
        diag,
        bucket_count,
    )
    attn_parts, input_grad, vectors, out_text_grad, dec_ffn_sums, held = stage(
        attn_parts, input_grad, vectors, out_text_grad, dec_ffn_sums, held
    )
    (out_text_grad,) = place_quarters(out_text_grad, owners, [text_half])
    out_enc, out_dec = place_quarters(held, owners, [half_len, text_half])
    attn_plane_back = scatter_plane(attn_parts)
    small = vectors[0] + swap_mp(vectors[1], 1)
    small = jnp.where(own, small, unspread(small, 0, 0))
    dec_attn_total = jnp.concatenate(
        [self_total[:4], cross_total[:4], self_total[4:], cross_total[4:]]
    )
    matrix_rate = MATRIX_RATE * root_frames
    vector_rate = VECTOR_RATE * root_frames
    ffn_new = update_matrices(
        [ffn_total],
        None,
        own_flag,
        (ffn_master, ffn_moment, ffn_average),
        matrix_rate,
        inverse,
        False,
    )
    dattn_new = update_matrices(
        [dec_attn_total],
        None,
        own_flag,
        (dec_attn_master, dec_attn_moment, dec_attn_average),
        matrix_rate,
        inverse,
        True,
    )
    dffn_new = update_matrices(
        dec_ffn_sums,
        plane_parts[0],
        own_flag,
        (dec_ffn_master, dec_ffn_moment, dec_ffn_average),
        matrix_rate,
        inverse,
        False,
    )
    small, out_dec, out_text_grad, out_enc, *_ = stage(
        small, out_dec, out_text_grad, out_enc, ffn_new[4], dattn_new[4], dffn_new[4]
    )
    small = small + swap_core(small)
    attn_parts, attn_plane_back, small, input_grad = stage(
        attn_parts, attn_plane_back, small, input_grad
    )
    attn_total = scatter_dp(sum_plane(attn_parts, attn_plane_back, own))
    (out_input_grad,) = place_quarters(to_owners(bf(input_grad)), owners, [half_len])
    small = sum_dp(small)
    def head_bias(i):
        row, lane = NORM_ROWS + i // 3, (i % 3) * 2 * PAIR
        return small[row, lane : lane + group_width]

    norm_total = small[: norm_vecs.shape[0]]
    dec_norm_total = small[norm_vecs.shape[0] : NORM_ROWS]
    col_total = jnp.concatenate([head_bias(0), head_bias(1), small[NORM_ROWS + 2]])
    dec_col_total = jnp.concatenate([head_bias(i) for i in range(2, 6)] + [small[NORM_ROWS + 3]])
    table_total = small[NORM_ROWS + 4 : NORM_ROWS + 4 + group_heads, :bucket_count].T

    attn_new = update_matrices(
        [attn_total],
        None,
        own_flag,
        (attn_master, attn_moment, attn_average),
        matrix_rate,
        inverse,
        True,
    )
    norm_new = update(norm_vecs, norm_moment, norm_average, norm_total, vector_rate, frame_total)
    col_new = update(col_bias, col_moment, col_average, col_total, vector_rate, frame_total)
    rel_new = update(rel_table, rel_moment, rel_average, table_total, vector_rate, frame_total)
    dnorm_new = update(
        dec_norm_vecs, dec_norm_moment, dec_norm_average, dec_norm_total, vector_rate, frame_total
    )
    dcol_new = update(
        dec_col_bias, dec_col_moment, dec_col_average, dec_col_total, vector_rate, frame_total
    )
    return (
        out_enc,
        out_input_grad,
        attn_new[0],
        ffn_new[0],
        *attn_new[1:],
        *ffn_new[1:],
        *norm_new[1:],
        *col_new[1:],
        *rel_new[1:],
        out_dec,
        out_text_grad,
        dattn_new[0],
        dffn_new[0],
        *dattn_new[1:],
        *dffn_new[1:],
        *dnorm_new[1:],
        *dcol_new[1:],
    )


def solution(mesh):
    rows = P("dp", "seq", None)
    matrix = P(None, ("dp", "seq"), "mp")
    table = P(None, "mp")
    enc_params = [matrix] * 6 + [P()] * 3 + [P("mp")] * 3 + [table] * 3
    dec_params = [matrix] * 6 + [P()] * 3 + [P("mp")] * 3
    in_specs = (rows, rows, P("dp"), *enc_params, rows, rows, P("dp"), *dec_params)
    out_specs = (
        [rows, rows]
        + [matrix] * 10
        + [P()] * 3
        + [P("mp")] * 3
        + [table] * 3
        + [rows, rows]
        + [matrix] * 10
        + [P()] * 3
        + [P("mp")] * 3
    )
    return jax.shard_map(
        local, mesh=mesh, in_specs=in_specs, out_specs=tuple(out_specs), check_vma=False
    )
```

```python
import functools

import jax
import jax.numpy as jnp
from jax import lax
from jax.experimental import pallas as pl
from jax.experimental.pallas import tpu as pltpu
from jax.sharding import PartitionSpec as P

EPSILON = 1e-05
MOMENTUM = 0.9
AVERAGING = 0.75
MATRIX_RATE = 0.02
VECTOR_RATE = 0.2
MASK_VALUE = -1e30
ROOT_HALF = 0.7071067811865476
INV_ROOT_TAU = 0.3989422804014327
BLOCK = 256
PAIR = 128
BF16 = jnp.bfloat16
F32 = jnp.float32
ON_CHIP = pl.BlockSpec(memory_space=pltpu.VMEM)
SCALARS = pl.BlockSpec(memory_space=pltpu.SMEM)


def bf(a):
    return a.astype(BF16)


def wide(a):
    return a.astype(F32)


def dot_nn(left, right):
    return jnp.dot(left, right, preferred_element_type=F32)


def dot_nt(left, right):
    return lax.dot_general(left, right, (((1,), (1,)), ((), ())), preferred_element_type=F32)


def dot_tn(left, right):
    return lax.dot_general(left, right, (((0,), (0,)), ((), ())), preferred_element_type=F32)


def swap_core(v):
    return lax.ppermute(v, "seq", [(0, 1), (1, 0)])


def swap_mp(v, bits):
    return lax.ppermute(v, "mp", [(m, m ^ bits) for m in range(4)])


def spread_perm(dx, flip):
    pairs = [
        (s * 4 + y * 2 + x, y * 4 + (s ^ flip) * 2 + (x ^ dx))
        for s in range(2)
        for y in range(2)
        for x in range(2)
    ]
    return [(a, b) for a, b in pairs if a != b]


ROUTES = [(dx, flip) for dx in range(2) for flip in range(2)]


def spread(v, dx, flip):
    return lax.ppermute(v, ("seq", "mp"), spread_perm(dx, flip))


def unspread(v, dx, flip):
    return lax.ppermute(v, ("seq", "mp"), [(d, s) for s, d in spread_perm(dx, flip)])


def sum_dp(v):
    n = lax.axis_size("dp")
    if n != 4:
        return lax.psum(v, "dp")
    for bits in (1, 2):
        v = v + lax.ppermute(v, "dp", [(i, i ^ bits) for i in range(n)])
    return v


def stage(*values):
    return lax.optimization_barrier(values)


def after(values, *others):
    return lax.optimization_barrier((values, others))[0]


def gather_dp(shard):
    return lax.all_gather(shard, "dp", axis=0, tiled=False)


def scatter_dp(whole):
    return lax.psum_scatter(whole, "dp", scatter_dimension=0, tiled=False)


def gather_plane(v):
    return [v] + [spread(v, dx, flip) for dx, flip in ROUTES]


def scatter_plane(pieces):
    return [unspread(p, dx, flip) for p, (dx, flip) in zip(pieces, ROUTES)]


def sum_plane(pieces, back, own):
    first = jnp.where(own, wide(pieces[0]), wide(back[0]))
    return bf(first + sum(wide(b) for b in back[1:]))


def pack_attn(shard):
    main, rest = shard[:, :, :PAIR], shard[:, :, PAIR:]
    return jnp.concatenate([main, jnp.concatenate([rest[0::2], rest[1::2]], axis=-1)], axis=0)


def half_lanes(shape):
    return lax.broadcasted_iota(jnp.int32, shape, len(shape) - 1) < PAIR // 2


def half_roll(v):
    return bf(pltpu.roll(wide(v), PAIR // 2, 1))


def assemble_attn(pieces, plans, count, yidx):
    n, tiles, rows, _ = pieces[0].shape

    def kernel(yi, *refs):
        ins, outs = refs[:5], refs[5:]
        low = half_lanes((rows, PAIR))
        for k in range(n):
            for a in range(2):
                side = yi[a]

                def tile(t, dx):
                    val = ins[1 + dx * 2 + a][k, t]
                    return jnp.where(yi[2] == 1, ins[0][k, t], val) if dx + a == 0 else val

                for out, plan in zip(outs, plans):
                    for place, (mat, j) in enumerate(plan):
                        if j < 2:
                            val = tile(mat, j)
                        else:
                            t0, t1 = tile(count + mat // 2, 0), tile(count + mat // 2, 1)
                            if mat % 2 == 0:
                                val = jnp.where(low, t0, half_roll(t1))
                            else:
                                val = jnp.where(low, half_roll(t0), t1)
                        out[k, side, :, place * PAIR : (place + 1) * PAIR] = val

    outs = pl.pallas_call(
        kernel,
        in_specs=[SCALARS] + [ON_CHIP] * 5,
        out_specs=[ON_CHIP] * len(plans),
        out_shape=[jax.ShapeDtypeStruct((n, 2, rows, PAIR * len(p)), BF16) for p in plans],
        cost_estimate=pl.CostEstimate(
            flops=0, transcendentals=0, bytes_accessed=9 * n * tiles * rows * PAIR * 2
        ),
        compiler_params=pltpu.CompilerParams(vmem_limit_bytes=12 << 20),
        name="assemble_attn",
    )(yidx, *pieces)
    return [o.reshape(n * 2 * rows, -1) for o in outs]


def split_attn(mats, plans, count, n, yidx):
    tiles = count + count // 2
    rows = mats[0].shape[0] // (2 * n)
    ins = [m.reshape(n, 2, rows, -1) for m in mats]
    where = {}
    for i, plan in enumerate(plans):
        for place, key in enumerate(plan):
            where[key] = (i, place)

    def kernel(yi, *refs):
        srcs, outs = refs[: len(mats)], refs[len(mats) :]
        low = half_lanes((rows, PAIR))
        for k in range(n):
            for a in range(2):
                side = yi[a]

                def get(mat, j):
                    i, place = where[(mat, j)]
                    return srcs[i][k, side, :, place * PAIR : (place + 1) * PAIR]

                for dx in range(2):
                    for t in range(tiles):
                        if t < count:
                            val = get(t, dx)
                        else:
                            p = t - count
                            t0, t1 = get(2 * p, 2), get(2 * p + 1, 2)
                            if dx == 0:
                                val = jnp.where(low, t0, half_roll(t1))
                            else:
                                val = jnp.where(low, half_roll(t0), t1)
                        outs[dx * 2 + a][k, t] = val

    return pl.pallas_call(
        kernel,
        in_specs=[SCALARS] + [ON_CHIP] * len(ins),
        out_specs=[ON_CHIP] * 4,
        out_shape=[jax.ShapeDtypeStruct((n, tiles, rows, PAIR), BF16)] * 4,
        cost_estimate=pl.CostEstimate(
            flops=0, transcendentals=0, bytes_accessed=8 * n * tiles * rows * PAIR * 2
        ),
        compiler_params=pltpu.CompilerParams(vmem_limit_bytes=12 << 20),
        name="split_attn",
    )(yidx, *ins)


def assemble_ffn(pieces, yidx):
    n, _, rows, cols = pieces[0].shape

    def kernel(yi, *refs):
        ins, outs = refs[:5], refs[5:]
        for k in range(n):
            for a in range(2):
                for h in range(2):
                    for dx in range(2):
                        val = ins[1 + dx * 2 + a][k, h]
                        val = jnp.where(yi[2] == 1, ins[0][k, h], val) if dx + a == 0 else val
                        outs[h][k, yi[a], :, dx * cols : (dx + 1) * cols] = val

    outs = pl.pallas_call(
        kernel,
        in_specs=[SCALARS] + [ON_CHIP] * 5,
        out_specs=[ON_CHIP] * 2,
        out_shape=[jax.ShapeDtypeStruct((n, 2, rows, 2 * cols), BF16)] * 2,
        cost_estimate=pl.CostEstimate(
            flops=0, transcendentals=0, bytes_accessed=2 * 9 * n * rows * cols * 2
        ),
        compiler_params=pltpu.CompilerParams(vmem_limit_bytes=16 << 20),
        name="assemble_ffn",
    )(yidx, *pieces)
    return [o.reshape(n * 2 * rows, 2 * cols) for o in outs]


def split_ffn(mats, n, yidx):
    rows = mats[0].shape[0] // (2 * n)
    cols = mats[0].shape[1] // 2
    ins = [m.reshape(n, 2, rows, 2 * cols) for m in mats]

    def kernel(yi, *refs):
        srcs, outs = refs[:2], refs[2:]
        for k in range(n):
            for a in range(2):
                for h in range(2):
                    for dx in range(2):
                        outs[dx * 2 + a][k, h] = srcs[h][
                            k, yi[a], :, dx * cols : (dx + 1) * cols
                        ]

    return pl.pallas_call(
        kernel,
        in_specs=[SCALARS] + [ON_CHIP] * 2,
        out_specs=[ON_CHIP] * 4,
        out_shape=[jax.ShapeDtypeStruct((n, 2, rows, cols), BF16)] * 4,
        cost_estimate=pl.CostEstimate(
            flops=0, transcendentals=0, bytes_accessed=2 * 8 * n * rows * cols * 2
        ),
        compiler_params=pltpu.CompilerParams(vmem_limit_bytes=16 << 20),
        name="split_ffn",
    )(yidx, *ins)


def assemble_planes(planes, yidx):
    n = planes.shape[0]
    rows, cols = planes.shape[4:]

    def kernel(yi, src, *outs):
        for k in range(n):
            for a in range(2):
                for h in range(2):
                    outs[h][k, yi[a]] = src[k, 0, a, h]

    outs = pl.pallas_call(
        kernel,
        grid_spec=pltpu.PrefetchScalarGridSpec(
            num_scalar_prefetch=1,
            grid=(2,),
            in_specs=[pl.BlockSpec((n, 1, 2, 2, rows, cols), lambda d, yi: (0, d, 0, 0, 0, 0))],
            out_specs=[pl.BlockSpec((n, 2, rows, cols), lambda d, yi: (0, 0, 0, d))] * 2,
        ),
        out_shape=[jax.ShapeDtypeStruct((n, 2, rows, 2 * cols), BF16)] * 2,
        cost_estimate=pl.CostEstimate(
            flops=0, transcendentals=0, bytes_accessed=2 * 8 * n * rows * cols * 2
        ),
        compiler_params=pltpu.CompilerParams(vmem_limit_bytes=24 << 20),
        name="assemble_planes",
    )(yidx, planes)
    return [o.reshape(n * 2 * rows, 2 * cols) for o in outs]


def split_planes(mats, n, yidx):
    rows = mats[0].shape[0] // (2 * n)
    cols = mats[0].shape[1] // 2
    ins = [m.reshape(n, 2, rows, 2 * cols) for m in mats]

    def kernel(yi, *refs):
        for k in range(n):
            for a in range(2):
                for h in range(2):
                    refs[2][k, 0, a, h] = refs[h][k, yi[a]]

    return pl.pallas_call(
        kernel,
        grid_spec=pltpu.PrefetchScalarGridSpec(
            num_scalar_prefetch=1,
            grid=(2,),
            in_specs=[pl.BlockSpec((n, 2, rows, cols), lambda d, yi: (0, 0, 0, d))] * 2,
            out_specs=pl.BlockSpec((n, 1, 2, 2, rows, cols), lambda d, yi: (0, d, 0, 0, 0, 0)),
        ),
        out_shape=jax.ShapeDtypeStruct((n, 2, 2, 2, rows, cols), BF16),
        cost_estimate=pl.CostEstimate(
            flops=0, transcendentals=0, bytes_accessed=2 * 8 * n * rows * cols * 2
        ),
        compiler_params=pltpu.CompilerParams(vmem_limit_bytes=24 << 20),
        name="split_planes",
    )(yidx, *ins)


def bias_tiles(line, blocks):
    heads, _, length = line.shape
    spans = 2 * blocks - 1
    width = 2 * BLOCK

    def kernel(line_ref, out_ref):
        row = lax.broadcasted_iota(jnp.int32, (8, width), 0)
        for d in range(spans):
            start = (spans - 1 - d) * BLOCK
            window = line_ref[0, :, start : start + width]
            turned = jnp.concatenate([window[:, BLOCK:], window[:, :BLOCK]], axis=1)
            tile = jnp.broadcast_to(turned, (8, width))
            for bit in (1, 2, 4):
                tile = jnp.where((row & bit) != 0, pltpu.roll(tile, bit, 1), tile)
            size = 8
            while size < BLOCK:
                tile = jnp.concatenate([tile, pltpu.roll(tile, size, 1)], axis=0)
                size *= 2
            out_ref[0, d] = tile[:, :BLOCK]

    return pl.pallas_call(
        kernel,
        grid=(heads,),
        in_specs=[pl.BlockSpec((1, 1, length), lambda h: (h, 0, 0))],
        out_specs=pl.BlockSpec((1, spans, BLOCK, BLOCK), lambda h: (h, 0, 0, 0)),
        out_shape=jax.ShapeDtypeStruct((heads, spans, BLOCK, BLOCK), F32),
        cost_estimate=pl.CostEstimate(
            flops=heads * spans * BLOCK * BLOCK * 8,
            transcendentals=0,
            bytes_accessed=heads * spans * BLOCK * BLOCK * 4,
        ),
        compiler_params=pltpu.CompilerParams(vmem_limit_bytes=8 << 20),
        name="bias_tiles",
    )(line)


def diagonal_sums(tile):
    width = 2 * BLOCK
    t = jnp.concatenate([tile, jnp.zeros_like(tile)], axis=1)
    size = BLOCK
    while size > 8:
        size //= 2
        t = t[:size] + pltpu.roll(t[size:], width - size, 1)
    row = lax.broadcasted_iota(jnp.int32, (8, width), 0)
    for bit in (1, 2, 4):
        t = jnp.where((row & bit) != 0, pltpu.roll(t, width - bit, 1), t)
    return jnp.sum(t, axis=0, keepdims=True)


def head_keys(keys, limit, a):
    lane = lax.broadcasted_iota(jnp.int32, keys.shape, 1)
    place = lax.broadcasted_iota(jnp.int32, keys.shape, 0)
    mine = (lane // (PAIR // 2)) == a
    flag = jnp.where(place < limit, 0.0, MASK_VALUE)
    other = jnp.where(lane == (1 - a) * (PAIR // 2), flag, 0.0)
    return bf(jnp.where(mine, wide(keys), other))


def head_queries(queries, scale, a, mark):
    lane = lax.broadcasted_iota(jnp.int32, queries.shape, 1)
    mine = (lane // (PAIR // 2)) == a
    other = jnp.where(lane == (1 - a) * (PAIR // 2), mark, 0.0)
    return bf(jnp.where(mine, wide(queries) * scale, other))


def only_head(values, a):
    lane = lax.broadcasted_iota(jnp.int32, values.shape, 1)
    return bf(jnp.where((lane // (PAIR // 2)) == a, wide(values), 0.0))


def score_blocks(key_a, query_a, bias_ref, a, qb, key_blocks, causal):
    out = []
    for kb in range(key_blocks):
        st = dot_nt(key_a[kb * BLOCK : (kb + 1) * BLOCK], query_a)
        if bias_ref is not None:
            st = st + bias_ref[a, kb - qb + key_blocks - 1]
        if causal:
            kpos = lax.broadcasted_iota(jnp.int32, st.shape, 0)
            qpos = lax.broadcasted_iota(jnp.int32, st.shape, 1)
            st = jnp.where(kpos <= qpos, st, MASK_VALUE)
        out.append(st)
    return out


def attention_forward(queries, memory, limit, bias, causal, fused):
    query_len = queries.shape[0]
    key_len = query_len if fused else memory.shape[0]
    pairs = queries.shape[1] // ((3 if fused else 1) * PAIR)
    key_blocks, query_blocks = key_len // BLOCK, query_len // BLOCK
    scale = (PAIR // 2) ** (-0.5)

    def kernel(limit_ref, q_ref, *refs):
        refs = list(refs)
        kv_ref = q_ref if fused else refs.pop(0)
        bias_ref = refs.pop(0) if bias is not None else None
        c_ref, lse_ref = refs
        k0 = PAIR if fused else 0
        keys = kv_ref[:, k0 : k0 + PAIR]
        values = kv_ref[:, k0 + PAIR : k0 + 2 * PAIR]
        key_a = [head_keys(keys, limit_ref[0], a) for a in range(2)]

        def visit(qb):
            rows = pl.ds(pl.multiple_of(qb * BLOCK, BLOCK), BLOCK)
            q = q_ref[rows, 0:PAIR]
            parts = []
            for a in range(2):
                st = score_blocks(
                    key_a[a], head_queries(q, scale, a, 1.0), bias_ref, a, qb, key_blocks, causal
                )
                top = functools.reduce(
                    jnp.maximum, [jnp.max(b, axis=0, keepdims=True) for b in st]
                )
                ex = [jnp.exp(b - top) for b in st]
                total = sum(jnp.sum(b, axis=0, keepdims=True) for b in ex)
                ct = sum(
                    dot_tn(values[kb * BLOCK : (kb + 1) * BLOCK], bf(ex[kb]))
                    for kb in range(key_blocks)
                )
                parts.append(ct[a * (PAIR // 2) : (a + 1) * (PAIR // 2)] * (1.0 / total))
                lse_ref[0, a : a + 1, rows] = top + jnp.log(total)
            c_ref[rows, :] = bf(jnp.transpose(jnp.concatenate(parts, axis=0)))

        if query_blocks == 1:
            visit(0)
        else:
            pl.loop(0, query_blocks)(visit)

    in_specs = [pl.BlockSpec((query_len, (3 if fused else 1) * PAIR), lambda j, n: (0, j))]
    args = [queries]
    if not fused:
        in_specs.append(pl.BlockSpec((key_len, 2 * PAIR), lambda j, n: (0, j)))
        args.append(memory)
    if bias is not None:
        in_specs.append(pl.BlockSpec((2,) + bias.shape[1:], lambda j, n: (j, 0, 0, 0)))
        args.append(pltpu.with_memory_space_constraint(bias, pltpu.HBM))
    return pl.pallas_call(
        kernel,
        grid_spec=pltpu.PrefetchScalarGridSpec(
            num_scalar_prefetch=1,
            grid=(pairs,),
            in_specs=in_specs,
            out_specs=[
                pl.BlockSpec((query_len, PAIR), lambda j, n: (0, j)),
                pl.BlockSpec((1, 8, query_len), lambda j, n: (j, 0, 0)),
            ],
        ),
        out_shape=[
            jax.ShapeDtypeStruct((query_len, pairs * PAIR), BF16),
            jax.ShapeDtypeStruct((pairs, 8, query_len), F32),
        ],
        compiler_params=pltpu.CompilerParams(vmem_limit_bytes=26 << 20),
        cost_estimate=pl.CostEstimate(
            flops=pairs * 2 * query_len * key_len * PAIR * 4,
            transcendentals=pairs * 2 * query_len * key_len,
            bytes_accessed=pairs * PAIR * 2 * 2 * (query_len + key_len),
        ),
        name="attend_" + ("enc" if bias is not None else "dec" if fused else "cross"),
    )(limit, *args)


def attention_backward(queries, memory, limit, bias, causal, fused, context, lse, context_grad):
    query_len = queries.shape[0]
    key_len = query_len if fused else memory.shape[0]
    pairs = queries.shape[1] // ((3 if fused else 1) * PAIR)
    key_blocks, query_blocks = key_len // BLOCK, query_len // BLOCK
    spans = 2 * key_blocks - 1
    scale = (PAIR // 2) ** (-0.5)

    def kernel(limit_ref, q_ref, *refs):
        refs = list(refs)
        kv_ref = q_ref if fused else refs.pop(0)
        bias_ref = refs.pop(0) if bias is not None else None
        c_ref, lse_ref, dc_ref = refs[:3]
        refs = refs[3:]
        dq_ref = refs.pop(0)
        dkv_ref = dq_ref if fused else refs.pop(0)
        dq_sum = refs.pop(0)
        dkv_sum = dq_sum if fused else refs.pop(0)
        diag_ref = refs.pop(0) if bias is not None else None
        dk_acc, dv_acc = refs[:2]
        tile_acc = refs[2] if bias is not None else None
        k0 = PAIR if fused else 0
        keys = kv_ref[:, k0 : k0 + PAIR]
        values = kv_ref[:, k0 + PAIR : k0 + 2 * PAIR]
        key_a = [head_keys(keys, limit_ref[0], a) for a in range(2)]
        pure_key_a = [only_head(keys, a) for a in range(2)]
        value_a = [only_head(values, a) for a in range(2)]
        dq_sum[...] = jnp.zeros_like(dq_sum)
        dk_acc[...] = jnp.zeros_like(dk_acc)
        dv_acc[...] = jnp.zeros_like(dv_acc)
        if bias is not None:
            tile_acc[...] = jnp.zeros_like(tile_acc)

        def visit(qb):
            rows = pl.ds(pl.multiple_of(qb * BLOCK, BLOCK), BLOCK)
            q = q_ref[rows, 0:PAIR]
            dc = dc_ref[rows, :]
            both = jnp.transpose(wide(dc) * wide(c_ref[rows, :]))
            dqt = jnp.zeros((PAIR, BLOCK), F32)
            for a in range(2):
                st = score_blocks(
                    key_a[a], head_queries(q, scale, a, 1.0), bias_ref, a, qb, key_blocks, causal
                )
                delta = jnp.sum(
                    both[a * (PAIR // 2) : (a + 1) * (PAIR // 2)], axis=0, keepdims=True
                )
                log_row = lse_ref[0, a : a + 1, rows]
                dc_a = only_head(dc, a)
                q_a = head_queries(q, scale, a, 0.0)
                for kb in range(key_blocks):
                    span = slice(kb * BLOCK, (kb + 1) * BLOCK)
                    p = jnp.exp(st[kb] - log_row)
                    dp = dot_nt(value_a[a][span], dc)
                    ds = p * (dp - delta)
                    dsb = bf(ds)
                    dv_acc[span, :] += dot_nn(bf(p), dc_a)
                    dk_acc[span, :] += dot_nn(dsb, q_a)
                    dqt = dqt + dot_tn(pure_key_a[a][span], dsb)
                    if bias is not None:
                        tile_acc[a, kb - qb + key_blocks - 1] += ds
            dq = bf(jnp.transpose(dqt) * scale)
            dq_ref[rows, 0:PAIR] = dq
            dq_sum[0:1, 0:PAIR] += jnp.sum(wide(dq), axis=0, keepdims=True)

        if query_blocks == 1:
            visit(0)
        else:
            pl.loop(0, query_blocks)(visit)
        dkv_ref[:, k0 : k0 + PAIR] = bf(dk_acc[...])
        dv = bf(dv_acc[...])
        dkv_ref[:, k0 + PAIR : k0 + 2 * PAIR] = dv
        dkv_sum[0:1, k0 + PAIR : k0 + 2 * PAIR] = jnp.sum(wide(dv), axis=0, keepdims=True)
        if bias is not None:
            for a in range(2):
                for d in range(spans):
                    diag_ref[a, d : d + 1, :] = diagonal_sums(tile_acc[a, d])

    in_specs = [pl.BlockSpec((query_len, (3 if fused else 1) * PAIR), lambda j, n: (0, j))]
    args = [queries]
    if not fused:
        in_specs.append(pl.BlockSpec((key_len, 2 * PAIR), lambda j, n: (0, j)))
        args.append(memory)
    if bias is not None:
        in_specs.append(pl.BlockSpec((2,) + bias.shape[1:], lambda j, n: (j, 0, 0, 0)))
        args.append(pltpu.with_memory_space_constraint(bias, pltpu.HBM))
    in_specs += [
        pl.BlockSpec((query_len, PAIR), lambda j, n: (0, j)),
        pl.BlockSpec((1, 8, query_len), lambda j, n: (j, 0, 0)),
        pl.BlockSpec((query_len, PAIR), lambda j, n: (0, j)),
    ]
    args += [context, lse, context_grad]
    out_specs = [pl.BlockSpec((query_len, (3 if fused else 1) * PAIR), lambda j, n: (0, j))]
    out_shape = [jax.ShapeDtypeStruct(queries.shape, BF16)]
    scratch = [pltpu.VMEM((key_len, PAIR), F32)] * 2
    if not fused:
        out_specs.append(pl.BlockSpec((key_len, 2 * PAIR), lambda j, n: (0, j)))
        out_shape.append(jax.ShapeDtypeStruct(memory.shape, BF16))
    for array, tiles in ((queries, 3 if fused else 1), (memory, 2)):
        if array is not None:
            out_specs.append(pl.BlockSpec((8, tiles * PAIR), lambda j, n: (0, j)))
            out_shape.append(jax.ShapeDtypeStruct((8, array.shape[1]), F32))
    if bias is not None:
        out_specs.append(pl.BlockSpec((2, 8, 2 * BLOCK), lambda j, n: (j, 0, 0)))
        out_shape.append(jax.ShapeDtypeStruct((2 * pairs, 8, 2 * BLOCK), F32))
        scratch.append(pltpu.VMEM((2, spans, BLOCK, BLOCK), F32))
    return pl.pallas_call(
        kernel,
        grid_spec=pltpu.PrefetchScalarGridSpec(
            num_scalar_prefetch=1,
            grid=(pairs,),
            in_specs=in_specs,
            out_specs=out_specs,
            scratch_shapes=scratch,
        ),
        out_shape=out_shape,
        compiler_params=pltpu.CompilerParams(vmem_limit_bytes=26 << 20),
        cost_estimate=pl.CostEstimate(
            flops=pairs * 2 * query_len * key_len * PAIR * 10,
            transcendentals=pairs * 2 * query_len * key_len,
            bytes_accessed=pairs * PAIR * 2 * 4 * (query_len + key_len),
        ),
        name="attend_back_" + ("enc" if bias is not None else "dec" if fused else "cross"),
    )(limit, *args)


def gelu(z):
    return z * (0.5 * (1.0 + lax.erf(z * ROOT_HALF)))


def gelu_slope(z):
    return 0.5 * (1.0 + lax.erf(z * ROOT_HALF)) + z * jnp.exp(-0.5 * z * z) * INV_ROOT_TAU


ROWS = 128


def row_steps(count, body):
    @pl.loop(0, count // ROWS)
    def _(step):
        body(pl.ds(pl.multiple_of(step * ROWS, ROWS), ROWS), step)


def add_norm(residual, own_part, other_part, vecs, bias, gain, shift):
    source, affine = residual if isinstance(residual, tuple) else (residual, None)
    count, width = source.shape

    def kernel(x_ref, p_ref, q_ref, v_ref, low_ref, normed_ref, inv_ref):
        def body(rows, step):
            base = wide(x_ref[rows])
            if affine is not None:
                base = base * v_ref[affine[0] : affine[0] + 1] + v_ref[affine[1] : affine[1] + 1]
            values = base + (wide(p_ref[rows]) + wide(q_ref[rows])) + v_ref[bias : bias + 1]
            center = values - jnp.sum(values, axis=-1, keepdims=True) * (1.0 / width)
            square = jnp.sum(center * center, axis=-1, keepdims=True)
            inv = lax.rsqrt(square * (1.0 / width) + EPSILON)
            normed = center * inv
            low_ref[rows] = bf(normed * v_ref[gain : gain + 1] + v_ref[shift : shift + 1])
            normed_ref[rows] = normed
            inv_ref[rows] = jnp.broadcast_to(inv, (ROWS, PAIR))

        row_steps(count, body)

    return pl.pallas_call(
        kernel,
        in_specs=[ON_CHIP] * 4,
        out_specs=[ON_CHIP] * 3,
        out_shape=[
            jax.ShapeDtypeStruct((count, width), BF16),
            jax.ShapeDtypeStruct((count, width), F32),
            jax.ShapeDtypeStruct((count, PAIR), F32),
        ],
        cost_estimate=pl.CostEstimate(
            flops=12 * count * width, transcendentals=count, bytes_accessed=14 * count * width
        ),
        compiler_params=pltpu.CompilerParams(vmem_limit_bytes=14 << 20),
        name="add_norm",
    )(source, own_part, other_part, vecs)


def norm_back(terms, limit, normed, inv, vecs, gain):
    count, width = normed.shape
    use = limit is not None

    def kernel(*refs):
        refs = list(refs)
        limit_ref = refs.pop(0) if use else None
        ins, (n_ref, inv_ref, v_ref, grad_ref, low_ref, sum_ref) = refs[:-6], refs[-6:]
        sum_ref[...] = jnp.zeros_like(sum_ref)

        def body(rows, step):
            up = wide(ins[0][rows])
            if use:
                place = step * ROWS + lax.broadcasted_iota(jnp.int32, up.shape, 0)
                up = jnp.where(place < limit_ref[0], up, 0.0)
            rest = [wide(r[rows]) for r in ins[1:]]
            if rest:
                up = up + (rest[0] + rest[1])
            values = n_ref[rows]
            scaled = up * v_ref[gain : gain + 1]
            mean = jnp.sum(scaled, axis=-1, keepdims=True) * (1.0 / width)
            along = jnp.sum(scaled * values, axis=-1, keepdims=True) * (1.0 / width)
            grad = inv_ref[rows, :1] * (scaled - mean - values * along)
            grad_ref[rows] = grad
            low_ref[rows] = bf(grad)
            sum_ref[0:1] += jnp.sum(up * values, axis=0, keepdims=True)
            sum_ref[1:2] += jnp.sum(up, axis=0, keepdims=True)
            sum_ref[2:3] += jnp.sum(grad, axis=0, keepdims=True)

        row_steps(count, body)

    smem = [pl.BlockSpec(memory_space=pltpu.SMEM)] if use else []
    return pl.pallas_call(
        kernel,
        in_specs=smem + [ON_CHIP] * (len(terms) + 3),
        out_specs=[ON_CHIP] * 3,
        out_shape=[
            jax.ShapeDtypeStruct((count, width), F32),
            jax.ShapeDtypeStruct((count, width), BF16),
            jax.ShapeDtypeStruct((8, width), F32),
        ],
        cost_estimate=pl.CostEstimate(
            flops=16 * count * width, transcendentals=0, bytes_accessed=20 * count * width
        ),
        compiler_params=pltpu.CompilerParams(vmem_limit_bytes=18 << 20),
        name="norm_back",
    )(*([limit] if use else []), *terms, normed, inv, vecs)


NORM_ROWS = 15


def pack_small(norm_sums, enc_sum, dec_sum, query_sum, memory_sum, unit_sums, diag, buckets):
    width = norm_sums[0].shape[1]
    heads, _, span = diag.shape
    spans = 2 * (span // BLOCK) + 1
    length = (spans + 1) * BLOCK

    def kernel(*refs):
        one, two, d_one, d_two, d_three = refs[:5]
        enc_ref, dec_ref, query_ref, memory_ref, unit_ref, dec_unit_ref, diag_ref = refs[5:12]
        outs, line = refs[12:14], refs[14]
        norms = [(one, 0), (one, 1), (two, 0), (two, 1), (one, 2), (two, 2)]
        norms += [(r, i) for r in (d_one, d_two, d_three) for i in range(2)]
        norms += [(r, 2) for r in (d_one, d_two, d_three)]
        tiles = [(enc_ref, 3, 0), (enc_ref, 3, 2), (dec_ref, 3, 0)]
        tiles += [(dec_ref, 3, 2), (query_ref, 1, 0), (memory_ref, 2, 1)]
        line[...] = jnp.zeros_like(line)
        for h in range(heads):
            for d in range(spans):
                row = diag_ref[h, d : d + 1, :]
                start = (spans - 1 - d) * BLOCK
                line[h : h + 1, start : start + BLOCK] += row[:, BLOCK:]
                line[h : h + 1, start + BLOCK : start + 2 * BLOCK] += row[:, :BLOCK]
        wide_table = -(-buckets // PAIR) * PAIR
        dist = length // 2 - lax.broadcasted_iota(jnp.int32, (length, wide_table), 0)
        bucket = jnp.clip(dist, -(buckets // 2), buckets // 2 - 1) + buckets // 2
        hot = jnp.where(
            bucket == lax.broadcasted_iota(jnp.int32, (length, wide_table), 1), 1.0, 0.0
        )
        table = jnp.dot(
            line[...], hot, precision=lax.Precision.HIGHEST, preferred_element_type=F32
        )
        for dx, out in enumerate(outs):
            out[...] = jnp.zeros_like(out)
            for i, (ref, r) in enumerate(norms):
                out[i : i + 1, :] = ref[r : r + 1, :]
            for i, (ref, stride, at) in enumerate(tiles):
                row, lane = NORM_ROWS + i // 3, (i % 3) * 2 * PAIR
                part = [ref[0:1, (j * stride + at) * PAIR : (j * stride + at + 1) * PAIR] for j in range(3)]
                out[row : row + 1, lane : lane + PAIR] = part[dx]
                both = jnp.broadcast_to(part[2], (8, PAIR))
                both = pltpu.roll(both, PAIR // 2, 1) if dx else both
                out[row : row + 1, lane + PAIR : lane + 2 * PAIR] = both[0:1]
            for i, ref in enumerate((unit_ref, dec_unit_ref)):
                out[NORM_ROWS + 2 + i : NORM_ROWS + 3 + i, :] = ref[0:1, dx * width : (dx + 1) * width]
            for i, h in enumerate(((0, 1, 4), (2, 3, 5))[dx]):
                out[NORM_ROWS + 4 + i : NORM_ROWS + 5 + i, 0:wide_table] = table[h : h + 1]

    return pl.pallas_call(
        kernel,
        out_shape=[jax.ShapeDtypeStruct((24, width), F32)] * 2,
        scratch_shapes=[pltpu.VMEM((8, length), F32)],
        compiler_params=pltpu.CompilerParams(vmem_limit_bytes=12 << 20),
        name="pack_small",
    )(*norm_sums, enc_sum, dec_sum, query_sum, memory_sum, *unit_sums, diag)


def update_matrices(sums, alternative, own, state, rate, inverse, packed):
    master = state[0]
    count, rows, cols = master.shape
    step = 2 if packed else 1
    arrays = list(sums) + ([alternative] if alternative is not None else [])

    def kernel(own_ref, inv_ref, *refs):
        if packed:
            groups = [refs[2 * i : 2 * i + 2] for i in range(len(arrays))]
            refs = refs[2 * len(arrays) :]
        else:
            groups = [refs[i : i + 1] for i in range(len(arrays))]
            refs = refs[len(arrays) :]
        state_refs, outs = refs[:3], refs[3:]
        inv = inv_ref[0]

        def total(part, i):
            vals = [wide(g[part][i]) for g in groups]
            if alternative is not None:
                vals = [jnp.where(own_ref[0] == 1, vals[-1], vals[0])] + vals[1:-1]
            return functools.reduce(jnp.add, vals)

        def advance(grad, i, span):
            mean_grad = grad * inv
            new_moment = MOMENTUM * state_refs[1][i, :, span] + mean_grad
            new_master = state_refs[0][i, :, span] - rate * (mean_grad + MOMENTUM * new_moment)
            outs[0][i, :, span] = mean_grad
            outs[1][i, :, span] = new_master
            outs[2][i, :, span] = new_moment
            outs[3][i, :, span] = (
                AVERAGING * state_refs[2][i, :, span] + (1.0 - AVERAGING) * new_master
            )
            outs[4][i, :, span] = bf(new_master)

        if packed:
            rest = total(1, 0)
            turned = pltpu.roll(rest, PAIR // 2, 1)
            for i in range(2):
                advance(total(0, i), i, slice(0, PAIR))
                advance((turned if i else rest)[:, : PAIR // 2], i, slice(PAIR, cols))
        else:
            advance(total(0, 0), 0, slice(0, cols))

    in_specs, args = [], []
    for a in arrays:
        in_specs.append(pl.BlockSpec((step, rows, a.shape[2]), lambda k, o: (k, 0, 0)))
        args.append(a)
        if packed:
            in_specs.append(pl.BlockSpec((1, rows, PAIR), lambda k, o: (count + k, 0, 0)))
            args.append(a)
    spec = pl.BlockSpec((step, rows, cols), lambda k, o: (k, 0, 0))
    return pl.pallas_call(
        kernel,
        grid_spec=pltpu.PrefetchScalarGridSpec(
            num_scalar_prefetch=1,
            grid=(count // step,),
            in_specs=[pl.BlockSpec(memory_space=pltpu.SMEM)] + in_specs + [spec] * 3,
            out_specs=[spec] * 5,
        ),
        out_shape=[jax.ShapeDtypeStruct(master.shape, F32)] * 4
        + [jax.ShapeDtypeStruct(master.shape, BF16)],
        cost_estimate=pl.CostEstimate(
            flops=12 * master.size, transcendentals=0, bytes_accessed=44 * master.size
        ),
        compiler_params=pltpu.CompilerParams(vmem_limit_bytes=8 << 20),
        name="update_matrices",
    )(own, inverse, *args, *state)


def place_quarters(parts, index, cuts):
    count, outputs = len(parts), len(cuts)
    starts = [sum(cuts[:i]) for i in range(outputs)]

    def kernel(idx, *refs):
        outs, sem = refs[count : count + outputs], refs[-1]
        copies = [
            pltpu.make_async_copy(
                refs[k].at[starts[i] : starts[i] + cuts[i]], outs[i].at[idx[k]], sem.at[k, i]
            )
            for k in range(count)
            for i in range(outputs)
        ]
        for copy in copies:
            copy.start()
        for copy in copies:
            copy.wait()

    return pl.pallas_call(
        kernel,
        in_specs=[SCALARS] + [ON_CHIP] * count,
        out_specs=[pl.BlockSpec(memory_space=pl.ANY)] * outputs,
        out_shape=[
            jax.ShapeDtypeStruct((count, c) + parts[0].shape[1:], parts[0].dtype) for c in cuts
        ],
        scratch_shapes=[pltpu.SemaphoreType.DMA((count, outputs))],
        cost_estimate=pl.CostEstimate(
            flops=0, transcendentals=0, bytes_accessed=4 * count * parts[0].size
        ),
        compiler_params=pltpu.CompilerParams(vmem_limit_bytes=8 << 20),
        name="place_quarters",
    )(index, *parts)


def update(master, moment, average, gradient, rate, frame_total):
    mean_grad = gradient / frame_total
    new_moment = MOMENTUM * moment + mean_grad
    new_master = master - rate * (mean_grad + MOMENTUM * new_moment)
    new_average = AVERAGING * average + (1.0 - AVERAGING) * new_master
    return mean_grad, new_master, new_moment, new_average


def order_cols(v0, v1):
    return jnp.concatenate(
        [v0[..., :PAIR], v1[..., :PAIR], v0[..., PAIR:], v1[..., PAIR:]], axis=-1
    )


CROSS_PLANS = [
    [(0, j) for j in range(3)],
    [(m, j) for j in range(3) for m in (1, 2)],
    [(3, j) for j in range(3)],
]
QKV_PLAN = [(m, j) for j in range(3) for m in range(3)]
ENC_PLANS = [QKV_PLAN, [(3, j) for j in range(3)]]

def local(
    frames,
    cotangent,
    lengths,
    attn_master,
    attn_moment,
    attn_average,
    ffn_master,
    ffn_moment,
    ffn_average,
    norm_vecs,
    norm_moment,
    norm_average,
    col_bias,
    col_moment,
    col_average,
    rel_table,
    rel_moment,
    rel_average,
    dec_frames,
    dec_cotangent,
    text_lengths,
    dec_attn_master,
    dec_attn_moment,
    dec_attn_average,
    dec_ffn_master,
    dec_ffn_moment,
    dec_ffn_average,
    dec_norm_vecs,
    dec_norm_moment,
    dec_norm_average,
    dec_col_bias,
    dec_col_moment,
    dec_col_average,
):
    n_dp = lax.axis_size("dp")
    z, s, m = lax.axis_index("dp"), lax.axis_index("seq"), lax.axis_index("mp")
    y = m // 2
    utt_count, half_len, width = frames.shape
    text_half = dec_frames.shape[1]
    full_len, text_full = 2 * half_len, 2 * text_half
    own = s == y
    yidx = jnp.stack([y, 1 - y, own.astype(jnp.int32)]).astype(jnp.int32)
    root_frames = float(utt_count * full_len * n_dp) ** 0.5

    mine = jnp.concatenate(
        [
            lax.dynamic_index_in_dim(parts, m, 0, keepdims=False)
            for parts in (frames, cotangent, dec_frames, dec_cotangent)
        ]
    )
    other = swap_core(mine)
    dffn_shard = bf(dec_ffn_master)
    dffn_parts = gather_plane(dffn_shard)
    attn_z = gather_dp(pack_attn(bf(attn_master)))
    packed = jnp.concatenate([col_bias, dec_col_bias, rel_table.T.reshape(-1)])
    groups = [jnp.where(own, packed, spread(packed, 0, 0)), spread(packed, 1, 0)]
    ffn_z = gather_dp(after(bf(ffn_master), attn_z))
    mine, other, dffn_parts, attn_z, groups, dattn_low, lengths = stage(
        mine, other, dffn_parts, attn_z, groups, dec_attn_master, lengths
    )
    dattn_low = bf(dattn_low)
    attn_pieces = gather_plane(attn_z)

    bucket_count, group_heads = rel_table.shape
    group_width = attn_master.shape[2]
    unit_count = ffn_master.shape[2]
    enc_cols, dec_cols = col_bias.shape[0], dec_col_bias.shape[0]

    def cols_at(start):
        return order_cols(*[g[start : start + group_width] for g in groups])

    def units_at(start):
        return jnp.concatenate([g[start : start + unit_count] for g in groups])

    def qkv_bias(q, v):
        blank = jnp.zeros((PAIR,), F32)
        cut = [slice(j * PAIR, (j + 1) * PAIR) for j in range(3)]
        return jnp.concatenate([part for c in cut for part in (q[c], blank, v[c])])

    bias_qkv = qkv_bias(cols_at(0), cols_at(group_width))
    bias_one = units_at(2 * group_width)
    tables = [
        g[enc_cols + dec_cols :].reshape(group_heads, bucket_count) for g in groups
    ]
    heads = jnp.stack(
        [tables[0][0], tables[0][1], tables[1][0], tables[1][1], tables[0][2], tables[1][2]]
    )
    max_dist = bucket_count // 2
    blocks = full_len // BLOCK
    lead = blocks * BLOCK - max_dist + 1
    tail = blocks * BLOCK - max_dist - 1
    line = jnp.pad(heads[:, ::-1], ((0, 0), (lead, tail)), mode="edge")
    bias = bias_tiles(line[:, None, :], blocks)

    def all_rows(start, count):
        ours, theirs = mine[start : start + count], other[start : start + count]
        return jnp.concatenate([jnp.where(s == 0, ours, theirs), jnp.where(s == 0, theirs, ours)])

    inputs = all_rows(0, half_len)
    limit = lax.dynamic_slice_in_dim(lengths, m, 1)
    text_limit = lax.dynamic_slice_in_dim(text_lengths, m, 1)
    own_flag = own.astype(jnp.int32).reshape(1)

    def my_half(rows):
        count = rows.shape[0] // 2
        return lax.dynamic_slice_in_dim(rows, s * count, count, 0)

    def to_owners(mine):
        return [mine] + [swap_mp(mine, bits) for bits in range(1, 4)]

    owners = m ^ jnp.arange(4, dtype=jnp.int32)

    frame_count = jnp.sum(lengths)
    digit_row = lax.broadcasted_iota(jnp.int32, (1,) + dec_attn_master.shape[1:2] + (PAIR,), 1)
    digits = bf(jnp.where(digit_row == 0, frame_count // 256, frame_count % 256))

    attn_pieces, ffn_z, bias, bias_qkv, inputs, dattn_shard, dffn_plane = stage(
        attn_pieces,
        ffn_z,
        bias,
        bias_qkv,
        inputs,
        jnp.concatenate(
            [pack_attn(dattn_low[:4]), pack_attn(dattn_low[4:]), digits]
        ),
        jnp.stack([jnp.where(own, dffn_parts[0], dffn_parts[1]), *dffn_parts[2:]]),
    )
    ffn_pieces = gather_plane(ffn_z)
    dattn_z = gather_dp(dattn_shard)
    w_qkv, w_o = assemble_attn(attn_pieces, ENC_PLANS, 4, yidx)
    qkv = bf(dot_nn(inputs, w_qkv) + bias_qkv)
    context, lse = attention_forward(qkv, None, limit, bias, False, True)
    part = bf(dot_nt(context, w_o))
    ffn_pieces, dattn_z, part, dffn_plane, groups, mine, other = stage(
        ffn_pieces, dattn_z, part, dffn_plane, groups, mine, other
    )
    bias_dqkv = qkv_bias(cols_at(enc_cols), cols_at(enc_cols + group_width))
    bias_cq = cols_at(enc_cols + 2 * group_width)
    cv = cols_at(enc_cols + 3 * group_width)
    blank = jnp.zeros((PAIR,), F32)
    bias_ckv = jnp.concatenate(
        [part for j in range(3) for part in (blank, cv[j * PAIR : (j + 1) * PAIR])]
    )
    bias_done = units_at(enc_cols + 4 * group_width)
    upstream_in = all_rows(half_len, half_len)
    text_in = all_rows(2 * half_len, text_half)
    text_upstream = all_rows(2 * half_len + text_half, text_half)
    tiles = dattn_z.shape[1] // 2
    frame_total = jnp.sum(wide(dattn_z[:, -1, 0, 0]) * 256.0 + wide(dattn_z[:, -1, 1, 0]))
    cross_z = dattn_z[:, tiles : 2 * tiles]
    self_pieces = gather_plane(dattn_z[:, :tiles])
    dffn_planes = gather_dp(dffn_plane.reshape((2, 2) + dffn_shard.shape))
    hidden_low, normed_one, inv_one = add_norm(
        inputs, part, swap_core(part), norm_vecs, 4, 0, 1
    )
    w_one, w_two = assemble_ffn(ffn_pieces, yidx)
    gate_in = dot_nn(hidden_low, w_one) + bias_one
    activated, slope = bf(gelu(gate_in)), bf(gelu_slope(gate_in))
    part = bf(dot_nt(activated, w_two))
    biases = (bias_dqkv, bias_cq, bias_ckv, bias_done)
    rows_in = (upstream_in, text_in, text_upstream)
    self_pieces, cross_z, part, activated, slope, frame_total, biases, rows_in = stage(
        self_pieces, cross_z, part, activated, slope, frame_total, biases, rows_in
    )
    bias_dqkv, bias_cq, bias_ckv, bias_done = biases
    upstream_in, text_in, text_upstream = rows_in
    inverse = (1.0 / frame_total).reshape(1)
    cross_pieces = gather_plane(cross_z)
    enc_low, normed_two, inv_two = add_norm(
        (normed_one, (0, 1)), part, swap_core(part), norm_vecs, 5, 2, 3
    )

    d_qkv, d_o = assemble_attn(self_pieces, ENC_PLANS, 4, yidx)
    dqkv = bf(dot_nn(text_in, d_qkv) + bias_dqkv)
    self_context, self_lse = attention_forward(dqkv, None, text_limit, None, True, True)
    part, cross_pieces = stage(bf(dot_nt(self_context, d_o)), cross_pieces)
    c_q, c_kv, c_o = assemble_attn(cross_pieces, CROSS_PLANS, 4, yidx)
    dw_one, dw_two = assemble_planes(dffn_planes, yidx)
    dec_one_low, normed_d1, inv_d1 = add_norm(
        text_in, part, swap_core(part), dec_norm_vecs, 6, 0, 1
    )
    cross_q = bf(dot_nn(dec_one_low, c_q) + bias_cq)
    cross_kv = bf(dot_nn(enc_low, c_kv) + bias_ckv)
    cross_context, cross_lse = attention_forward(cross_q, cross_kv, limit, None, False, False)
    part = bf(dot_nt(cross_context, c_o))
    dec_two_low, normed_d2, inv_d2 = add_norm(
        (normed_d1, (0, 1)), part, swap_core(part), dec_norm_vecs, 7, 2, 3
    )
    dec_gate = dot_nn(dec_two_low, dw_one) + bias_done
    dec_act, dec_slope = bf(gelu(dec_gate)), bf(gelu_slope(dec_gate))
    part, dec_act, dec_slope = stage(bf(dot_nt(dec_act, dw_two)), dec_act, dec_slope)
    dec_low, normed_d3, inv_d3 = add_norm(
        (normed_d2, (2, 3)), part, swap_core(part), dec_norm_vecs, 8, 4, 5
    )
    grad_d3, dec_ffn_back, sums_d3 = norm_back(
        [text_upstream], text_limit, normed_d3, inv_d3, dec_norm_vecs, 4
    )
    dec_gate_grad = bf(dot_nn(dec_ffn_back, dw_two) * wide(dec_slope))
    dec_gate_sum = jnp.sum(dec_gate_grad, axis=0, dtype=F32)[None]
    part = bf(dot_nt(dec_gate_grad, dw_one))
    dec_ffn_grads = [
        bf(dot_tn(dec_two_low, dec_gate_grad)),
        bf(dot_tn(dec_ffn_back, dec_act)),
    ]
    dec_ffn_planes, part, sent = stage(
        split_planes(dec_ffn_grads, n_dp, yidx),
        part,
        jnp.concatenate([my_half(enc_low), my_half(dec_low)]),
    )
    dec_ffn_plane = scatter_dp(dec_ffn_planes)
    held = to_owners(sent)

    grad_d2, cross_back, sums_d2 = norm_back(
        [grad_d3, part, swap_core(part)], None, normed_d2, inv_d2, dec_norm_vecs, 2
    )
    cross_qg, cross_kvg, query_sum, memory_sum = attention_backward(
        cross_q,
        cross_kv,
        limit,
        None,
        False,
        False,
        cross_context,
        cross_lse,
        bf(dot_nn(cross_back, c_o)),
    )
    cross_grads = [
        bf(dot_tn(dec_one_low, cross_qg)),
        bf(dot_tn(enc_low, cross_kvg)),
        bf(dot_tn(cross_back, cross_context)),
    ]
    query_part, memory_part, cross_parts, held = stage(
        bf(dot_nt(cross_qg, c_q)),
        bf(dot_nt(cross_kvg, c_kv)),
        split_attn(cross_grads, CROSS_PLANS, 4, n_dp, yidx),
        held,
    )
    cross_plane_back = scatter_plane(cross_parts)
    memory_other = swap_core(memory_part)
    grad_d1, self_back, sums_d1 = norm_back(
        [grad_d2, query_part, swap_core(query_part)], None, normed_d1, inv_d1, dec_norm_vecs, 0
    )
    self_g, dec_sum = attention_backward(
        dqkv,
        None,
        text_limit,
        None,
        True,
        True,
        self_context,
        self_lse,
        bf(dot_nn(self_back, d_o)),
    )
    text_part = bf(dot_nt(self_g, d_qkv))
    self_grads = [bf(dot_tn(text_in, self_g)), bf(dot_tn(self_back, self_context))]
    self_parts = split_attn(self_grads, ENC_PLANS, 4, n_dp, yidx)

    grad_two, ffn_back, sums_two = norm_back(
        [upstream_in, memory_part, memory_other], limit, normed_two, inv_two, norm_vecs, 2
    )
    gate_grad = bf(dot_nn(ffn_back, w_two) * wide(slope))
    gate_sum = jnp.sum(gate_grad, axis=0, dtype=F32)[None]
    self_parts, gate_grad, ffn_back, cross_parts, cross_plane_back, text_part = stage(
        self_parts, gate_grad, ffn_back, cross_parts, cross_plane_back, text_part
    )
    self_plane_back = scatter_plane(self_parts)
    text_other = swap_core(text_part)
    cross_total = scatter_dp(sum_plane(cross_parts, cross_plane_back, own))
    ffn_grads = [bf(dot_tn(hidden_low, gate_grad)), bf(dot_tn(ffn_back, activated))]
    part, self_parts, self_plane_back, ffn_parts, text_other = stage(
        bf(dot_nt(gate_grad, w_one)),
        self_parts,
        self_plane_back,
        split_ffn(ffn_grads, n_dp, yidx),
        text_other,
    )
    text_grad = my_half(grad_d1) + (wide(my_half(text_part)) + wide(my_half(text_other)))
    self_total = scatter_dp(sum_plane(self_parts, self_plane_back, own))
    ffn_plane_back = scatter_plane(ffn_parts)
    grad_one, attn_back, sums_one = norm_back(
        [grad_two, part, swap_core(part)], None, normed_one, inv_one, norm_vecs, 0
    )
    enc_g, enc_sum, diag = attention_backward(
        qkv, None, limit, bias, False, True, context, lse, bf(dot_nn(attn_back, w_o))
    )
    ffn_parts, ffn_plane_back, part, enc_g, diag, text_low, plane_parts = stage(
        ffn_parts,
        ffn_plane_back,
        bf(dot_nt(enc_g, w_qkv)),
        enc_g,
        diag,
        bf(text_grad),
        [dec_ffn_plane[dx, a] for dx, a in ROUTES],
    )
    ffn_total = scatter_dp(sum_plane(ffn_parts, ffn_plane_back, own))
    dec_ffn_sums = scatter_plane(plane_parts)
    out_text_grad = to_owners(text_low)
    input_grad = my_half(grad_one) + (wide(my_half(part)) + wide(my_half(swap_core(part))))
    attn_grads = [bf(dot_tn(inputs, enc_g)), bf(dot_tn(attn_back, context))]
    attn_parts = split_attn(attn_grads, ENC_PLANS, 4, n_dp, yidx)
    vectors = pack_small(
        [sums_one, sums_two, sums_d1, sums_d2, sums_d3],
        enc_sum,
        dec_sum,
        query_sum,
        memory_sum,
        [gate_sum, dec_gate_sum],
        diag,
        bucket_count,
    )
    attn_parts, input_grad, vectors, out_text_grad, dec_ffn_sums, held = stage(
        attn_parts, input_grad, vectors, out_text_grad, dec_ffn_sums, held
    )
    (out_text_grad,) = place_quarters(out_text_grad, owners, [text_half])
    out_enc, out_dec = place_quarters(held, owners, [half_len, text_half])
    attn_plane_back = scatter_plane(attn_parts)
    small = vectors[0] + swap_mp(vectors[1], 1)
    small = jnp.where(own, small, unspread(small, 0, 0))
    dec_attn_total = jnp.concatenate(
        [self_total[:4], cross_total[:4], self_total[4:], cross_total[4:]]
    )
    matrix_rate = MATRIX_RATE * root_frames
    vector_rate = VECTOR_RATE * root_frames
    ffn_new = update_matrices(
        [ffn_total],
        None,
        own_flag,
        (ffn_master, ffn_moment, ffn_average),
        matrix_rate,
        inverse,
        False,
    )
    dattn_new = update_matrices(
        [dec_attn_total],
        None,
        own_flag,
        (dec_attn_master, dec_attn_moment, dec_attn_average),
        matrix_rate,
        inverse,
        True,
    )
    dffn_new = update_matrices(
        dec_ffn_sums,
        plane_parts[0],
        own_flag,
        (dec_ffn_master, dec_ffn_moment, dec_ffn_average),
        matrix_rate,
        inverse,
        False,
    )
    small, out_dec, out_text_grad, out_enc, *_ = stage(
        small, out_dec, out_text_grad, out_enc, ffn_new[4], dattn_new[4], dffn_new[4]
    )
    small = small + swap_core(small)
    attn_parts, attn_plane_back, small, input_grad = stage(
        attn_parts, attn_plane_back, small, input_grad
    )
    attn_total = scatter_dp(sum_plane(attn_parts, attn_plane_back, own))
    (out_input_grad,) = place_quarters(to_owners(bf(input_grad)), owners, [half_len])
    small = sum_dp(small)
    def head_bias(i):
        row, lane = NORM_ROWS + i // 3, (i % 3) * 2 * PAIR
        return small[row, lane : lane + group_width]

    norm_total = small[: norm_vecs.shape[0]]
    dec_norm_total = small[norm_vecs.shape[0] : NORM_ROWS]
    col_total = jnp.concatenate([head_bias(0), head_bias(1), small[NORM_ROWS + 2]])
    dec_col_total = jnp.concatenate([head_bias(i) for i in range(2, 6)] + [small[NORM_ROWS + 3]])
    table_total = small[NORM_ROWS + 4 : NORM_ROWS + 4 + group_heads, :bucket_count].T

    attn_new = update_matrices(
        [attn_total],
        None,
        own_flag,
        (attn_master, attn_moment, attn_average),
        matrix_rate,
        inverse,
        True,
    )
    norm_new = update(norm_vecs, norm_moment, norm_average, norm_total, vector_rate, frame_total)
    col_new = update(col_bias, col_moment, col_average, col_total, vector_rate, frame_total)
    rel_new = update(rel_table, rel_moment, rel_average, table_total, vector_rate, frame_total)
    dnorm_new = update(
        dec_norm_vecs, dec_norm_moment, dec_norm_average, dec_norm_total, vector_rate, frame_total
    )
    dcol_new = update(
        dec_col_bias, dec_col_moment, dec_col_average, dec_col_total, vector_rate, frame_total
    )
    return (
        out_enc,
        out_input_grad,
        attn_new[0],
        ffn_new[0],
        *attn_new[1:],
        *ffn_new[1:],
        *norm_new[1:],
        *col_new[1:],
        *rel_new[1:],
        out_dec,
        out_text_grad,
        dattn_new[0],
        dffn_new[0],
        *dattn_new[1:],
        *dffn_new[1:],
        *dnorm_new[1:],
        *dcol_new[1:],
    )


def solution(mesh):
    rows = P("dp", "seq", None)
    matrix = P(None, ("dp", "seq"), "mp")
    table = P(None, "mp")
    enc_params = [matrix] * 6 + [P()] * 3 + [P("mp")] * 3 + [table] * 3
    dec_params = [matrix] * 6 + [P()] * 3 + [P("mp")] * 3
    in_specs = (rows, rows, P("dp"), *enc_params, rows, rows, P("dp"), *dec_params)
    out_specs = (
        [rows, rows]
        + [matrix] * 10
        + [P()] * 3
        + [P("mp")] * 3
        + [table] * 3
        + [rows, rows]
        + [matrix] * 10
        + [P()] * 3
        + [P("mp")] * 3
    )
    return jax.shard_map(
        local, mesh=mesh, in_specs=in_specs, out_specs=tuple(out_specs), check_vma=False
    )
```
